32 devices in a mesh: fsdp: 8 (over y, x, core), sp: 4 (over z).
Axes of the slice: x: 2, y: 2, z: 4, core: 2. Of those that a mesh axis runs over, the one named last changes fastest.
Arguments:
- tokens: bfloat16 [16384, 1024], P(('fsdp', 'sp')), may hold values from -6 to 6
- query_weight: float32 [1024, 1024], P('fsdp'), may hold values from -0.1875 to 0.1875
- key_projection_weight: float32 [1024, 512], P('fsdp'), may hold values from -0.1875 to 0.1875
- value_projection_weight: float32 [1024, 512], P('fsdp'), may hold values from -0.1875 to 0.1875
- output_weight: float32 [1024, 1024], P('fsdp'), may hold values from -1.5 to 1.5
- router_weight: float32 [1024, 32], P('fsdp'), may hold values from -0.09375 to 0.09375
- first_gain: float32 [1024], P('fsdp'), may hold values from 0.5 to 1.5
- second_gain: float32 [1024], P('fsdp'), may hold values from 0.5 to 1.5
- expert_gate: float32 [32, 1024, 512], P('fsdp', 'sp'), may hold values from -0.1875 to 0.1875
- expert_up: float32 [32, 1024, 512], P('fsdp', 'sp'), may hold values from -0.1875 to 0.1875
- expert_down: float32 [32, 512, 1024], P('fsdp', None, 'sp'), may hold values from -1 to 1
- routes: int32 [16384, 8], P(('fsdp', 'sp')), may hold values from 0 to 31, all different within a row; in each aligned block of 512 rows (0 to 511, 512 to 1023, ...) at most 192 rows name the same one
- dealing: int32 [8, 2048], P('fsdp'), may hold values from 0 to 2047, each once within a row
- lengths: int32 [8, 3], P('fsdp'), may hold values from 1 to 1024, 2048 in all within a row
- cotangent: bfloat16 [16384, 1024], P(('fsdp', 'sp')), may hold values from -6 to 6
Outputs:
- layer_out: bfloat16 [16384, 1024], P(('fsdp', 'sp'))
- tokens_grad: bfloat16 [16384, 1024], P(('fsdp', 'sp'))
- grad_query_weight: float32 [1024, 1024], P('fsdp')
- grad_key_weight: float32 [1024, 512], P('fsdp')
- grad_value_weight: float32 [1024, 512], P('fsdp')
- grad_output_weight: float32 [1024, 1024], P('fsdp')
- grad_router_weight: float32 [1024, 32], P('fsdp')
- grad_first_gain: float32 [1024], P('fsdp')
- grad_second_gain: float32 [1024], P('fsdp')
- grad_expert_gate: float32 [32, 1024, 512], P('fsdp', 'sp')
- grad_expert_up: float32 [32, 1024, 512], P('fsdp', 'sp')
- grad_expert_down: float32 [32, 512, 1024], P('fsdp', None, 'sp')
The draws below stay inside these ranges and needn't reach their ends.
Inputs may be any that keep to these rules, and one draw needn't show every extreme that they name: `routes`: each token names 8 different experts; among the 512 rows of one device no expert is named more than 192 times, and in some devices' rows an expert is named exactly 192 times. `dealing`: each row names every place of its group once. `lengths`: each row sums to 2048, and its largest entry is exactly 1024.
All inputs are finite; a program needn't handle non-finite values.
Results may differ from the reference program's by a relative error of at most 0.02.
Values may be sent and summed in bfloat16 or wider, within the bound.
No kernel may reach another device: no remote copies, remote signals or barrier semaphores. Data moves between devices by JAX's collectives and lax.ppermute only.
A program may use at most 256 MiB of HBM per device.

```python
import math
import jax
import jax.numpy as jnp
import numpy as np
from jax import lax

MODEL_WIDTH = 1024
QUERY_HEADS = 16
KEY_VALUE_HEADS = 8
HEAD_SIZE = 64
FF = 512
EXPERTS = 32
TOPK = 8
TOK_DEV = 512
SEQS = 3
BLOCK = 512
GROUP = 2048
GROUPS = 8
TOKEN_TOTAL = 16384
MOST = 1024
CAP = 192
N_FSDP = 8
N_SP = 4


def block_levels(rng, dims, cuts, low, top_value):
    loudness, own = 1.0, jax.random.fold_in(rng, 6)
    for dim, blocks in cuts:
        draws = jnp.exp(jax.random.uniform(jax.random.fold_in(own, dim), (blocks,), jnp.float32, low / len(cuts), top_value / len(cuts)))
        loudness = loudness * jnp.repeat(draws, dims[dim] // blocks).reshape([-1 if axis == dim else 1 for axis in range(len(dims))])
    return loudness


def length_profile(amount, total, reach, skew):
    portions = [(1 << 20) // math.isqrt(rank ** skew) + 1 for rank in range(2, amount + 1)]
    spare, given = total - reach - (amount - 1), [1] * (amount - 1)
    while spare > 0:
        movable = [i for i in range(amount - 1) if given[i] < reach]
        mass, left = sum([portions[i] for i in movable]), spare
        for i in movable:
            extra = min(reach - given[i], max(1, left * portions[i] // mass), spare)
            given[i] = given[i] + extra
            spare = spare - extra
    return np.array([reach] + given)


def uneven(own_key, number_of, total, bound, skew):
    if number_of == 2:
        one = jax.random.randint(own_key, (), max(1, total - bound), min(bound, total - 1) + 1)
        return jnp.stack([one, total - one])
    sizes = jnp.asarray(length_profile(number_of, total, bound, skew), jnp.int32)
    couples = (number_of - 1) // 2
    donor, sink = sizes[1:1 + 2 * couples:2], sizes[2:2 + 2 * couples:2]
    room = jnp.minimum(donor - 1, bound - sink)
    passed = jax.random.randint(jax.random.fold_in(own_key, 1), (couples,), 0, 1 << 20) % (room + 1)
    sizes = sizes.at[1:1 + 2 * couples:2].set(donor - passed).at[2:2 + 2 * couples:2].set(sink + passed)
    return sizes[jax.random.permutation(jax.random.fold_in(own_key, 2), number_of)]


def assign_block(rng, own, number, rows, number_of, top, limit, lean):
    order = jax.random.permutation(rng, number_of)
    crowded, ordinary = load_shares(number_of, rows * top, limit, lean, True), load_shares(number_of, rows * top, limit, lean, False)
    places = jnp.arange(number_of)

    def named(sizes, turn):
        used = int((sizes > 0).sum())
        fixed = max(1, used // 4)
        shifted = fixed + (places - fixed + turn * (used - fixed)) % max(1, number_of - fixed)
        return jnp.zeros((number_of,), jnp.int32).at[order[jnp.where(places < fixed, places, shifted)]].set(jnp.asarray(sizes, jnp.int32))

    sizes = jnp.where(number % 4 == 0, named(crowded, number // 4), named(ordinary, number - number // 4 - 1))
    mixed = jax.random.permutation(jax.random.fold_in(own, 3), number_of)
    donor, receiver = mixed[0:number_of // 2 * 2:2], mixed[1:number_of // 2 * 2:2]
    room = jnp.minimum(sizes[donor] - 1, limit - sizes[receiver]) // 2
    room = jnp.where((donor == order[0]) | (receiver == order[0]) | (sizes[receiver] == 0), 0, jnp.maximum(room, 0))
    shifted = jax.random.randint(jax.random.fold_in(own, 4), (number_of // 2,), 0, 1 << 20) % (room + 1)
    sizes = sizes.at[donor].add(-shifted).at[receiver].add(shifted)
    labels = jnp.searchsorted(jnp.cumsum(sizes), jnp.arange(rows * top), side="right").astype(jnp.int32)
    listing = labels.reshape(top, rows).T
    listing = listing[jax.random.permutation(jax.random.fold_in(own, 1), rows)]
    turn = jax.random.randint(jax.random.fold_in(own, 2), (rows, 1), 0, top)
    return jnp.take_along_axis(listing, (jnp.arange(top)[None, :] + turn) % top, axis=1)


def load_shares(amount, total, bound, slope, full):
    weights = [(1 << 20) // math.isqrt(rank ** slope) + 1 for rank in range(1, amount + 1)]
    largest = bound if full else min(bound, max(-(-total // amount), total * weights[0] // sum(weights)))
    least = 1 if total - largest >= amount - 1 else 0
    counts, spare = [largest] + [least] * (amount - 1), total - largest - least * (amount - 1)
    while spare > 0:
        movable = [i for i in range(1, amount) if counts[i] < largest] or [i for i in range(1, amount) if counts[i] < bound]
        whole, budget = sum([weights[i] for i in movable]), spare
        for i in movable:
            addition = min(bound - counts[i], max(1, budget * weights[i] // whole), spare)
            counts[i] = counts[i] + addition
            spare = spare - addition
    return np.array(counts)


def noise(rng, extent, width, limit, split=(), held_as=jnp.bfloat16):
    values = width * jax.random.normal(rng, extent, jnp.float32)
    if split:
        values = values * block_levels(rng, extent, split, -0.22, 0.18)
    return jnp.clip(values, -limit, limit).astype(held_as)


def setup_inputs(seed: int = 0) -> dict:
    splits = jax.random.split(jax.random.key(seed), 16)
    tokens = noise(splits[0], (TOKEN_TOTAL, MODEL_WIDTH), 1.0, 6.0, ((0, 32),))
    query_weight = noise(splits[1], (MODEL_WIDTH, QUERY_HEADS * HEAD_SIZE), MODEL_WIDTH ** -0.5, 0.1875, ((0, 8),), jnp.float32)
    key_projection_weight = noise(splits[2], (MODEL_WIDTH, KEY_VALUE_HEADS * HEAD_SIZE), MODEL_WIDTH ** -0.5, 0.1875, ((0, 8),), jnp.float32)
    value_projection_weight = noise(splits[3], (MODEL_WIDTH, KEY_VALUE_HEADS * HEAD_SIZE), MODEL_WIDTH ** -0.5, 0.1875, ((0, 8),), jnp.float32)
    output_weight = noise(splits[4], (QUERY_HEADS * HEAD_SIZE, MODEL_WIDTH), (MODEL_WIDTH // 64) ** -0.5, 1.5, ((0, 8),), jnp.float32)
    router_weight = noise(splits[5], (MODEL_WIDTH, EXPERTS), (4 * MODEL_WIDTH) ** -0.5, 0.09375, ((0, 8),), jnp.float32)
    first_gain = jnp.clip(1.0 + 0.1 * jax.random.normal(splits[6], (MODEL_WIDTH,), jnp.float32), 0.5, 1.5)
    second_gain = jnp.clip(1.0 + 0.1 * jax.random.normal(splits[7], (MODEL_WIDTH,), jnp.float32), 0.5, 1.5)
    expert_gate = noise(splits[8], (EXPERTS, MODEL_WIDTH, FF), MODEL_WIDTH ** -0.5, 0.1875, ((0, 8), (1, 4)), jnp.float32)
    expert_up = noise(splits[9], (EXPERTS, MODEL_WIDTH, FF), MODEL_WIDTH ** -0.5, 0.1875, ((0, 8), (1, 4)), jnp.float32)
    expert_down = noise(splits[10], (EXPERTS, FF, MODEL_WIDTH), (FF // 16) ** -0.5, 1.0, ((0, 8), (2, 4)), jnp.float32)
    routes_keys = jax.random.split(jax.random.fold_in(splits[11], 1), TOKEN_TOTAL // TOK_DEV)
    routes_turns = jax.random.permutation(jax.random.fold_in(splits[11], 3), TOKEN_TOTAL // TOK_DEV)
    routes = jax.vmap(lambda own, number: assign_block(jax.random.fold_in(splits[11], 2), own, number, TOK_DEV, EXPERTS, TOPK, CAP, 1))(routes_keys, routes_turns).reshape((TOKEN_TOTAL, TOPK))
    dealing = jax.vmap(lambda own: jax.random.permutation(own, GROUP))(jax.random.split(splits[12], GROUPS)).reshape((GROUPS, GROUP)).astype(jnp.int32)
    lengths = jax.vmap(lambda own: uneven(own, SEQS, GROUP, MOST, 1))(jax.random.split(splits[13], GROUPS)).reshape((GROUPS, SEQS)).astype(jnp.int32)
    cotangent = noise(splits[14], (TOKEN_TOTAL, MODEL_WIDTH), 1.0, 6.0, ((0, 32),))
    return dict(tokens=tokens, query_weight=query_weight, key_projection_weight=key_projection_weight, value_projection_weight=value_projection_weight, output_weight=output_weight, router_weight=router_weight, first_gain=first_gain, second_gain=second_gain, expert_gate=expert_gate, expert_up=expert_up, expert_down=expert_down, routes=routes, dealing=dealing, lengths=lengths, cotangent=cotangent)


NORM_EPS = 1e-06
ROPE_BASE = 10000.0
MASKED = -1e+30
TOP_PRECISION = lax.Precision.HIGHEST

@jax.custom_vjp
def low(v):
    return lax.optimization_barrier(v.astype(jnp.bfloat16)).astype(jnp.float32)

@jax.custom_vjp
def low_back(v):
    return v

def low_keep(v):
    return (low(v), None)

def low_pass(kept, grad):
    return (grad,)

def back_keep(v):
    return (v, None)

def back_low(kept, grad):
    return (low(grad),)
low.defvjp(low_keep, low_pass)
low_back.defvjp(back_keep, back_low)

def rms_scale(values):
    return values * lax.rsqrt(lax.optimization_barrier(jnp.mean(values * values, axis=-1, keepdims=True)) + NORM_EPS)

def apply_rotary(values, places, direction):
    half_dim = HEAD_SIZE // 2
    frequency = ROPE_BASE ** (-(jnp.arange(half_dim, dtype=jnp.float32) * 2.0 / HEAD_SIZE))
    angles = places[:, None] * frequency[None, :]
    cosine = jnp.cos(angles)[:, None, :]
    sine_part = direction * jnp.sin(angles)[:, None, :]
    first_half = values[..., :half_dim]
    second_half = values[..., half_dim:]
    return jnp.concatenate([first_half * cosine - second_half * sine_part, second_half * cosine + first_half * sine_part], axis=-1)

def sequence_info(length_row, places):
    seq_ends = jnp.cumsum(length_row).astype(jnp.int32)
    starts = (seq_ends - length_row).astype(jnp.int32)
    within = starts[None, :] <= places[:, None]
    first_place = lax.optimization_barrier(jnp.max(jnp.where(within, starts[None, :], 0), axis=1)).astype(jnp.int32)
    seq_index = (lax.optimization_barrier(jnp.sum(within.astype(jnp.int32), axis=1)) - 1).astype(jnp.int32)
    return (first_place, seq_index)

def invert(order_row):
    size_row = order_row.shape[0]
    return jnp.zeros((size_row,), jnp.int32).at[order_row].set(jnp.arange(size_row, dtype=jnp.int32))

def dealt_places(length_row, order_row):
    return (order_row - sequence_info(length_row, order_row)[0]).astype(jnp.int32)

def reference(tokens, query_weight, key_projection_weight, value_projection_weight, output_weight, router_weight, first_gain, second_gain, expert_gate, expert_up, expert_down, routes, dealing, lengths, cotangent):
    grouped_row_count = TOK_DEV * N_SP
    block_count = grouped_row_count // BLOCK
    device_count = N_FSDP * N_SP
    slot_count = device_count * CAP
    query_per_key_ratio = QUERY_HEADS // KEY_VALUE_HEADS
    score_scale = 1.0 / math.sqrt(HEAD_SIZE)
    inverse = jax.vmap(invert)(dealing)
    offset_rows = jnp.arange(N_FSDP, dtype=jnp.int32)[:, None] * grouped_row_count
    return_to_start = (inverse + offset_rows).reshape(-1).astype(jnp.int32)
    places_dealt = jax.vmap(dealt_places)(lengths, dealing).reshape(-1).astype(jnp.float32)
    every_place = jnp.arange(grouped_row_count, dtype=jnp.int32)
    segments = jax.vmap(lambda length_row: sequence_info(length_row, every_place)[1])(lengths)
    expert_ids = routes.reshape(device_count, TOK_DEV * TOPK)
    expert_hot = (expert_ids[:, :, None] == jnp.arange(EXPERTS, dtype=jnp.int32)[None, None, :]).astype(jnp.int32)
    running = jnp.cumsum(expert_hot, axis=1).astype(jnp.int32)
    slot_ids = lax.optimization_barrier(jnp.sum((running - 1) * expert_hot, axis=2)).astype(jnp.int32)
    device_ids = jnp.arange(device_count, dtype=jnp.int32)[:, None]
    flat_index = (expert_ids * slot_count + device_ids * CAP + slot_ids).reshape(-1).astype(jnp.int32)
    token_ids = jnp.arange(TOKEN_TOTAL * TOPK, dtype=jnp.int32) // TOPK
    tables = jnp.full((EXPERTS * slot_count,), TOKEN_TOTAL, jnp.int32).at[flat_index].set(token_ids).reshape(EXPERTS, slot_count)
    pair_index = flat_index.reshape(TOKEN_TOTAL, TOPK)

    def attend_group(group_args):
        query_group, key_group, value_group, segment_group = group_args
        key_wide = jnp.repeat(key_group, query_per_key_ratio, axis=1)
        value_wide = jnp.repeat(value_group, query_per_key_ratio, axis=1)
        key_places = jnp.arange(grouped_row_count, dtype=jnp.int32)

        def query_block(block_args):
            query_part, first_row = block_args
            raw_scores = jnp.einsum('qhd,khd->hqk', query_part, key_wide, precision=TOP_PRECISION)
            scores = low_back(raw_scores) * score_scale
            query_places = first_row + jnp.arange(BLOCK, dtype=jnp.int32)
            query_segments = lax.dynamic_slice_in_dim(segment_group, first_row, BLOCK)
            allowed = (key_places[None, :] <= query_places[:, None]) & (segment_group[None, :] == query_segments[:, None])
            probs = jax.nn.softmax(jnp.where(allowed[None], scores, MASKED), axis=-1)
            return jnp.einsum('hqk,khd->qhd', low(probs), value_wide, precision=TOP_PRECISION)
        first_rows = jnp.arange(block_count, dtype=jnp.int32) * BLOCK
        blocks = lax.map(jax.checkpoint(query_block), (query_group.reshape(block_count, BLOCK, QUERY_HEADS, HEAD_SIZE), first_rows))
        return blocks.reshape(grouped_row_count, QUERY_HEADS, HEAD_SIZE)

    def layer(x_in, wq_in, wk_in, wv_in, wo_in, wr_in, gain_one, gain_two, gate_in, up_in, down_in):
        query_w = low(wq_in)
        key_matrix = low(wk_in)
        value_matrix = low(wv_in)
        out_w = low(wo_in)
        router_w = low(wr_in)
        gain_attend = low(gain_one)
        gain_mixer = low(gain_two)
        gate_w = low(gate_in)
        up_w = low(up_in)
        down_w = low(down_in)
        first_activation = low(rms_scale(x_in) * gain_attend)
        query_pre = jnp.dot(first_activation, query_w, precision=TOP_PRECISION).reshape(TOKEN_TOTAL, QUERY_HEADS, HEAD_SIZE)
        key_projected = jnp.dot(first_activation, key_matrix, precision=TOP_PRECISION).reshape(TOKEN_TOTAL, KEY_VALUE_HEADS, HEAD_SIZE)
        value_projected = jnp.dot(first_activation, value_matrix, precision=TOP_PRECISION).reshape(TOKEN_TOTAL, KEY_VALUE_HEADS, HEAD_SIZE)
        query_sent = low(apply_rotary(low_back(query_pre), places_dealt, 1.0))
        key_outbound = low(apply_rotary(low_back(key_projected), places_dealt, 1.0))
        value_outbound = low(low_back(value_projected))
        query_orig = jnp.take(query_sent, return_to_start, axis=0).reshape(N_FSDP, grouped_row_count, QUERY_HEADS, HEAD_SIZE)
        key_unrotated = jnp.take(key_outbound, return_to_start, axis=0).reshape(N_FSDP, grouped_row_count, KEY_VALUE_HEADS, HEAD_SIZE)
        value_unrotated = jnp.take(value_outbound, return_to_start, axis=0).reshape(N_FSDP, grouped_row_count, KEY_VALUE_HEADS, HEAD_SIZE)
        residual = jnp.take(low_back(x_in), return_to_start, axis=0)
        attended = lax.map(jax.checkpoint(attend_group), (query_orig, key_unrotated, value_unrotated, segments))
        attended = low(low_back(attended.reshape(TOKEN_TOTAL, QUERY_HEADS * HEAD_SIZE)))
        middle = residual + low_back(jnp.dot(attended, out_w, precision=TOP_PRECISION))
        act_two = low(rms_scale(middle) * gain_mixer)
        logits = low_back(jnp.dot(act_two, router_w, precision=TOP_PRECISION))
        gate_probs = jax.nn.softmax(jnp.take_along_axis(logits, routes, axis=1), axis=-1)
        padded = jnp.concatenate([act_two, jnp.zeros((1, MODEL_WIDTH), jnp.float32)], axis=0)

        def expert_rows(expert_args):
            table_row, gate_one, up_one, down_one = expert_args
            rows_in = low_back(jnp.take(padded, table_row, axis=0))
            gate_pre = low_back(jnp.dot(rows_in, gate_one, precision=TOP_PRECISION))
            up_pre = low_back(jnp.dot(rows_in, up_one, precision=TOP_PRECISION))
            hidden = low(jax.nn.silu(gate_pre) * up_pre)
            return low(low_back(jnp.dot(hidden, down_one, precision=TOP_PRECISION)))
        produced = lax.map(jax.checkpoint(expert_rows), (tables, gate_w, up_w, down_w)).reshape(EXPERTS * slot_count, MODEL_WIDTH)
        mixture = jnp.zeros((TOKEN_TOTAL, MODEL_WIDTH), jnp.float32)
        for position in range(TOPK):
            mixture = mixture + gate_probs[:, position:position + 1] * jnp.take(produced, pair_index[:, position], axis=0)
        return middle + mixture
    x_value = tokens.astype(jnp.float32)
    out_value, pull_back = jax.vjp(layer, x_value, query_weight, key_projection_weight, value_projection_weight, output_weight, router_weight, first_gain, second_gain, expert_gate, expert_up, expert_down)
    gradients = pull_back(cotangent.astype(jnp.float32))
    return (out_value.astype(jnp.bfloat16), gradients[0].astype(jnp.bfloat16), gradients[1], gradients[2], gradients[3], gradients[4], gradients[5], gradients[6], gradients[7], gradients[8], gradients[9], gradients[10])
```

```python
import math

import jax
import jax.numpy as jnp
from jax import lax
from jax.experimental import pallas as pl
from jax.experimental.pallas import tpu as pltpu
from jax.sharding import PartitionSpec as P

MODEL_WIDTH = 1024
QUERY_HEADS = 16
KEY_VALUE_HEADS = 8
HEAD_SIZE = 64
EXPERTS = 32
TOPK = 8
BLOCK = 512
CAP = 192


NORM_EPS = 1e-06
ROPE_BASE = 10000.0
MASKED = -1e30
VMEM_LIMIT = 60 * 1024 * 1024


def apply_rotary(values, places, direction):
    half_dim = HEAD_SIZE // 2
    frequency = ROPE_BASE ** (-(jnp.arange(half_dim, dtype=jnp.float32) * 2.0 / HEAD_SIZE))
    angles = places[:, None] * frequency[None, :]
    cosine = jnp.cos(angles)[:, None, :]
    sine_part = direction * jnp.sin(angles)[:, None, :]
    first_half = values[..., :half_dim]
    second_half = values[..., half_dim:]
    return jnp.concatenate(
        [
            first_half * cosine - second_half * sine_part,
            second_half * cosine + first_half * sine_part,
        ],
        axis=-1,
    )


def sequence_info(length_row, places):
    seq_ends = jnp.cumsum(length_row)
    starts = seq_ends - length_row
    within = starts[None, :] <= places[:, None]
    first_place = jnp.max(jnp.where(within, starts[None, :], 0), axis=1)
    seq_index = jnp.sum(within.astype(jnp.int32), axis=1) - 1
    return (first_place, seq_index)


def block_scores(q_block, k_block, q_first, k_first, seq_ids, score_scale):
    span = q_block.shape[0]
    raw_scores = (
        jnp.einsum("qlgd,kld->lgqk", q_block, k_block, preferred_element_type=jnp.float32)
        * score_scale
    )
    q_places = q_first + jnp.arange(span, dtype=jnp.int32)
    k_places = k_first + jnp.arange(span, dtype=jnp.int32)
    q_seqs = lax.dynamic_slice_in_dim(seq_ids, q_first, span)
    k_seqs = lax.dynamic_slice_in_dim(seq_ids, k_first, span)
    allowed = (k_places[None, :] <= q_places[:, None]) & (k_seqs[None, :] == q_seqs[:, None])
    return jnp.where(allowed, raw_scores, MASKED)


def contract(left, right, left_dim, right_dim):
    return lax.dot_general(
        left, right, (((left_dim,), (right_dim,)), ((), ())), preferred_element_type=jnp.float32
    )


def axis_bits(count):
    bits = [1 << place for place in range(count.bit_length() - 1)]
    return bits[::-1]


def flip(values, axis_name, bit):
    count = lax.axis_size(axis_name)
    return lax.ppermute(values, axis_name, [(place, place ^ bit) for place in range(count)])


def gather_rows(values, axis_name):
    count = lax.axis_size(axis_name)
    high, low = axis_bits(count), []
    if count > 2:
        low = high[1:2] + high[:1] + high[2:]
        orders = (high, low)
    else:
        orders = (high, high)
    half = values.shape[1] // 2
    halves = []
    for order, part in zip(orders, (values[:, :half], values[:, half:])):
        pieces = {0: part}
        for bit in order:
            pieces.update({r ^ bit: flip(piece, axis_name, bit) for r, piece in list(pieces.items())})
        halves.append(jnp.stack([pieces[r] for r in range(count)]))
    return jnp.concatenate(halves, axis=2)


def reduce_rows(values, axis_name):
    count = lax.axis_size(axis_name)
    high = axis_bits(count)
    if count > 2:
        orders = (high[::-1], high[2:][::-1] + high[:1] + high[1:2])
    else:
        orders = (high, high)
    half = values.shape[2] // 2
    sums = []
    for order, part in zip(orders, (values[:, :, :half], values[:, :, half:])):
        kept, pieces = list(range(count)), part
        for bit in order:
            stay = [i for i, r in enumerate(kept) if not r & bit]
            leave = [kept.index(kept[i] ^ bit) for i in stay]
            arrived = flip(jnp.stack([pieces[i] for i in leave]), axis_name, bit)
            pieces = (
                jnp.stack([pieces[i] for i in stay]).astype(jnp.float32) + arrived.astype(jnp.float32)
            ).astype(jnp.bfloat16)
            kept = [kept[i] for i in stay]
        sums.append(pieces[0])
    return jnp.concatenate(sums, axis=1).astype(jnp.float32)


def expert_step(
    slot_ref,
    share_ref,
    act_ref,
    cot_ref,
    gate_ref,
    up_ref,
    down_ref,
    mixed_ref,
    back_ref,
    share_grad_ref,
    gate_grad_ref,
    up_grad_ref,
    down_grad_ref,
    act_rows,
    hidden_rows,
    down_rows,
    gate_rows,
    up_rows,
):
    sources, rows, width = act_ref.shape
    shards, shard_width = down_ref.shape[0], down_ref.shape[3]
    hidden_width = gate_ref.shape[3]
    gate_w = gate_ref[...].reshape(width, hidden_width)
    up_w = up_ref[...].reshape(width, hidden_width)
    picked, cots, shares, masks = [], [], [], []
    for source in range(sources):
        mask = lax.broadcasted_iota(jnp.int32, (CAP, rows), 0) == slot_ref[0, source]
        choose = jnp.where(mask, 1.0, 0.0).astype(jnp.bfloat16)
        picked.append(contract(choose, act_ref[source], 1, 0).astype(jnp.bfloat16))
        cots.append(contract(choose, cot_ref[source], 1, 0))
        shares.append(
            jnp.sum(jnp.where(mask, share_ref[0, source], 0.0), axis=1, keepdims=True)
        )
        masks.append(mask)
    act = jnp.concatenate(picked, 0)
    cot = jnp.concatenate(cots, 0)
    share = jnp.concatenate(shares, 0)
    gate_pre = contract(act, gate_w, 1, 0)
    up_pre = contract(act, up_w, 1, 0)
    sigmoid = 1.0 / (1.0 + jnp.exp(-gate_pre))
    silu = gate_pre * sigmoid
    hidden = (silu * up_pre).astype(jnp.bfloat16)
    made = jnp.concatenate(
        [contract(hidden, down_ref[shard, 0], 1, 0) for shard in range(shards)], axis=1
    )
    made = made.astype(jnp.bfloat16).astype(jnp.float32)
    share_grad = jnp.sum(made * cot, axis=1, keepdims=True)
    mixed = (made * share).astype(jnp.bfloat16)
    made_grad = (share * cot).astype(jnp.bfloat16)
    hidden_grad = sum(
        contract(
            made_grad[:, shard * shard_width : (shard + 1) * shard_width], down_ref[shard, 0], 1, 1
        )
        for shard in range(shards)
    )
    up_grad = (hidden_grad * silu).astype(jnp.bfloat16)
    gate_grad = (
        hidden_grad * up_pre * sigmoid * (1.0 + gate_pre * (1.0 - sigmoid))
    ).astype(jnp.bfloat16)
    back = (contract(gate_grad, gate_w, 1, 1) + contract(up_grad, up_w, 1, 1)).astype(jnp.bfloat16)
    for source in range(sources):
        part = slice(source * CAP, (source + 1) * CAP)
        mixed_ref[0, source] = mixed[part]
        back_ref[0, source] = back[part]
        share_grad_ref[0, source] = jnp.sum(
            jnp.where(masks[source], share_grad[part], 0.0), axis=0, keepdims=True
        )
    step = pl.program_id(1)
    here = pl.ds(pl.multiple_of(step * sources * CAP, sources * CAP), sources * CAP)
    act_rows[here, :] = act
    hidden_rows[here, :] = hidden
    down_rows[here, :] = made_grad
    gate_rows[here, :] = gate_grad
    up_rows[here, :] = up_grad

    @pl.when(step == pl.num_programs(1) - 1)
    def _():
        gate_sum = contract(act_rows[...], gate_rows[...], 0, 0)
        gate_grad_ref[...] = gate_sum.astype(jnp.bfloat16).reshape(gate_grad_ref.shape)
        up_sum = contract(act_rows[...], up_rows[...], 0, 0)
        up_grad_ref[...] = up_sum.astype(jnp.bfloat16).reshape(up_grad_ref.shape)
        for shard in range(shards):
            cols = slice(shard * shard_width, (shard + 1) * shard_width)
            down_grad_ref[shard, 0] = contract(
                hidden_rows[...], down_rows[:, cols], 0, 0
            ).astype(jnp.bfloat16)


def run_experts(slots, shares, act_all, cot_all, gate_all, up_all, down_all):
    experts, sources, rows = slots.shape
    width = act_all.shape[2]
    shards, _, gate_shard, hidden_width = gate_all.shape
    down_shard = down_all.shape[3]
    pair = 2
    listed = sources * CAP

    def by_source(*shape):
        return pl.BlockSpec((1, pair) + shape, lambda e, s: (e, s) + (0,) * len(shape))

    def rows_of(*shape):
        return pl.BlockSpec((pair,) + shape, lambda e, s: (s,) + (0,) * len(shape))

    def weight_of(*shape):
        return pl.BlockSpec((shards, 1) + shape, lambda e, s: (0, e) + (0,) * len(shape))

    low = jnp.bfloat16
    outs = pl.pallas_call(
        expert_step,
        grid=(experts, sources // pair),
        in_specs=[
            by_source(1, rows),
            by_source(1, rows),
            rows_of(rows, width),
            rows_of(rows, width),
            weight_of(gate_shard, hidden_width),
            weight_of(gate_shard, hidden_width),
            weight_of(hidden_width, down_shard),
        ],
        out_specs=[
            by_source(CAP, width),
            by_source(CAP, width),
            by_source(1, rows),
            weight_of(gate_shard, hidden_width),
            weight_of(gate_shard, hidden_width),
            weight_of(hidden_width, down_shard),
        ],
        out_shape=[
            jax.ShapeDtypeStruct((experts, sources, CAP, width), low),
            jax.ShapeDtypeStruct((experts, sources, CAP, width), low),
            jax.ShapeDtypeStruct((experts, sources, 1, rows), jnp.float32),
            jax.ShapeDtypeStruct(gate_all.shape, low),
            jax.ShapeDtypeStruct(up_all.shape, low),
            jax.ShapeDtypeStruct(down_all.shape, low),
        ],
        scratch_shapes=[
            pltpu.VMEM((listed, width), low),
            pltpu.VMEM((listed, hidden_width), low),
            pltpu.VMEM((listed, width), low),
            pltpu.VMEM((listed, hidden_width), low),
            pltpu.VMEM((listed, hidden_width), low),
        ],
        compiler_params=pltpu.CompilerParams(
            dimension_semantics=("arbitrary", "arbitrary"), vmem_limit_bytes=VMEM_LIMIT
        ),
        name="experts",
    )(slots[:, :, None], shares[:, :, None], act_all, cot_all, gate_all, up_all, down_all)
    return (outs[0], outs[1], outs[2][:, :, 0], outs[3], outs[4], outs[5])


def combine_step(slot_ref, mixed_ref, back_ref, mixture_ref, act_grad_ref):
    experts, _, _, width = mixed_ref.shape
    rows = mixture_ref.shape[1]
    place = lax.broadcasted_iota(jnp.int32, (rows, experts * CAP), 1)
    hit = None
    for expert in range(experts):
        slot = slot_ref[0, :, expert : expert + 1]
        match = place == jnp.where(slot >= 0, slot + expert * CAP, -1)
        hit = match if hit is None else hit | match
    choose = jnp.where(hit, 1.0, 0.0).astype(jnp.bfloat16)
    for source, target in ((mixed_ref, mixture_ref), (back_ref, act_grad_ref)):
        listed = source[:, 0].reshape(experts * CAP, width)
        target[0] = contract(choose, listed, 1, 0).astype(jnp.bfloat16)


def combine_rows(slots_by_row, mixed_rows, back_rows):
    sources, rows, experts = slots_by_row.shape
    width = mixed_rows.shape[3]
    listed = pl.BlockSpec((experts, 1, CAP, width), lambda s: (0, s, 0, 0))
    dense = pl.BlockSpec((1, rows, width), lambda s: (s, 0, 0))
    return pl.pallas_call(
        combine_step,
        grid=(sources,),
        in_specs=[pl.BlockSpec((1, rows, experts), lambda s: (s, 0, 0)), listed, listed],
        out_specs=[dense, dense],
        out_shape=[jax.ShapeDtypeStruct((sources, rows, width), jnp.bfloat16)] * 2,
        compiler_params=pltpu.CompilerParams(
            dimension_semantics=("arbitrary",), vmem_limit_bytes=VMEM_LIMIT
        ),
        name="combine",
    )(slots_by_row, mixed_rows, back_rows)


def body(
    tokens,
    query_weight,
    key_projection_weight,
    value_projection_weight,
    output_weight,
    router_weight,
    first_gain,
    second_gain,
    expert_gate,
    expert_up,
    expert_down,
    routes,
    dealing,
    lengths,
    cotangent,
):
    token_row_block = tokens.shape[0]
    sequence_parallel_count = lax.axis_size("sp")
    sp_index = lax.axis_index("sp")
    fsdp_count = lax.axis_size("fsdp")
    grouped_row_count = token_row_block * sequence_parallel_count
    local_experts = EXPERTS // fsdp_count
    key_value_resident = KEY_VALUE_HEADS // sequence_parallel_count
    query_per_key_ratio = QUERY_HEADS // KEY_VALUE_HEADS
    score_scale = 1.0 / math.sqrt(HEAD_SIZE)
    block_count = grouped_row_count // BLOCK
    pair_count = token_row_block * TOPK
    query_full, key_full, value_full, output_full, router_full, gain_attend, gain_mixer = (
        lax.all_gather(query_weight.astype(jnp.bfloat16), "fsdp", axis=0, tiled=True),
        lax.all_gather(key_projection_weight.astype(jnp.bfloat16), "fsdp", axis=0, tiled=True),
        lax.all_gather(value_projection_weight.astype(jnp.bfloat16), "fsdp", axis=0, tiled=True),
        lax.all_gather(output_weight.astype(jnp.bfloat16), "fsdp", axis=0, tiled=True),
        lax.all_gather(router_weight.astype(jnp.bfloat16), "fsdp", axis=0, tiled=True),
        lax.all_gather(first_gain.astype(jnp.bfloat16), "fsdp", axis=0, tiled=True),
        lax.all_gather(second_gain.astype(jnp.bfloat16), "fsdp", axis=0, tiled=True),
    )
    gain_attend = gain_attend.astype(jnp.float32)
    gain_mixer = gain_mixer.astype(jnp.float32)
    tokens_value = tokens.astype(jnp.float32)
    inv_one = lax.rsqrt(jnp.mean(tokens_value * tokens_value, axis=1, keepdims=True) + NORM_EPS)
    normed_one = tokens_value * inv_one
    first_activation = (normed_one * gain_attend).astype(jnp.bfloat16)
    query_pre = jnp.dot(first_activation, query_full, preferred_element_type=jnp.float32)
    key_projected = jnp.dot(first_activation, key_full, preferred_element_type=jnp.float32)
    value_projected = jnp.dot(first_activation, value_full, preferred_element_type=jnp.float32)
    order_row = dealing[0]
    length_row = lengths[0]
    mine_places = lax.dynamic_slice_in_dim(order_row, sp_index * token_row_block, token_row_block)
    mine_start = sequence_info(length_row, mine_places)[0]
    resident_positions = (mine_places - mine_start).astype(jnp.float32)
    query_rot = apply_rotary(
        query_pre.reshape(token_row_block, QUERY_HEADS, HEAD_SIZE), resident_positions, 1.0
    ).astype(jnp.bfloat16)
    key_rotated = apply_rotary(
        key_projected.reshape(token_row_block, KEY_VALUE_HEADS, HEAD_SIZE), resident_positions, 1.0
    ).astype(jnp.bfloat16)
    value_second_part = value_projected.reshape(token_row_block, KEY_VALUE_HEADS, HEAD_SIZE).astype(
        jnp.bfloat16
    )
    key_value_packed = jnp.stack([key_rotated, value_second_part], axis=2).reshape(
        token_row_block, KEY_VALUE_HEADS * 2 * HEAD_SIZE
    )
    query_heads, kv_heads, token_cols = (
        lax.all_to_all(
            query_rot.reshape(token_row_block, QUERY_HEADS * HEAD_SIZE),
            "sp",
            split_axis=1,
            concat_axis=0,
            tiled=True,
        ),
        lax.all_to_all(key_value_packed, "sp", split_axis=1, concat_axis=0, tiled=True),
        lax.all_to_all(tokens, "sp", split_axis=1, concat_axis=0, tiled=True),
    )
    inverse_row = (
        jnp.zeros((grouped_row_count,), jnp.int32)
        .at[order_row]
        .set(jnp.arange(grouped_row_count, dtype=jnp.int32))
    )
    query_orig = jnp.take(query_heads, inverse_row, axis=0).reshape(
        grouped_row_count, key_value_resident, query_per_key_ratio, HEAD_SIZE
    )
    kv_orig = jnp.take(kv_heads, inverse_row, axis=0).reshape(
        grouped_row_count, key_value_resident, 2, HEAD_SIZE
    )
    keys_orig = kv_orig[:, :, 0]
    values_orig = kv_orig[:, :, 1]
    resid_cols = jnp.take(token_cols, inverse_row, axis=0)
    every_place = jnp.arange(grouped_row_count, dtype=jnp.int32)
    seq_start, seq_ids = sequence_info(length_row, every_place)
    seq_pos = (every_place - seq_start).astype(jnp.float32)
    first_block = seq_start[::BLOCK] // BLOCK

    def attend_block(block_index):
        q_first = block_index * BLOCK
        q_block = lax.dynamic_slice_in_dim(query_orig, q_first, BLOCK)
        lowest = first_block[block_index]

        def stat_step(k_index, carry):
            running_max, running_sum = carry
            k_first = k_index * BLOCK
            scores = block_scores(
                q_block,
                lax.dynamic_slice_in_dim(keys_orig, k_first, BLOCK),
                q_first,
                k_first,
                seq_ids,
                score_scale,
            )
            new_max = jnp.maximum(running_max, jnp.max(scores, axis=-1))
            terms = jnp.where(scores > MASKED, jnp.exp(scores - new_max[..., None]), 0.0)
            running_sum = running_sum * jnp.exp(running_max - new_max) + jnp.sum(terms, axis=-1)
            return (new_max, running_sum)

        start_stats = (
            jnp.full((key_value_resident, query_per_key_ratio, BLOCK), MASKED, jnp.float32),
            jnp.zeros((key_value_resident, query_per_key_ratio, BLOCK), jnp.float32),
        )
        top_value, total_value = lax.fori_loop(lowest, block_index + 1, stat_step, start_stats)
        log_total = top_value + jnp.log(total_value)

        def value_step(k_index, accum):
            k_first = k_index * BLOCK
            scores = block_scores(
                q_block,
                lax.dynamic_slice_in_dim(keys_orig, k_first, BLOCK),
                q_first,
                k_first,
                seq_ids,
                score_scale,
            )
            probs = jnp.exp(scores - log_total[..., None]).astype(jnp.bfloat16)
            v_block = lax.dynamic_slice_in_dim(values_orig, k_first, BLOCK)
            return accum + jnp.einsum(
                "lgqk,kld->qlgd", probs, v_block, preferred_element_type=jnp.float32
            )

        attended_block = lax.fori_loop(
            lowest,
            block_index + 1,
            value_step,
            jnp.zeros((BLOCK, key_value_resident, query_per_key_ratio, HEAD_SIZE), jnp.float32),
        )
        return (attended_block.astype(jnp.bfloat16), log_total)

    attended, log_totals = lax.map(attend_block, jnp.arange(block_count, dtype=jnp.int32))
    attended_rows = attended.reshape(
        grouped_row_count, key_value_resident * query_per_key_ratio * HEAD_SIZE
    )
    attn_back, resid_back = (
        lax.all_to_all(attended_rows, "sp", split_axis=0, concat_axis=1, tiled=True),
        lax.all_to_all(resid_cols, "sp", split_axis=0, concat_axis=1, tiled=True),
    )
    branch = jnp.dot(attn_back, output_full, preferred_element_type=jnp.float32)
    middle = resid_back.astype(jnp.float32) + branch
    inv_two = lax.rsqrt(jnp.mean(middle * middle, axis=1, keepdims=True) + NORM_EPS)
    normed_two = middle * inv_two
    act_two = (normed_two * gain_mixer).astype(jnp.bfloat16)
    logits = jnp.dot(act_two, router_full, preferred_element_type=jnp.float32)
    expert_range = jnp.arange(EXPERTS, dtype=jnp.int32)
    member = jnp.any(routes[:, :, None] == expert_range[None, None, :], axis=1)
    row_range = jnp.arange(token_row_block, dtype=jnp.int32)
    upto = (row_range[:, None] <= row_range[None, :]).astype(jnp.bfloat16)
    member_rows = member.T.astype(jnp.bfloat16)
    rank = jnp.dot(member_rows, upto, preferred_element_type=jnp.float32).astype(jnp.int32) - 1
    slots = jnp.where(member.T, rank, -1)
    relative = lax.axis_index("fsdp") ^ jnp.arange(fsdp_count, dtype=jnp.int32)

    def to_experts(by_expert):
        arrived = lax.all_to_all(
            by_expert.reshape(fsdp_count, local_experts, token_row_block),
            "fsdp",
            split_axis=0,
            concat_axis=0,
            tiled=True,
        )
        return jnp.swapaxes(jnp.take(arrived, relative, axis=0), 0, 1)

    slots_here = to_experts(slots)
    gate_dense = jax.nn.softmax(jnp.where(member, logits, -jnp.inf), axis=-1)
    gates_here = to_experts(gate_dense.T)
    gate_all, up_all, down_all = (
        lax.all_gather(expert_gate.astype(jnp.bfloat16), "sp", axis=0, tiled=False),
        lax.all_gather(expert_up.astype(jnp.bfloat16), "sp", axis=0, tiled=False),
        lax.all_gather(expert_down.astype(jnp.bfloat16), "sp", axis=0, tiled=False),
    )
    cotangent_all = gather_rows(cotangent, "fsdp")
    act_all = gather_rows(act_two, "fsdp")
    mixed_rows, back_rows, gate_grads, grad_gate_w, grad_up_w, grad_down = run_experts(
        slots_here, gates_here, act_all, cotangent_all, gate_all, up_all, down_all
    )
    mixture_parts, act_grad_parts = combine_rows(
        jnp.transpose(slots_here, (1, 2, 0)), mixed_rows, back_rows
    )
    grad_act_moe = reduce_rows(act_grad_parts, "fsdp")
    mixture = reduce_rows(mixture_parts, "fsdp")
    layer_out = (middle + mixture).astype(jnp.bfloat16)
    upstream = cotangent.astype(jnp.float32)
    gate_grad_back = lax.all_to_all(
        jnp.take(jnp.swapaxes(gate_grads, 0, 1), relative, axis=0),
        "fsdp",
        split_axis=0,
        concat_axis=0,
        tiled=True,
    )
    gate_grad = gate_grad_back.reshape(EXPERTS, token_row_block).T
    weighted = jnp.sum(gate_dense * gate_grad, axis=1, keepdims=True)
    logit_grad = (gate_dense * (gate_grad - weighted)).astype(jnp.bfloat16)
    grad_router_w = jnp.einsum("td,te->de", act_two, logit_grad, preferred_element_type=jnp.float32)
    grad_act_two = grad_act_moe + jnp.dot(
        logit_grad, router_full.T, preferred_element_type=jnp.float32
    )
    grad_gain_two = jnp.sum(grad_act_two * normed_two, axis=0)
    scaled_two = grad_act_two * gain_mixer
    grad_middle = upstream + inv_two * (
        scaled_two - normed_two * jnp.mean(scaled_two * normed_two, axis=1, keepdims=True)
    )
    middle_low = grad_middle.astype(jnp.bfloat16)
    grad_output_w = jnp.einsum(
        "tc,td->cd", attn_back, middle_low, preferred_element_type=jnp.float32
    )
    grad_attn = jnp.dot(middle_low, output_full.T, preferred_element_type=jnp.float32).astype(
        jnp.bfloat16
    )
    grad_heads, grad_resid = (
        lax.all_to_all(grad_attn, "sp", split_axis=1, concat_axis=0, tiled=True),
        lax.all_to_all(middle_low, "sp", split_axis=1, concat_axis=0, tiled=True),
    )
    grad_heads_four = grad_heads.reshape(
        grouped_row_count, key_value_resident, query_per_key_ratio, HEAD_SIZE
    )

    def backward_block(block_index, carry):
        grad_query_all, grad_key_all, grad_value_all = carry
        q_first = block_index * BLOCK
        q_block = lax.dynamic_slice_in_dim(query_orig, q_first, BLOCK)
        dout_block = lax.dynamic_slice_in_dim(grad_heads_four, q_first, BLOCK)
        log_block = log_totals[block_index]
        lowest = first_block[block_index]

        def dot_step(k_index, accum):
            k_first = k_index * BLOCK
            scores = block_scores(
                q_block,
                lax.dynamic_slice_in_dim(keys_orig, k_first, BLOCK),
                q_first,
                k_first,
                seq_ids,
                score_scale,
            )
            probs = jnp.exp(scores - log_block[..., None])
            prob_grad = jnp.einsum(
                "qlgd,kld->lgqk",
                dout_block,
                lax.dynamic_slice_in_dim(values_orig, k_first, BLOCK),
                preferred_element_type=jnp.float32,
            )
            return accum + jnp.sum(probs * prob_grad, axis=-1)

        row_dots = lax.fori_loop(
            lowest,
            block_index + 1,
            dot_step,
            jnp.zeros((key_value_resident, query_per_key_ratio, BLOCK), jnp.float32),
        )

        def grad_step(k_index, inner):
            query_grad, key_grad_all, value_grad_all = inner
            k_first = k_index * BLOCK
            k_block = lax.dynamic_slice_in_dim(keys_orig, k_first, BLOCK)
            v_block = lax.dynamic_slice_in_dim(values_orig, k_first, BLOCK)
            scores = block_scores(q_block, k_block, q_first, k_first, seq_ids, score_scale)
            probs = jnp.exp(scores - log_block[..., None])
            prob_grad = jnp.einsum(
                "qlgd,kld->lgqk", dout_block, v_block, preferred_element_type=jnp.float32
            )
            score_grad = (probs * (prob_grad - row_dots[..., None]) * score_scale).astype(
                jnp.bfloat16
            )
            query_grad = query_grad + jnp.einsum(
                "lgqk,kld->qlgd", score_grad, k_block, preferred_element_type=jnp.float32
            )
            key_add = jnp.einsum(
                "lgqk,qlgd->kld", score_grad, q_block, preferred_element_type=jnp.float32
            )
            value_add = jnp.einsum(
                "lgqk,qlgd->kld",
                probs.astype(jnp.bfloat16),
                dout_block,
                preferred_element_type=jnp.float32,
            )
            key_grad_all = lax.dynamic_update_slice_in_dim(
                key_grad_all,
                lax.dynamic_slice_in_dim(key_grad_all, k_first, BLOCK) + key_add,
                k_first,
                0,
            )
            value_grad_all = lax.dynamic_update_slice_in_dim(
                value_grad_all,
                lax.dynamic_slice_in_dim(value_grad_all, k_first, BLOCK) + value_add,
                k_first,
                0,
            )
            return (query_grad, key_grad_all, value_grad_all)

        start_inner = (
            jnp.zeros((BLOCK, key_value_resident, query_per_key_ratio, HEAD_SIZE), jnp.float32),
            grad_key_all,
            grad_value_all,
        )
        query_grad, grad_key_all, grad_value_all = lax.fori_loop(
            lowest, block_index + 1, grad_step, start_inner
        )
        grad_query_all = lax.dynamic_update_slice_in_dim(grad_query_all, query_grad, q_first, 0)
        return (grad_query_all, grad_key_all, grad_value_all)

    start_grads = (
        jnp.zeros(
            (grouped_row_count, key_value_resident, query_per_key_ratio, HEAD_SIZE), jnp.float32
        ),
        jnp.zeros((grouped_row_count, key_value_resident, HEAD_SIZE), jnp.float32),
        jnp.zeros((grouped_row_count, key_value_resident, HEAD_SIZE), jnp.float32),
    )
    grad_query_all, grad_key_all, grad_value_all = lax.fori_loop(
        0, block_count, backward_block, start_grads
    )
    grad_query_rows = apply_rotary(
        grad_query_all.reshape(
            grouped_row_count, key_value_resident * query_per_key_ratio, HEAD_SIZE
        ),
        seq_pos,
        -1.0,
    ).astype(jnp.bfloat16)
    grad_key_rows = apply_rotary(grad_key_all, seq_pos, -1.0).astype(jnp.bfloat16)
    grad_value_rows = grad_value_all.astype(jnp.bfloat16)
    grad_kv_rows = jnp.stack([grad_key_rows, grad_value_rows], axis=2).reshape(
        grouped_row_count, key_value_resident * 2 * HEAD_SIZE
    )
    grad_query_dealt, key_value_gradient_shared, grad_resid_dealt = (
        lax.all_to_all(
            jnp.take(
                grad_query_rows.reshape(
                    grouped_row_count, key_value_resident * query_per_key_ratio * HEAD_SIZE
                ),
                order_row,
                axis=0,
            ),
            "sp",
            split_axis=0,
            concat_axis=1,
            tiled=True,
        ),
        lax.all_to_all(
            jnp.take(grad_kv_rows, order_row, axis=0), "sp", split_axis=0, concat_axis=1, tiled=True
        ),
        lax.all_to_all(
            jnp.take(grad_resid, order_row, axis=0), "sp", split_axis=0, concat_axis=1, tiled=True
        ),
    )
    key_value_gradient_split = key_value_gradient_shared.reshape(
        token_row_block, KEY_VALUE_HEADS, 2, HEAD_SIZE
    )
    key_gradient_shared = key_value_gradient_split[:, :, 0].reshape(
        token_row_block, KEY_VALUE_HEADS * HEAD_SIZE
    )
    value_gradient_shared = key_value_gradient_split[:, :, 1].reshape(
        token_row_block, KEY_VALUE_HEADS * HEAD_SIZE
    )
    grad_act_one = (
        jnp.dot(grad_query_dealt, query_full.T, preferred_element_type=jnp.float32)
        + jnp.dot(key_gradient_shared, key_full.T, preferred_element_type=jnp.float32)
        + jnp.dot(value_gradient_shared, value_full.T, preferred_element_type=jnp.float32)
    )
    grad_query_w = jnp.einsum(
        "td,tc->dc", first_activation, grad_query_dealt, preferred_element_type=jnp.float32
    )
    grad_key_w = jnp.einsum(
        "td,tc->dc", first_activation, key_gradient_shared, preferred_element_type=jnp.float32
    )
    grad_value_w = jnp.einsum(
        "td,tc->dc", first_activation, value_gradient_shared, preferred_element_type=jnp.float32
    )
    grad_gain_one = jnp.sum(grad_act_one * normed_one, axis=0)
    scaled_one = grad_act_one * gain_attend
    tokens_grad = (
        grad_resid_dealt.astype(jnp.float32)
        + inv_one
        * (scaled_one - normed_one * jnp.mean(scaled_one * normed_one, axis=1, keepdims=True))
    ).astype(jnp.bfloat16)
    expert_sums = tuple(
        lax.psum_scatter(grads, "sp", scatter_dimension=0, tiled=False).astype(jnp.float32)
        for grads in (grad_gate_w, grad_up_w, grad_down)
    )
    shard_sums = (
        lax.psum_scatter(
            grad_query_w.astype(jnp.bfloat16), "fsdp", scatter_dimension=0, tiled=True
        ).astype(jnp.float32),
        lax.psum_scatter(
            grad_key_w.astype(jnp.bfloat16), "fsdp", scatter_dimension=0, tiled=True
        ).astype(jnp.float32),
        lax.psum_scatter(
            grad_value_w.astype(jnp.bfloat16), "fsdp", scatter_dimension=0, tiled=True
        ).astype(jnp.float32),
        lax.psum_scatter(
            grad_output_w.astype(jnp.bfloat16), "fsdp", scatter_dimension=0, tiled=True
        ).astype(jnp.float32),
        lax.psum_scatter(
            grad_router_w.astype(jnp.bfloat16), "fsdp", scatter_dimension=0, tiled=True
        ).astype(jnp.float32),
        lax.psum_scatter(
            grad_gain_one.astype(jnp.bfloat16), "fsdp", scatter_dimension=0, tiled=True
        ).astype(jnp.float32),
        lax.psum_scatter(
            grad_gain_two.astype(jnp.bfloat16), "fsdp", scatter_dimension=0, tiled=True
        ).astype(jnp.float32),
    )
    summed = (
        lax.psum(shard_sums[0].astype(jnp.bfloat16), "sp").astype(jnp.float32),
        lax.psum(shard_sums[1].astype(jnp.bfloat16), "sp").astype(jnp.float32),
        lax.psum(shard_sums[2].astype(jnp.bfloat16), "sp").astype(jnp.float32),
        lax.psum(shard_sums[3].astype(jnp.bfloat16), "sp").astype(jnp.float32),
        lax.psum(shard_sums[4].astype(jnp.bfloat16), "sp").astype(jnp.float32),
        lax.psum(shard_sums[5].astype(jnp.bfloat16), "sp").astype(jnp.float32),
        lax.psum(shard_sums[6].astype(jnp.bfloat16), "sp").astype(jnp.float32),
    )
    return (
        layer_out,
        tokens_grad,
        summed[0],
        summed[1],
        summed[2],
        summed[3],
        summed[4],
        summed[5],
        summed[6],
        expert_sums[0],
        expert_sums[1],
        expert_sums[2],
    )


def solution(mesh):
    return jax.shard_map(
        body,
        mesh=mesh,
        in_specs=(
            P(("fsdp", "sp"), None),
            P("fsdp", None),
            P("fsdp", None),
            P("fsdp", None),
            P("fsdp", None),
            P("fsdp", None),
            P("fsdp"),
            P("fsdp"),
            P("fsdp", "sp", None),
            P("fsdp", "sp", None),
            P("fsdp", None, "sp"),
            P(("fsdp", "sp"), None),
            P("fsdp", None),
            P("fsdp", None),
            P(("fsdp", "sp"), None),
        ),
        out_specs=(
            P(("fsdp", "sp"), None),
            P(("fsdp", "sp"), None),
            P("fsdp", None),
            P("fsdp", None),
            P("fsdp", None),
            P("fsdp", None),
            P("fsdp", None),
            P("fsdp"),
            P("fsdp"),
            P("fsdp", "sp", None),
            P("fsdp", "sp", None),
            P("fsdp", None, "sp"),
        ),
        check_vma=False,
    )
```

```python
import functools
import math

import jax
import jax.numpy as jnp
from jax import lax
from jax.experimental import pallas as pl
from jax.experimental.pallas import tpu as pltpu
from jax.sharding import PartitionSpec as P

MODEL_WIDTH = 1024
QUERY_HEADS = 16
KEY_VALUE_HEADS = 8
HEAD_SIZE = 64
EXPERTS = 32
SPAN = 256
CAP = 192


NORM_EPS = 1e-06
ROPE_BASE = 10000.0
MASKED = -1e30
VMEM_LIMIT = 60 * 1024 * 1024


def contract(left, right, left_dim, right_dim):
    return lax.dot_general(
        left, right, (((left_dim,), (right_dim,)), ((), ())), preferred_element_type=jnp.float32
    )


def axis_bits(count):
    bits = [1 << place for place in range(count.bit_length() - 1)]
    return bits[::-1]


def flip(values, axis_name, bit):
    count = lax.axis_size(axis_name)
    return lax.ppermute(values, axis_name, [(place, place ^ bit) for place in range(count)])


def stage_orders(count):
    high = axis_bits(count)
    if count <= 2:
        return (high, high)
    return (high, high[1:2] + high[:1] + high[2:])


def gather_pieces(values, axis_name):
    count = lax.axis_size(axis_name)
    half = values.shape[1] // 2
    lists = []
    for order, part in zip(stage_orders(count), (values[:, :half], values[:, half:])):
        pieces = {0: part}
        for bit in order:
            pieces.update({r ^ bit: flip(piece, axis_name, bit) for r, piece in list(pieces.items())})
        lists.append([pieces[r] for r in range(count)])
    return lists


def chunk_place(index, order):
    place = 0
    for bit in order:
        place = place * 2 + (index * 2 // bit) % 2
    return place


def reduce_halves(leave, stay, axis_name):
    count = lax.axis_size(axis_name)
    sums = []
    for order, gone, kept in zip(stage_orders(count), leave, stay):
        for bit in order[::-1]:
            arrived = flip(gone, axis_name, bit).astype(jnp.float32)
            middle = kept.shape[0] // 2
            if middle:
                gone = (kept[middle:].astype(jnp.float32) + arrived[middle:]).astype(jnp.bfloat16)
                kept = (kept[:middle].astype(jnp.float32) + arrived[:middle]).astype(jnp.bfloat16)
            else:
                kept = kept[0].astype(jnp.float32) + arrived[0]
        sums.append(kept)
    return jnp.concatenate(sums, axis=1)


def reduce_rows(values, axis_name):
    count = lax.axis_size(axis_name)
    half = values.shape[2] // 2
    leave, stay = [], []
    for order, part in zip(stage_orders(count), (values[:, :, :half], values[:, :, half:])):
        later = order[:-1][::-1]
        evens = sorted(range(count // 2), key=lambda i: chunk_place(i, later))
        leave.append(jnp.stack([part[2 * i + 1] for i in evens]))
        stay.append(jnp.stack([part[2 * i] for i in evens]))
    return reduce_halves(leave, stay, axis_name)


def pack_expert(gate, up, down):
    rows = gate.shape[0]
    blocks = [down[k * rows : (k + 1) * rows] for k in range(down.shape[0] // rows)]
    return jnp.concatenate([gate, up, jnp.concatenate(blocks, axis=1)], axis=0)


def expert_step(slot_ref, share_ref, weight_ref, *refs, count):
    acts, cots = refs[: 2 * count], refs[2 * count : 4 * count]
    mixed_ref, back_ref, share_grad_ref, weight_grad_ref = refs[4 * count : 4 * count + 4]
    act_buf, cot_buf, arrive, act_rows, hidden_rows, down_rows, gate_rows, up_rows = refs[
        4 * count + 4 :
    ]
    pair, rows = act_buf.shape[1], act_buf.shape[3]
    shards, packed_rows, hidden_width = weight_ref.shape
    deep = packed_rows // 3
    width = shards * deep
    step, steps = pl.program_id(0), pl.num_programs(0)

    def copies(first, slot):
        made = []
        for source in range(pair):
            for half in range(2):
                lane = 2 * source + half
                index = half * count + first + source
                made.append(
                    pltpu.make_async_copy(
                        acts[index], act_buf.at[slot, source, half], arrive.at[slot, 0, lane]
                    )
                )
                made.append(
                    pltpu.make_async_copy(
                        cots[index], cot_buf.at[slot, source, half], arrive.at[slot, 1, lane]
                    )
                )
        return made

    def fetch(target, slot):
        for known in range(count // pair):

            @pl.when(target == known)
            def _():
                for copy in copies(known * pair, slot):
                    copy.start()

    @pl.when(step == 0)
    def _():
        fetch(0, 0)

    @pl.when(step + 1 < steps)
    def _():
        fetch(step + 1, (step + 1) % 2)

    slot = step % 2
    for copy in copies(0, slot):
        copy.wait()

    gate_w = weight_ref[:, :deep, :].reshape(width, hidden_width)
    up_w = weight_ref[:, deep : 2 * deep, :].reshape(width, hidden_width)

    def down_w(shard):
        part = weight_ref[shard, 2 * deep :, :]
        blocks = [part[:, k * deep : (k + 1) * deep] for k in range(hidden_width // deep)]
        return jnp.concatenate(blocks, axis=0)

    picked, cots_here, shares, masks = [], [], [], []
    for source in range(pair):
        mask = lax.broadcasted_iota(jnp.int32, (CAP, rows), 0) == slot_ref[source]
        choose = jnp.where(mask, 1.0, 0.0).astype(jnp.bfloat16)
        picked.append(
            jnp.concatenate(
                [contract(choose, act_buf[slot, source, half], 1, 0) for half in range(2)], axis=1
            )
        )
        cots_here.append(
            jnp.concatenate(
                [contract(choose, cot_buf[slot, source, half], 1, 0) for half in range(2)], axis=1
            )
        )
        shares.append(jnp.sum(jnp.where(mask, share_ref[source], 0.0), axis=1, keepdims=True))
        masks.append(mask)
    act = jnp.concatenate(picked, 0).astype(jnp.bfloat16)
    cot = jnp.concatenate(cots_here, 0)
    share = jnp.concatenate(shares, 0)
    gate_pre = contract(act, gate_w, 1, 0)
    up_pre = contract(act, up_w, 1, 0)
    sigmoid = 1.0 / (1.0 + jnp.exp(-gate_pre))
    silu = gate_pre * sigmoid
    hidden = (silu * up_pre).astype(jnp.bfloat16)
    made = jnp.concatenate(
        [contract(hidden, down_w(shard), 1, 0) for shard in range(shards)], axis=1
    )
    made = made.astype(jnp.bfloat16).astype(jnp.float32)
    share_grad = jnp.sum(made * cot, axis=1, keepdims=True)
    mixed = (made * share).astype(jnp.bfloat16)
    made_grad = (share * cot).astype(jnp.bfloat16)
    hidden_grad = sum(
        contract(made_grad[:, shard * deep : (shard + 1) * deep], down_w(shard), 1, 1)
        for shard in range(shards)
    )
    up_grad = (hidden_grad * silu).astype(jnp.bfloat16)
    gate_grad = (
        hidden_grad * up_pre * sigmoid * (1.0 + gate_pre * (1.0 - sigmoid))
    ).astype(jnp.bfloat16)
    back = (contract(gate_grad, gate_w, 1, 1) + contract(up_grad, up_w, 1, 1)).astype(jnp.bfloat16)
    for source in range(pair):
        part = slice(source * CAP, (source + 1) * CAP)
        mixed_ref[source] = mixed[part]
        back_ref[source] = back[part]
        share_grad_ref[source] = jnp.sum(
            jnp.where(masks[source], share_grad[part], 0.0), axis=0, keepdims=True
        )
    here = pl.ds(pl.multiple_of(step * pair * CAP, pair * CAP), pair * CAP)
    act_rows[here, :] = act
    hidden_rows[here, :] = hidden
    down_rows[here, :] = made_grad
    gate_rows[here, :] = gate_grad
    up_rows[here, :] = up_grad

    @pl.when(step == steps - 1)
    def _():
        gate_sum = contract(act_rows[...], gate_rows[...], 0, 0).astype(jnp.bfloat16)
        weight_grad_ref[:, :deep, :] = gate_sum.reshape(shards, deep, hidden_width)
        up_sum = contract(act_rows[...], up_rows[...], 0, 0).astype(jnp.bfloat16)
        weight_grad_ref[:, deep : 2 * deep, :] = up_sum.reshape(shards, deep, hidden_width)
        for shard in range(shards):
            cols = slice(shard * deep, (shard + 1) * deep)
            down_sum = contract(hidden_rows[...], down_rows[:, cols], 0, 0).astype(jnp.bfloat16)
            for k in range(hidden_width // deep):
                weight_grad_ref[shard, 2 * deep :, k * deep : (k + 1) * deep] = down_sum[
                    k * deep : (k + 1) * deep
                ]


def run_expert(slots, shares, weights, acts, cots):
    count, rows = slots.shape
    half = acts[0].shape[1]
    hidden_width = weights.shape[2]
    pair = 2
    listed = count * CAP
    low = jnp.bfloat16

    def by_source(*shape):
        return pl.BlockSpec((pair,) + shape, lambda s: (s,) + (0,) * len(shape))

    anywhere = pl.BlockSpec(memory_space=pl.ANY)
    outs = pl.pallas_call(
        functools.partial(expert_step, count=count),
        grid=(count // pair,),
        in_specs=[by_source(1, rows), by_source(1, rows), whole_block(weights)]
        + [anywhere] * (4 * count),
        out_specs=[
            by_source(CAP, 2 * half),
            by_source(CAP, 2 * half),
            by_source(1, rows),
            pl.BlockSpec(weights.shape, lambda s: (0, 0, 0)),
        ],
        out_shape=[
            jax.ShapeDtypeStruct((count, CAP, 2 * half), low),
            jax.ShapeDtypeStruct((count, CAP, 2 * half), low),
            jax.ShapeDtypeStruct((count, 1, rows), jnp.float32),
            jax.ShapeDtypeStruct(weights.shape, low),
        ],
        scratch_shapes=[
            pltpu.VMEM((2, pair, 2, rows, half), low),
            pltpu.VMEM((2, pair, 2, rows, half), low),
            pltpu.SemaphoreType.DMA((2, 2, 2 * pair)),
            pltpu.VMEM((listed, 2 * half), low),
            pltpu.VMEM((listed, hidden_width), low),
            pltpu.VMEM((listed, 2 * half), low),
            pltpu.VMEM((listed, hidden_width), low),
            pltpu.VMEM((listed, hidden_width), low),
        ],
        compiler_params=pltpu.CompilerParams(
            dimension_semantics=("arbitrary",), vmem_limit_bytes=VMEM_LIMIT
        ),
        name="expert",
    )(slots[:, None], shares[:, None], weights, *acts, *cots)
    return (outs[0], outs[1], outs[2][:, 0], outs[3])


def combine_step(slot_ref, *refs):
    parts, (left_ref, right_ref) = refs[:-2], refs[-2:]
    experts = len(parts)
    rows, half = left_ref.shape[1:]
    place = lax.broadcasted_iota(jnp.int32, (rows, experts * CAP), 1)
    hit = None
    for expert in range(experts):
        slot = slot_ref[0, :, expert : expert + 1]
        match = place == jnp.where(slot >= 0, slot + expert * CAP, -1)
        hit = match if hit is None else hit | match
    choose = jnp.where(hit, 1.0, 0.0).astype(jnp.bfloat16)
    listed = jnp.concatenate([part[0] for part in parts], axis=0)
    total = contract(choose, listed, 1, 0).astype(jnp.bfloat16)
    left_ref[0] = total[:, :half]
    right_ref[0] = total[:, half:]


def combine_rows(slots_by_row, parts, odd):
    sources, rows, experts = slots_by_row.shape
    width = parts[0].shape[2]
    orders = [order[:-1][::-1] for order in stage_orders(sources)]

    def half_of(order):
        return pl.BlockSpec((1, rows, width // 2), lambda i: (chunk_place(i, order), 0, 0))

    return pl.pallas_call(
        combine_step,
        grid=(sources // 2,),
        in_specs=[pl.BlockSpec((1, rows, experts), lambda i: (2 * i + odd, 0, 0))]
        + [pl.BlockSpec((1, CAP, width), lambda i: (2 * i + odd, 0, 0))] * experts,
        out_specs=[half_of(order) for order in orders],
        out_shape=[jax.ShapeDtypeStruct((sources // 2, rows, width // 2), jnp.bfloat16)] * 2,
        compiler_params=pltpu.CompilerParams(
            dimension_semantics=("arbitrary",), vmem_limit_bytes=VMEM_LIMIT
        ),
        name="combine",
    )(slots_by_row, *parts)


def ring_pieces(values, axis_name):
    count = lax.axis_size(axis_name)
    ahead = [(place, (place + 1) % count) for place in range(count)]
    behind = [(place, (place - 1) % count) for place in range(count)]
    half = values.shape[1] // 2
    lists = []
    for pairs, part in ((ahead, values[:, :half]), (behind, values[:, half:])):
        pieces = [part]
        for _ in range(count - 1):
            pieces.append(lax.ppermute(pieces[-1], axis_name, pairs))
        lists.append(pieces)
    return lists


def ring_reduce(values, axis_name):
    count = lax.axis_size(axis_name)
    ahead = [(place, (place + 1) % count) for place in range(count)]
    behind = [(place, (place - 1) % count) for place in range(count)]
    half = values.shape[2] // 2
    sums = []
    for pairs, turn, part in ((ahead, -1, values[:, :, :half]), (behind, 1, values[:, :, half:])):
        moving = part[turn % count]
        for step in range(1, count):
            moving = lax.ppermute(moving, axis_name, pairs)
            own = part[(turn * (step + 1)) % count]
            moving = moving.astype(jnp.float32) + own.astype(jnp.float32)
            if step < count - 1:
                moving = moving.astype(jnp.bfloat16)
        sums.append(moving)
    return jnp.concatenate(sums, axis=1)


def sequence_starts(length_row, places):
    count = length_row.shape[0]
    ends = [length_row[0]]
    for index in range(1, count):
        ends.append(ends[-1] + length_row[index])
    first = jnp.zeros_like(places)
    for index in range(count - 1):
        first = jnp.where(places >= ends[index], ends[index], first)
    return first


def turn_halves(values, cosine, sine, turned_lanes):
    groups = []
    for first in range(0, values.shape[1], 128):
        group = values[:, first : first + 128]
        lane = lax.broadcasted_iota(jnp.int32, group.shape, 1)
        partner = jnp.where(
            lane % HEAD_SIZE < HEAD_SIZE // 2,
            pltpu.roll(group, 128 - HEAD_SIZE // 2, 1),
            pltpu.roll(group, HEAD_SIZE // 2, 1),
        )
        turned = group * cosine + partner * sine
        groups.append(jnp.where(lane + first < turned_lanes, turned, group))
    return jnp.concatenate(groups, axis=1)


def scale_rows(values):
    return lax.rsqrt(jnp.mean(values * values, axis=1, keepdims=True) + NORM_EPS)


def project_step(order_ref, gain_ref, weight_ref, cos_ref, sin_ref, *refs):
    pieces, (rows_ref, query_ref, key_ref, value_ref) = refs[:-4], refs[-4:]
    count = len(pieces) // 2
    span, width = rows_ref.shape
    token_rows = pieces[0].shape[0]
    first = pl.program_id(0) * span
    places = first + lax.broadcasted_iota(jnp.int32, (span, token_rows), 0)
    left, right = 0.0, 0.0
    for index in range(count):
        part = order_ref[:, index * token_rows : (index + 1) * token_rows]
        choose = jnp.where(part == places, 1.0, 0.0).astype(jnp.bfloat16)
        left = left + contract(choose, pieces[index][...], 1, 0)
        right = right + contract(choose, pieces[count + index][...], 1, 0)
    values = jnp.concatenate([left, right], axis=1)
    rows_ref[...] = values.astype(jnp.bfloat16)
    act = (values * scale_rows(values) * gain_ref[...]).astype(jnp.bfloat16)
    made = contract(act, weight_ref[...], 1, 0)
    share = made.shape[1] // 4
    made = turn_halves(made, cos_ref[...], sin_ref[...], 3 * share).astype(jnp.bfloat16)
    query_ref[...] = made[:, : 2 * share]
    key_ref[...] = made[:, 2 * share : 3 * share]
    value_ref[...] = made[:, 3 * share :]


def whole_block(array):
    return pl.BlockSpec(
        array.shape, lambda *_: (0,) * array.ndim, pipeline_mode=pl.Buffered(1)
    )


def row_block(width):
    return pl.BlockSpec((SPAN, width), lambda i, *_: (i, 0))


def project(order_row, gain, weight, cosine, sine, pieces):
    rows = order_row.shape[1]
    width, columns = weight.shape
    share = columns // 4
    low = jnp.bfloat16
    return pl.pallas_call(
        project_step,
        grid=(rows // SPAN,),
        in_specs=[
            whole_block(order_row),
            whole_block(gain),
            whole_block(weight),
            row_block(128),
            row_block(128),
        ]
        + [whole_block(piece) for piece in pieces],
        out_specs=[row_block(width), row_block(2 * share), row_block(share), row_block(share)],
        out_shape=[
            jax.ShapeDtypeStruct((rows, width), low),
            jax.ShapeDtypeStruct((rows, 2 * share), low),
            jax.ShapeDtypeStruct((rows, share), low),
            jax.ShapeDtypeStruct((rows, share), low),
        ],
        compiler_params=pltpu.CompilerParams(
            dimension_semantics=("arbitrary",), vmem_limit_bytes=VMEM_LIMIT
        ),
        name="project",
    )(order_row, gain, weight, cosine, sine, *pieces)


def stack_heads(values, lanes):
    lane = lax.broadcasted_iota(jnp.int32, (values.shape[0], lanes), 1)
    blocks = []
    for member in range(values.shape[1] // lanes):
        part = values[:, member * lanes : (member + 1) * lanes]
        for head in range(lanes // HEAD_SIZE):
            blocks.append(jnp.where(lane // HEAD_SIZE == head, part, jnp.zeros_like(part)))
    return jnp.concatenate(blocks, axis=0)


def unstack_heads(values, lanes, span):
    lane = lax.broadcasted_iota(jnp.int32, (span, lanes), 1)
    heads = lanes // HEAD_SIZE
    members = []
    for member in range(values.shape[0] // span // heads):
        merged = None
        for head in range(heads):
            first = (member * heads + head) * span
            part = values[first : first + span]
            merged = part if merged is None else jnp.where(lane // HEAD_SIZE == head, part, merged)
        members.append(merged)
    return jnp.concatenate(members, axis=1)


def allowed_pairs(start_ref, block, key_block, span):
    query_place = block * span + lax.broadcasted_iota(jnp.int32, (span, span), 0)
    key_place = key_block * span + lax.broadcasted_iota(jnp.int32, (span, span), 1)
    return (key_place <= query_place) & (key_place >= start_ref[...])


def mask_scores(scores, allowed):
    span = allowed.shape[0]
    heads = scores.shape[0] // span
    stacked = scores.reshape(heads, span, span)
    return jnp.where(allowed[None], stacked, MASKED).reshape(scores.shape)


def attend_step(lowest_ref, start_ref, query_ref, key_ref, value_ref, out_ref, log_ref, best, accum):
    block = pl.program_id(0)
    span = query_ref.shape[0]
    lanes = key_ref.shape[1]
    query = stack_heads(query_ref[...], lanes) * jnp.bfloat16(1.0 / math.sqrt(HEAD_SIZE))
    lowest = lowest_ref[block]

    def scores_of(key_block):
        here = pl.ds(pl.multiple_of(key_block * span, span), span)
        scores = contract(query, key_ref[here, :], 1, 1)
        return mask_scores(scores, allowed_pairs(start_ref, block, key_block, span))

    best[...] = scores_of(block)

    def look(key_block, _):
        best[...] = jnp.maximum(best[...], scores_of(key_block))
        return 0

    lax.fori_loop(lowest, block, look, 0)
    top = jnp.max(best[...], axis=1, keepdims=True)
    accum[...] = jnp.zeros_like(accum)

    def visit(key_block, _):
        here = pl.ds(pl.multiple_of(key_block * span, span), span)
        terms = jnp.exp(scores_of(key_block) - top).astype(jnp.bfloat16)
        values = value_ref[here, :]
        values = jnp.concatenate([values, jnp.ones((span, 128), jnp.bfloat16)], axis=1)
        accum[...] += contract(terms, values, 1, 0)
        return 0

    lax.fori_loop(lowest, block + 1, visit, 0)
    total = accum[:, lanes : lanes + 1]
    out_ref[...] = unstack_heads(accum[:, :lanes] / total, lanes, span).astype(jnp.bfloat16)
    logs = top + jnp.log(total)
    heads = logs.shape[0] // span
    log_ref[...] = jnp.concatenate(
        [logs[head * span : (head + 1) * span] for head in range(heads)], axis=1
    )


def attend(lowest, start, query, key, value):
    rows, columns = query.shape
    lanes = key.shape[1]
    heads = columns // HEAD_SIZE
    return pl.pallas_call(
        attend_step,
        grid_spec=pltpu.PrefetchScalarGridSpec(
            num_scalar_prefetch=1,
            grid=(rows // SPAN,),
            in_specs=[row_block(1), row_block(columns), whole_block(key), whole_block(value)],
            out_specs=[row_block(columns), row_block(heads)],
            scratch_shapes=[
                pltpu.VMEM((heads * SPAN, SPAN), jnp.float32),
                pltpu.VMEM((heads * SPAN, lanes + 128), jnp.float32),
            ],
        ),
        out_shape=[
            jax.ShapeDtypeStruct((rows, columns), jnp.bfloat16),
            jax.ShapeDtypeStruct((rows, heads), jnp.float32),
        ],
        compiler_params=pltpu.CompilerParams(
            dimension_semantics=("arbitrary",), vmem_limit_bytes=VMEM_LIMIT
        ),
        name="attend",
    )(lowest, start, query, key, value)


def attend_back_step(
    lowest_ref,
    start_ref,
    log_ref,
    query_ref,
    out_ref,
    cot_ref,
    key_ref,
    value_ref,
    query_grad_ref,
    key_grad_ref,
    value_grad_ref,
    accum,
):
    block = pl.program_id(0)
    span = query_ref.shape[0]
    lanes = key_ref.shape[1]
    scale = 1.0 / math.sqrt(HEAD_SIZE)

    @pl.when(block == 0)
    def _():
        key_grad_ref[...] = jnp.zeros_like(key_grad_ref)
        value_grad_ref[...] = jnp.zeros_like(value_grad_ref)

    query = stack_heads(query_ref[...], lanes) * jnp.bfloat16(scale)
    cot = stack_heads(cot_ref[...], lanes)
    out = stack_heads(out_ref[...], lanes)
    dots = jnp.sum(cot.astype(jnp.float32) * out.astype(jnp.float32), axis=1, keepdims=True)
    heads = log_ref.shape[1]
    logs = jnp.concatenate([log_ref[:, head : head + 1] for head in range(heads)], axis=0)
    accum[...] = jnp.zeros_like(accum)

    def visit(key_block, _):
        here = pl.ds(pl.multiple_of(key_block * span, span), span)
        keys = key_ref[here, :]
        scores = contract(query, keys, 1, 1)
        scores = mask_scores(scores, allowed_pairs(start_ref, block, key_block, span))
        probs = jnp.exp(scores - logs)
        prob_grad = contract(cot, value_ref[here, :], 1, 1)
        score_grad = (probs * (prob_grad - dots)).astype(jnp.bfloat16)
        accum[...] += contract(score_grad, keys, 1, 0)
        key_grad_ref[here, :] += contract(score_grad, query, 0, 0)
        value_grad_ref[here, :] += contract(probs.astype(jnp.bfloat16), cot, 0, 0)
        return 0

    lax.fori_loop(lowest_ref[block], block + 1, visit, 0)
    query_grad_ref[...] = unstack_heads(accum[...] * scale, lanes, span)


def attend_back(lowest, start, logs, query, out, cot, key, value):
    rows, columns = query.shape
    lanes = key.shape[1]
    heads = columns // HEAD_SIZE
    return pl.pallas_call(
        attend_back_step,
        grid_spec=pltpu.PrefetchScalarGridSpec(
            num_scalar_prefetch=1,
            grid=(rows // SPAN,),
            in_specs=[
                row_block(1),
                row_block(heads),
                row_block(columns),
                row_block(columns),
                row_block(columns),
                whole_block(key),
                whole_block(value),
            ],
            out_specs=[
                row_block(columns),
                pl.BlockSpec((rows, lanes), lambda *_: (0, 0)),
                pl.BlockSpec((rows, lanes), lambda *_: (0, 0)),
            ],
            scratch_shapes=[pltpu.VMEM((heads * SPAN, lanes), jnp.float32)],
        ),
        out_shape=[
            jax.ShapeDtypeStruct((rows, columns), jnp.float32),
            jax.ShapeDtypeStruct((rows, lanes), jnp.float32),
            jax.ShapeDtypeStruct((rows, lanes), jnp.float32),
        ],
        compiler_params=pltpu.CompilerParams(
            dimension_semantics=("arbitrary",), vmem_limit_bytes=VMEM_LIMIT
        ),
        name="attend_back",
    )(lowest, start, logs, query, out, cot, key, value)


def project_back_step(
    own_ref,
    order_ref,
    gain_ref,
    weight_ref,
    cos_ref,
    sin_ref,
    query_ref,
    key_ref,
    value_ref,
    rows_ref,
    residual_ref,
    out_ref,
    weight_grad_ref,
    gain_grad_ref,
    act_rows,
    grad_rows,
    token_rows,
    gain_sum,
):
    phase, block = pl.program_id(0), pl.program_id(1)
    blocks = pl.num_programs(1)
    span, width = rows_ref.shape
    here = pl.ds(pl.multiple_of(block * span, span), span)

    @pl.when(phase == 0)
    def _():
        grads = jnp.concatenate([query_ref[...], key_ref[...], value_ref[...]], axis=1)
        share = grads.shape[1] // 4
        grads = turn_halves(grads, cos_ref[...], -sin_ref[...], 3 * share).astype(jnp.bfloat16)
        values = rows_ref[...].astype(jnp.float32)
        scale = scale_rows(values)
        normed = values * scale
        gain = gain_ref[...]
        act_grad = contract(grads, weight_ref[...], 1, 1)
        scaled = act_grad * gain
        token_grad = scale * (scaled - normed * jnp.mean(scaled * normed, axis=1, keepdims=True))
        per_device = residual_ref.shape[0]
        offset = block * span - own_ref[0] * per_device
        owned = (offset >= 0) & (offset < per_device)
        at = pl.ds(pl.multiple_of(jnp.where(owned, offset, 0), span), span)
        residual = jnp.where(owned, residual_ref[at, :].astype(jnp.float32), 0.0)
        token_rows[here, :] = (token_grad + residual).astype(jnp.bfloat16)
        act_rows[here, :] = (normed * gain).astype(jnp.bfloat16)
        grad_rows[here, :] = grads
        part = jnp.sum(act_grad * normed, axis=0, keepdims=True)

        @pl.when(block == 0)
        def _():
            gain_sum[...] = part

        @pl.when(block > 0)
        def _():
            gain_sum[...] += part

        @pl.when(block == blocks - 1)
        def _():
            weight_grad_ref[...] = contract(act_rows[...], grad_rows[...], 0, 0).astype(
                jnp.bfloat16
            )
            gain_grad_ref[...] = gain_sum[...]

    @pl.when(phase == 1)
    def _():
        total = token_rows.shape[0]
        places = lax.broadcasted_iota(jnp.int32, (span, total), 1)
        choose = jnp.where(order_ref[...] == places, 1.0, 0.0).astype(jnp.bfloat16)
        out_ref[...] = contract(choose, token_rows[...], 1, 0).astype(jnp.bfloat16)


def project_back(own, order_column, gain, weight, cosine, sine, query_grad, key_grad, value_grad, rows_in, residual):
    rows, width = rows_in.shape
    columns = weight.shape[1]
    share = columns // 4
    blocks = rows // SPAN
    low = jnp.bfloat16

    def early(columns):
        return pl.BlockSpec((SPAN, columns), lambda p, i, *_: (jnp.where(p == 0, i, blocks - 1), 0))

    def late(columns):
        return pl.BlockSpec((SPAN, columns), lambda p, i, *_: (jnp.where(p == 0, 0, i), 0))

    return pl.pallas_call(
        project_back_step,
        grid_spec=pltpu.PrefetchScalarGridSpec(
            num_scalar_prefetch=1,
            grid=(2, blocks),
            in_specs=[
                late(1),
                whole_block(gain),
                whole_block(weight),
                early(128),
                early(128),
                early(2 * share),
                early(share),
                early(share),
                early(width),
                whole_block(residual),
            ],
            out_specs=[
                late(width),
                pl.BlockSpec((width, columns), lambda *_: (0, 0)),
                pl.BlockSpec((1, width), lambda *_: (0, 0)),
            ],
            scratch_shapes=[
                pltpu.VMEM((rows, width), low),
                pltpu.VMEM((rows, columns), low),
                pltpu.VMEM((rows, width), low),
                pltpu.VMEM((1, width), jnp.float32),
            ],
        ),
        out_shape=[
            jax.ShapeDtypeStruct((rows, width), low),
            jax.ShapeDtypeStruct((width, columns), low),
            jax.ShapeDtypeStruct((1, width), jnp.float32),
        ],
        compiler_params=pltpu.CompilerParams(
            dimension_semantics=("arbitrary", "arbitrary"), vmem_limit_bytes=VMEM_LIMIT
        ),
        name="project_back",
    )(own, order_column, gain, weight, cosine, sine, query_grad, key_grad, value_grad, rows_in, residual)


def body(
    tokens,
    query_weight,
    key_projection_weight,
    value_projection_weight,
    output_weight,
    router_weight,
    first_gain,
    second_gain,
    expert_gate,
    expert_up,
    expert_down,
    routes,
    dealing,
    lengths,
    cotangent,
):
    low = jnp.bfloat16
    token_rows = tokens.shape[0]
    sp_count = lax.axis_size("sp")
    sp_index = lax.axis_index("sp")
    fsdp_count = lax.axis_size("fsdp")
    fsdp_index = lax.axis_index("fsdp")
    group_rows = token_rows * sp_count
    local_experts = EXPERTS // fsdp_count
    kept_heads = KEY_VALUE_HEADS // sp_count
    ratio = QUERY_HEADS // KEY_VALUE_HEADS
    share = kept_heads * HEAD_SIZE
    shard_rows = query_weight.shape[0]
    relative = fsdp_index ^ jnp.arange(fsdp_count, dtype=jnp.int32)

    def own_columns(weight, heads):
        part = lax.dynamic_slice_in_dim(weight, sp_index * heads * HEAD_SIZE, heads * HEAD_SIZE, 1)
        return part.astype(low)

    query_part = own_columns(query_weight, kept_heads * ratio)
    query_part = query_part.reshape(shard_rows, kept_heads, ratio, HEAD_SIZE)
    query_part = jnp.swapaxes(query_part, 1, 2).reshape(shard_rows, ratio * share)
    packed = jnp.concatenate(
        [
            query_part,
            own_columns(key_projection_weight, kept_heads),
            own_columns(value_projection_weight, kept_heads),
            output_weight.astype(low),
            router_weight.astype(low),
            first_gain.astype(low)[:, None],
            second_gain.astype(low)[:, None],
            jnp.zeros((shard_rows, 128 - EXPERTS - 2), low),
        ],
        axis=1,
    )
    packed_all = lax.all_gather(packed, "fsdp", axis=0, tiled=True)
    qkv_columns = (ratio + 2) * share
    qkv_weight = packed_all[:, :qkv_columns]
    output_full = packed_all[:, qkv_columns : qkv_columns + MODEL_WIDTH]
    output_full = output_full.reshape(sp_count, kept_heads, ratio, HEAD_SIZE, MODEL_WIDTH)
    output_full = jnp.swapaxes(output_full, 1, 2).reshape(sp_count, ratio * share, MODEL_WIDTH)
    rest = packed_all[:, qkv_columns + MODEL_WIDTH :]
    router_full = rest[:, :EXPERTS]
    gain_attend = rest[:, EXPERTS].astype(jnp.float32)[None, :]
    gain_mixer = rest[:, EXPERTS + 1].astype(jnp.float32)[None, :]

    left, right = ring_pieces(tokens, "sp")
    pieces = [left[-k % sp_count] for k in range(sp_count)] + right
    expert_parts = [
        pack_expert(expert_gate[e].astype(low), expert_up[e].astype(low), expert_down[e].astype(low))
        for e in range(local_experts)
    ]
    *expert_parts, routes, _, _ = lax.optimization_barrier(
        (*expert_parts, routes, left[-1], right[-1])
    )
    cot_source, _, _ = lax.optimization_barrier((cotangent, left[1], right[1]))
    expert_weights = [lax.all_gather(part, "sp", axis=0, tiled=False) for part in expert_parts]
    order_row = dealing[0]
    order_here = lax.dynamic_slice_in_dim(
        jnp.concatenate([order_row, order_row]), sp_index * token_rows, group_rows
    )
    places = jnp.arange(group_rows, dtype=jnp.int32)
    starts = sequence_starts(lengths[0], places)
    lowest = starts[::SPAN] // SPAN
    start_column = starts[:, None]
    half_dim = HEAD_SIZE // 2
    frequency = ROPE_BASE ** (-(jnp.arange(half_dim, dtype=jnp.float32) * 2.0 / HEAD_SIZE))
    angles = (places - starts).astype(jnp.float32)[:, None] * frequency[None, :]
    cosine = jnp.tile(jnp.cos(angles), (1, 4))
    sine = jnp.sin(angles)
    sine = jnp.concatenate([-sine, sine, -sine, sine], axis=1)

    rows_initial, query, key, value = project(
        order_here[None, :], gain_attend, qkv_weight, cosine, sine, pieces
    )
    attended, logs = attend(lowest, start_column, query, key, value)
    attn_back = lax.all_to_all(
        attended.reshape(sp_count, token_rows, ratio * share),
        "sp",
        split_axis=0,
        concat_axis=0,
        tiled=True,
    )
    resid = lax.dynamic_slice_in_dim(rows_initial, sp_index * token_rows, token_rows)
    branch = jnp.einsum("stc,scd->td", attn_back, output_full, preferred_element_type=jnp.float32)
    middle = resid.astype(jnp.float32) + branch
    inv_two = lax.rsqrt(jnp.mean(middle * middle, axis=1, keepdims=True) + NORM_EPS)
    normed_two = middle * inv_two
    act_two = (normed_two * gain_mixer).astype(low)
    logits = jnp.dot(act_two, router_full, preferred_element_type=jnp.float32)
    expert_range = jnp.arange(EXPERTS, dtype=jnp.int32)
    member = jnp.any(routes[:, :, None] == expert_range[None, None, :], axis=1)
    row_range = jnp.arange(token_rows, dtype=jnp.int32)
    upto = (row_range[:, None] <= row_range[None, :]).astype(low)
    rank = jnp.dot(member.T.astype(low), upto, preferred_element_type=jnp.float32)
    slots = jnp.where(member.T, rank.astype(jnp.int32) - 1, -1)

    def to_experts(by_expert):
        arrived = lax.all_to_all(
            by_expert.reshape(fsdp_count, local_experts, token_rows),
            "fsdp",
            split_axis=0,
            concat_axis=0,
            tiled=True,
        )
        return jnp.swapaxes(jnp.take(arrived, relative, axis=0), 0, 1)

    slots_here = to_experts(slots)
    gate_dense = jax.nn.softmax(jnp.where(member, logits, -jnp.inf), axis=-1)
    gates_here = to_experts(gate_dense.T)
    cot_left, cot_right = gather_pieces(cot_source, "fsdp")
    act_left, act_right = gather_pieces(act_two, "fsdp")
    mixed_rows, back_rows, gate_grads, expert_sums = [], [], [], []
    for e in range(local_experts):
        mixed, back, gate_grad, weight_grad = run_expert(
            slots_here[e], gates_here[e], expert_weights[e], act_left + act_right, cot_left + cot_right
        )
        mixed_rows.append(mixed)
        back_rows.append(back)
        gate_grads.append(gate_grad)
        expert_sums.append(lax.psum_scatter(weight_grad, "sp", scatter_dimension=0, tiled=False))
    gate_grads = jnp.stack(gate_grads, axis=1)
    slots_by_row = jnp.transpose(slots_here, (1, 2, 0))
    leave = combine_rows(slots_by_row, back_rows, 1)
    stay = combine_rows(slots_by_row, back_rows, 0)
    grad_act_moe = reduce_halves(leave, stay, "fsdp")
    upstream = cotangent.astype(jnp.float32)
    gate_grad_back = lax.all_to_all(
        jnp.take(gate_grads, relative, axis=0),
        "fsdp",
        split_axis=0,
        concat_axis=0,
        tiled=True,
    )
    gate_grad = gate_grad_back.reshape(EXPERTS, token_rows).T
    weighted = jnp.sum(gate_dense * gate_grad, axis=1, keepdims=True)
    logit_grad = (gate_dense * (gate_grad - weighted)).astype(low)
    grad_router_w = jnp.einsum("td,te->de", act_two, logit_grad, preferred_element_type=jnp.float32)
    grad_act_two = grad_act_moe + jnp.dot(
        logit_grad, router_full.T, preferred_element_type=jnp.float32
    )
    grad_gain_two = jnp.sum(grad_act_two * normed_two, axis=0)
    scaled_two = grad_act_two * gain_mixer
    grad_middle = upstream + inv_two * (
        scaled_two - normed_two * jnp.mean(scaled_two * normed_two, axis=1, keepdims=True)
    )
    middle_low = grad_middle.astype(low)
    grad_attn = jnp.einsum(
        "td,scd->stc", middle_low, output_full, preferred_element_type=jnp.float32
    ).astype(low)
    grad_heads = lax.all_to_all(
        grad_attn, "sp", split_axis=0, concat_axis=0, tiled=True
    ).reshape(group_rows, ratio * share)
    leave = combine_rows(slots_by_row, mixed_rows, 1)
    stay = combine_rows(slots_by_row, mixed_rows, 0)
    *leave, grad_heads = lax.optimization_barrier((*leave, grad_heads))
    mixture = reduce_halves(leave, stay, "fsdp")
    layer_out = (middle + mixture).astype(low)
    grad_output_w = jnp.einsum(
        "stc,td->scd", attn_back, middle_low, preferred_element_type=jnp.float32
    ).astype(low)
    grad_output_w = grad_output_w.reshape(sp_count, ratio, kept_heads, HEAD_SIZE, MODEL_WIDTH)
    grad_output_w = jnp.swapaxes(grad_output_w, 1, 2).reshape(MODEL_WIDTH, MODEL_WIDTH)
    early_grads = jnp.concatenate(
        [
            grad_output_w,
            grad_router_w.astype(low),
            grad_gain_two.astype(low)[:, None],
            jnp.zeros((MODEL_WIDTH, 256 - EXPERTS - 1), low),
        ],
        axis=1,
    ).reshape(fsdp_count, shard_rows, MODEL_WIDTH + 256)
    early_sum = reduce_rows(jnp.take(early_grads, relative, axis=0), "fsdp").astype(low)
    early_left, early_right = ring_pieces(early_sum, "sp")
    early_sum = jnp.concatenate(
        [sum(part.astype(jnp.float32) for part in parts) for parts in (early_left, early_right)],
        axis=1,
    )

    grad_query, grad_key, grad_value = attend_back(
        lowest, start_column, logs, query, attended, grad_heads, key, value
    )
    token_grads, grad_qkv, grad_gain_one = project_back(
        sp_index[None],
        order_here[:, None],
        gain_attend,
        qkv_weight,
        cosine,
        sine,
        grad_query,
        grad_key,
        grad_value,
        rows_initial,
        middle_low,
    )
    tokens_grad = ring_reduce(
        token_grads.reshape(sp_count, token_rows, MODEL_WIDTH), "sp"
    ).astype(low)
    late_grads = jnp.concatenate(
        [
            grad_qkv,
            grad_gain_one.astype(low).T,
            jnp.zeros((MODEL_WIDTH, 255), low),
        ],
        axis=1,
    ).reshape(fsdp_count, shard_rows, qkv_columns + 256)
    late_sum = reduce_rows(jnp.take(late_grads, relative, axis=0), "fsdp").astype(low)
    late_left, late_right = ring_pieces(late_sum, "sp")
    late_left = [late_left[-k % sp_count] for k in range(sp_count)]
    late_all = jnp.concatenate([jnp.stack(late_left), jnp.stack(late_right)], axis=2)
    late_all = jnp.take(late_all, (jnp.arange(sp_count) - sp_index) % sp_count, axis=0)
    late_all = late_all.astype(jnp.float32)
    query_sum = late_all[:, :, : ratio * share]
    query_sum = query_sum.reshape(sp_count, shard_rows, ratio, kept_heads, HEAD_SIZE)
    query_sum = jnp.transpose(query_sum, (1, 0, 3, 2, 4)).reshape(shard_rows, MODEL_WIDTH)
    key_sum = jnp.swapaxes(late_all[:, :, ratio * share : (ratio + 1) * share], 0, 1)
    deep = expert_gate.shape[1]

    def unpack_down(part):
        blocks = [part[:, k * deep : (k + 1) * deep] for k in range(part.shape[1] // deep)]
        return jnp.concatenate(blocks, axis=0)

    value_sum = jnp.swapaxes(late_all[:, :, (ratio + 1) * share : qkv_columns], 0, 1)
    return (
        layer_out,
        tokens_grad,
        query_sum,
        key_sum.reshape(shard_rows, KEY_VALUE_HEADS * HEAD_SIZE),
        value_sum.reshape(shard_rows, KEY_VALUE_HEADS * HEAD_SIZE),
        early_sum[:, :MODEL_WIDTH],
        early_sum[:, MODEL_WIDTH : MODEL_WIDTH + EXPERTS],
        jnp.sum(late_all[:, :, qkv_columns], axis=0),
        early_sum[:, MODEL_WIDTH + EXPERTS],
        jnp.stack([part[:deep] for part in expert_sums]).astype(jnp.float32),
        jnp.stack([part[deep : 2 * deep] for part in expert_sums]).astype(jnp.float32),
        jnp.stack([unpack_down(part[2 * deep :]) for part in expert_sums]).astype(jnp.float32),
    )


def solution(mesh):
    return jax.shard_map(
        body,
        mesh=mesh,
        in_specs=(
            P(("fsdp", "sp"), None),
            P("fsdp", None),
            P("fsdp", None),
            P("fsdp", None),
            P("fsdp", None),
            P("fsdp", None),
            P("fsdp"),
            P("fsdp"),
            P("fsdp", "sp", None),
            P("fsdp", "sp", None),
            P("fsdp", None, "sp"),
            P(("fsdp", "sp"), None),
            P("fsdp", None),
            P("fsdp", None),
            P(("fsdp", "sp"), None),
        ),
        out_specs=(
            P(("fsdp", "sp"), None),
            P(("fsdp", "sp"), None),
            P("fsdp", None),
            P("fsdp", None),
            P("fsdp", None),
            P("fsdp", None),
            P("fsdp", None),
            P("fsdp"),
            P("fsdp"),
            P("fsdp", "sp", None),
            P("fsdp", "sp", None),
            P("fsdp", None, "sp"),
        ),
        check_vma=False,
    )
```

```python
import functools
import math

import jax
import jax.numpy as jnp
from jax import lax
from jax.experimental import pallas as pl
from jax.experimental.pallas import tpu as pltpu
from jax.sharding import PartitionSpec as P

MODEL_WIDTH = 1024
QUERY_HEADS = 16
KEY_VALUE_HEADS = 8
HEAD_SIZE = 64
EXPERTS = 32
SPAN = 256
CAP = 192


NORM_EPS = 1e-06
ROPE_BASE = 10000.0
MASKED = -1e30
VMEM_LIMIT = 60 * 1024 * 1024


def contract(left, right, left_dim, right_dim):
    return lax.dot_general(
        left, right, (((left_dim,), (right_dim,)), ((), ())), preferred_element_type=jnp.float32
    )


def axis_bits(count):
    bits = [1 << place for place in range(count.bit_length() - 1)]
    return bits[::-1]


def flip(values, axis_name, bit):
    count = lax.axis_size(axis_name)
    return lax.ppermute(values, axis_name, [(place, place ^ bit) for place in range(count)])


def stage_orders(count):
    high = axis_bits(count)
    if count <= 2:
        return (high, high)
    return (high, high[1:2] + high[:1] + high[2:])


def gather_begin(values):
    half = values.shape[1] // 2
    return [{0: values[:, :half]}, {0: values[:, half:]}]


def gather_stage(lists, axis_name, stage, gates=()):
    count = lax.axis_size(axis_name)
    grown = []
    for order, pieces in zip(stage_orders(count), lists):
        keys = list(pieces)
        held = after([pieces[r] for r in keys], *gates) if gates else [pieces[r] for r in keys]
        new = dict(zip(keys, held))
        new.update({r ^ order[stage]: flip(new[r], axis_name, order[stage]) for r in keys})
        grown.append(new)
    return grown


def gather_end(lists):
    return [pieces[r] for pieces in lists for r in sorted(pieces)]


def newest(lists, stage):
    return [piece for pieces in lists for piece in list(pieces.values())[1 << stage :]]


def chunk_place(index, order):
    place = 0
    for bit in order:
        place = place * 2 + (index * 2 // bit) % 2
    return place


def reduce_stage(leave, stay, axis_name, stage):
    count = lax.axis_size(axis_name)
    gone_next, kept_next = [], []
    for order, gone, kept in zip(stage_orders(count), leave, stay):
        arrived = flip(gone, axis_name, order[::-1][stage])
        middle = kept.shape[0] // 2
        if middle:
            total = kept[middle:].astype(jnp.float32) + arrived[middle:].astype(jnp.float32)
            gone_next.append(total.astype(jnp.bfloat16))
            total = kept[:middle].astype(jnp.float32) + arrived[:middle].astype(jnp.float32)
            kept_next.append(total.astype(jnp.bfloat16))
        else:
            kept_next.append(kept[0].astype(jnp.float32) + arrived[0].astype(jnp.float32))
    return gone_next, kept_next


def after(values, *others):
    held = lax.optimization_barrier((*values, *others))
    return list(held[: len(values)])


def shift_pairs(count, by):
    return [(place, (place + by) % count) for place in range(count)]


def exchange_blocks(values, axis_name):
    return lax.all_to_all(values, axis_name, split_axis=0, concat_axis=0, tiled=True)


def pack_expert(gate, up, down):
    rows = gate.shape[0]
    blocks = [down[k * rows : (k + 1) * rows] for k in range(down.shape[0] // rows)]
    return jnp.concatenate([gate, up, jnp.concatenate(blocks, axis=1)], axis=0)


def expert_step(slot_ref, share_ref, weight_ref, *refs, count):
    acts, cots = refs[: 2 * count], refs[2 * count : 4 * count]
    mixed_ref, back_ref, share_grad_ref, weight_grad_ref = refs[4 * count : 4 * count + 4]
    act_buf, cot_buf, arrive, act_rows, hidden_rows, down_rows, gate_rows, up_rows = refs[
        4 * count + 4 :
    ]
    pair, rows = act_buf.shape[1], act_buf.shape[3]
    shards, packed_rows, hidden_width = weight_ref.shape
    deep = packed_rows // 3
    width = shards * deep
    step, steps = pl.program_id(0), pl.num_programs(0)

    def copies(first, slot):
        made = []
        for source in range(pair):
            for half in range(2):
                lane = 2 * source + half
                index = half * count + first + source
                made.append(
                    pltpu.make_async_copy(
                        acts[index], act_buf.at[slot, source, half], arrive.at[slot, 0, lane]
                    )
                )
                made.append(
                    pltpu.make_async_copy(
                        cots[index], cot_buf.at[slot, source, half], arrive.at[slot, 1, lane]
                    )
                )
        return made

    def fetch(target, slot):
        for known in range(count // pair):

            @pl.when(target == known)
            def _():
                for copy in copies(known * pair, slot):
                    copy.start()

    @pl.when(step == 0)
    def _():
        fetch(0, 0)

    @pl.when(step + 1 < steps)
    def _():
        fetch(step + 1, (step + 1) % 2)

    slot = step % 2
    for copy in copies(0, slot):
        copy.wait()

    gate_w = weight_ref[:, :deep, :].reshape(width, hidden_width)
    up_w = weight_ref[:, deep : 2 * deep, :].reshape(width, hidden_width)

    def down_w(shard):
        part = weight_ref[shard, 2 * deep :, :]
        blocks = [part[:, k * deep : (k + 1) * deep] for k in range(hidden_width // deep)]
        return jnp.concatenate(blocks, axis=0)

    picked, cots_here, shares, masks = [], [], [], []
    for source in range(pair):
        mask = lax.broadcasted_iota(jnp.int32, (CAP, rows), 0) == slot_ref[source]
        choose = jnp.where(mask, 1.0, 0.0).astype(jnp.bfloat16)
        picked.append(
            jnp.concatenate(
                [contract(choose, act_buf[slot, source, half], 1, 0) for half in range(2)], axis=1
            )
        )
        cots_here.append(
            jnp.concatenate(
                [contract(choose, cot_buf[slot, source, half], 1, 0) for half in range(2)], axis=1
            )
        )
        shares.append(jnp.sum(jnp.where(mask, share_ref[source], 0.0), axis=1, keepdims=True))
        masks.append(mask)
    act = jnp.concatenate(picked, 0).astype(jnp.bfloat16)
    cot = jnp.concatenate(cots_here, 0)
    share = jnp.concatenate(shares, 0)
    gate_pre = contract(act, gate_w, 1, 0)
    up_pre = contract(act, up_w, 1, 0)
    sigmoid = 1.0 / (1.0 + jnp.exp(-gate_pre))
    silu = gate_pre * sigmoid
    hidden = (silu * up_pre).astype(jnp.bfloat16)
    made = jnp.concatenate(
        [contract(hidden, down_w(shard), 1, 0) for shard in range(shards)], axis=1
    )
    made = made.astype(jnp.bfloat16).astype(jnp.float32)
    share_grad = jnp.sum(made * cot, axis=1, keepdims=True)
    mixed = (made * share).astype(jnp.bfloat16)
    made_grad = (share * cot).astype(jnp.bfloat16)
    hidden_grad = sum(
        contract(made_grad[:, shard * deep : (shard + 1) * deep], down_w(shard), 1, 1)
        for shard in range(shards)
    )
    up_grad = (hidden_grad * silu).astype(jnp.bfloat16)
    gate_grad = (
        hidden_grad * up_pre * sigmoid * (1.0 + gate_pre * (1.0 - sigmoid))
    ).astype(jnp.bfloat16)
    back = (contract(gate_grad, gate_w, 1, 1) + contract(up_grad, up_w, 1, 1)).astype(jnp.bfloat16)
    for source in range(pair):
        part = slice(source * CAP, (source + 1) * CAP)
        mixed_ref[source] = mixed[part]
        back_ref[source] = back[part]
        share_grad_ref[source] = jnp.sum(
            jnp.where(masks[source], share_grad[part], 0.0), axis=0, keepdims=True
        )
    here = pl.ds(pl.multiple_of(step * pair * CAP, pair * CAP), pair * CAP)
    act_rows[here, :] = act
    hidden_rows[here, :] = hidden
    down_rows[here, :] = made_grad
    gate_rows[here, :] = gate_grad
    up_rows[here, :] = up_grad

    @pl.when(step == steps - 1)
    def _():
        gate_sum = contract(act_rows[...], gate_rows[...], 0, 0).astype(jnp.bfloat16)
        up_sum = contract(act_rows[...], up_rows[...], 0, 0).astype(jnp.bfloat16)
        for shard in range(shards):
            cols = slice(shard * deep, (shard + 1) * deep)
            weight_grad_ref[shard, :deep, :] = gate_sum[cols]
            weight_grad_ref[shard, deep : 2 * deep, :] = up_sum[cols]
            down_sum = contract(hidden_rows[...], down_rows[:, cols], 0, 0).astype(jnp.bfloat16)
            for k in range(hidden_width // deep):
                weight_grad_ref[shard, 2 * deep :, k * deep : (k + 1) * deep] = down_sum[
                    k * deep : (k + 1) * deep
                ]


def run_expert(slots, shares, weights, acts, cots):
    count, rows = slots.shape
    half = acts[0].shape[1]
    hidden_width = weights.shape[2]
    pair = 2
    listed = count * CAP
    low = jnp.bfloat16

    def by_source(*shape):
        return pl.BlockSpec((pair,) + shape, lambda s, *_: (s,) + (0,) * len(shape))

    anywhere = pl.BlockSpec(memory_space=pl.ANY)
    outs = pl.pallas_call(
        functools.partial(expert_step, count=count),
        grid=(count // pair,),
        in_specs=[by_source(1, rows), by_source(1, rows), whole_block(weights)]
        + [anywhere] * (4 * count),
        out_specs=[
            by_source(CAP, 2 * half),
            by_source(CAP, 2 * half),
            by_source(1, rows),
            pl.BlockSpec(weights.shape, lambda *_: (0, 0, 0)),
        ],
        scratch_shapes=[
            pltpu.VMEM((2, pair, 2, rows, half), low),
            pltpu.VMEM((2, pair, 2, rows, half), low),
            pltpu.SemaphoreType.DMA((2, 2, 2 * pair)),
            pltpu.VMEM((listed, 2 * half), low),
            pltpu.VMEM((listed, hidden_width), low),
            pltpu.VMEM((listed, 2 * half), low),
            pltpu.VMEM((listed, hidden_width), low),
            pltpu.VMEM((listed, hidden_width), low),
        ],
        out_shape=[
            jax.ShapeDtypeStruct((count, CAP, 2 * half), low),
            jax.ShapeDtypeStruct((count, CAP, 2 * half), low),
            jax.ShapeDtypeStruct((count, 1, rows), jnp.float32),
            jax.ShapeDtypeStruct(weights.shape, low),
        ],
        compiler_params=pltpu.CompilerParams(
            dimension_semantics=("arbitrary",), vmem_limit_bytes=VMEM_LIMIT
        ),
        name="expert",
    )(slots[:, None], shares[:, None], weights, *acts, *cots)
    return (outs[0], outs[1], outs[2][:, 0], outs[3])


def combine_step(slot_ref, *refs):
    parts, (left_ref, right_ref) = refs[:-2], refs[-2:]
    experts = len(parts)
    rows, half = left_ref.shape[1:]
    place = lax.broadcasted_iota(jnp.int32, (rows, experts * CAP), 1)
    hit = None
    for expert in range(experts):
        slot = slot_ref[0, :, expert : expert + 1]
        match = place == jnp.where(slot >= 0, slot + expert * CAP, -1)
        hit = match if hit is None else hit | match
    choose = jnp.where(hit, 1.0, 0.0).astype(jnp.bfloat16)
    listed = jnp.concatenate([part[0] for part in parts], axis=0)
    total = contract(choose, listed, 1, 0).astype(jnp.bfloat16)
    left_ref[0] = total[:, :half]
    right_ref[0] = total[:, half:]


def combine_rows(slots_by_row, parts, odd):
    sources, rows, experts = slots_by_row.shape
    width = parts[0].shape[2]
    orders = [order[:-1][::-1] for order in stage_orders(sources)]

    def half_of(order):
        return pl.BlockSpec((1, rows, width // 2), lambda i: (chunk_place(i, order), 0, 0))

    return pl.pallas_call(
        combine_step,
        grid=(sources // 2,),
        in_specs=[pl.BlockSpec((1, rows, experts), lambda i: (2 * i + odd, 0, 0))]
        + [pl.BlockSpec((1, CAP, width), lambda i: (2 * i + odd, 0, 0))] * experts,
        out_specs=[half_of(order) for order in orders],
        out_shape=[jax.ShapeDtypeStruct((sources // 2, rows, width // 2), jnp.bfloat16)] * 2,
        compiler_params=pltpu.CompilerParams(
            dimension_semantics=("arbitrary",), vmem_limit_bytes=VMEM_LIMIT
        ),
        name="combine",
    )(slots_by_row, *parts)


def ring_begin(values):
    half = values.shape[1] // 2
    return [values[:, :half]], [values[:, half:]]


def ring_step(lists, axis_name, gates=()):
    count = lax.axis_size(axis_name)
    moving = [part[-1] for part in lists]
    if gates:
        moving = after(moving, *gates)
    return [
        part + [lax.ppermute(one, axis_name, shift_pairs(count, by))]
        for by, part, one in zip((1, -1), lists, moving)
    ]


def reduce_ring_begin(values):
    half = values.shape[2] // 2
    parts = (values[:, :, :half], values[:, :, half:])
    return [part[turn % values.shape[0]] for turn, part in zip((-1, 1), parts)], parts


def reduce_ring_step(state, axis_name, step, gates=()):
    moving, parts = state
    count = lax.axis_size(axis_name)
    if gates:
        moving = after(moving, *gates)
    made = []
    for turn, part, one in zip((-1, 1), parts, moving):
        arrived = lax.ppermute(one, axis_name, shift_pairs(count, -turn))
        own = part[(turn * (step + 1)) % count]
        total = arrived.astype(jnp.float32) + own.astype(jnp.float32)
        made.append(total.astype(jnp.bfloat16) if step < count - 1 else total)
    return made, parts


def sequence_starts(length_row, places):
    count = length_row.shape[0]
    ends = [length_row[0]]
    for index in range(1, count):
        ends.append(ends[-1] + length_row[index])
    first = jnp.zeros_like(places)
    for index in range(count - 1):
        first = jnp.where(places >= ends[index], ends[index], first)
    return first


def turn_halves(values, cosine, sine, turned_lanes):
    groups = []
    for first in range(0, values.shape[1], 128):
        group = values[:, first : first + 128]
        lane = lax.broadcasted_iota(jnp.int32, group.shape, 1)
        partner = jnp.where(
            lane % HEAD_SIZE < HEAD_SIZE // 2,
            pltpu.roll(group, 128 - HEAD_SIZE // 2, 1),
            pltpu.roll(group, HEAD_SIZE // 2, 1),
        )
        turned = group * cosine + partner * sine
        groups.append(jnp.where(lane + first < turned_lanes, turned, group))
    return jnp.concatenate(groups, axis=1)


def scale_rows(values):
    return lax.rsqrt(jnp.mean(values * values, axis=1, keepdims=True) + NORM_EPS)


def project_step(order_ref, gain_ref, weight_ref, cos_ref, sin_ref, *refs):
    pieces, (rows_ref, query_ref, key_ref, value_ref) = refs[:-4], refs[-4:]
    count = len(pieces) // 2
    span, width = rows_ref.shape
    token_rows = pieces[0].shape[0]
    first = pl.program_id(0) * span
    places = first + lax.broadcasted_iota(jnp.int32, (span, token_rows), 0)
    left, right = 0.0, 0.0
    for index in range(count):
        part = order_ref[:, index * token_rows : (index + 1) * token_rows]
        choose = jnp.where(part == places, 1.0, 0.0).astype(jnp.bfloat16)
        left = left + contract(choose, pieces[index][...], 1, 0)
        right = right + contract(choose, pieces[count + index][...], 1, 0)
    values = jnp.concatenate([left, right], axis=1)
    rows_ref[...] = values.astype(jnp.bfloat16)
    act = (values * scale_rows(values) * gain_ref[...]).astype(jnp.bfloat16)
    made = contract(act, weight_ref[...], 1, 0)
    share = made.shape[1] // 4
    made = turn_halves(made, cos_ref[...], sin_ref[...], 3 * share).astype(jnp.bfloat16)
    query_ref[...] = made[:, : 2 * share]
    key_ref[...] = made[:, 2 * share : 3 * share]
    value_ref[...] = made[:, 3 * share :]


def whole_block(array):
    return pl.BlockSpec(
        array.shape, lambda *_: (0,) * array.ndim, pipeline_mode=pl.Buffered(1)
    )


def row_block(width):
    return pl.BlockSpec((SPAN, width), lambda i, *_: (i, 0))


def project(order_row, gain, weight, cosine, sine, pieces):
    rows = order_row.shape[1]
    width, columns = weight.shape
    share = columns // 4
    low = jnp.bfloat16
    return pl.pallas_call(
        project_step,
        grid=(rows // SPAN,),
        in_specs=[
            whole_block(order_row),
            whole_block(gain),
            whole_block(weight),
            row_block(128),
            row_block(128),
        ]
        + [whole_block(piece) for piece in pieces],
        out_specs=[row_block(width), row_block(2 * share), row_block(share), row_block(share)],
        out_shape=[
            jax.ShapeDtypeStruct((rows, width), low),
            jax.ShapeDtypeStruct((rows, 2 * share), low),
            jax.ShapeDtypeStruct((rows, share), low),
            jax.ShapeDtypeStruct((rows, share), low),
        ],
        compiler_params=pltpu.CompilerParams(
            dimension_semantics=("arbitrary",), vmem_limit_bytes=VMEM_LIMIT
        ),
        name="project",
    )(order_row, gain, weight, cosine, sine, *pieces)


def stack_heads(values, lanes):
    lane = lax.broadcasted_iota(jnp.int32, (values.shape[0], lanes), 1)
    blocks = []
    for member in range(values.shape[1] // lanes):
        part = values[:, member * lanes : (member + 1) * lanes]
        for head in range(lanes // HEAD_SIZE):
            blocks.append(jnp.where(lane // HEAD_SIZE == head, part, jnp.zeros_like(part)))
    return jnp.concatenate(blocks, axis=0)


def unstack_heads(values, lanes, span):
    lane = lax.broadcasted_iota(jnp.int32, (span, lanes), 1)
    heads = lanes // HEAD_SIZE
    members = []
    for member in range(values.shape[0] // span // heads):
        merged = None
        for head in range(heads):
            first = (member * heads + head) * span
            part = values[first : first + span]
            merged = part if merged is None else jnp.where(lane // HEAD_SIZE == head, part, merged)
        members.append(merged)
    return jnp.concatenate(members, axis=1)


def allowed_pairs(start_ref, block, key_block, span):
    query_place = block * span + lax.broadcasted_iota(jnp.int32, (span, span), 0)
    key_place = key_block * span + lax.broadcasted_iota(jnp.int32, (span, span), 1)
    return (key_place <= query_place) & (key_place >= start_ref[...])


def mask_scores(scores, allowed):
    span = allowed.shape[0]
    heads = scores.shape[0] // span
    stacked = scores.reshape(heads, span, span)
    return jnp.where(allowed[None], stacked, MASKED).reshape(scores.shape)


def attend_step(lowest_ref, start_ref, query_ref, key_ref, value_ref, out_ref, log_ref, best, accum):
    block = pl.program_id(0)
    span = query_ref.shape[0]
    lanes = key_ref.shape[1]
    query = stack_heads(query_ref[...], lanes) * jnp.bfloat16(1.0 / math.sqrt(HEAD_SIZE))
    lowest = lowest_ref[block]

    def scores_of(key_block):
        here = pl.ds(pl.multiple_of(key_block * span, span), span)
        scores = contract(query, key_ref[here, :], 1, 1)
        return mask_scores(scores, allowed_pairs(start_ref, block, key_block, span))

    best[...] = scores_of(block)

    def look(key_block, _):
        best[...] = jnp.maximum(best[...], scores_of(key_block))
        return 0

    lax.fori_loop(lowest, block, look, 0)
    top = jnp.max(best[...], axis=1, keepdims=True)
    accum[...] = jnp.zeros_like(accum)

    def visit(key_block, _):
        here = pl.ds(pl.multiple_of(key_block * span, span), span)
        terms = jnp.exp(scores_of(key_block) - top).astype(jnp.bfloat16)
        values = value_ref[here, :]
        values = jnp.concatenate([values, jnp.ones((span, 128), jnp.bfloat16)], axis=1)
        accum[...] += contract(terms, values, 1, 0)
        return 0

    lax.fori_loop(lowest, block + 1, visit, 0)
    total = accum[:, lanes : lanes + 1]
    out_ref[...] = unstack_heads(accum[:, :lanes] / total, lanes, span).astype(jnp.bfloat16)
    logs = top + jnp.log(total)
    heads = logs.shape[0] // span
    log_ref[...] = jnp.concatenate(
        [logs[head * span : (head + 1) * span] for head in range(heads)], axis=1
    )


def attend(lowest, start, query, key, value):
    rows, columns = query.shape
    lanes = key.shape[1]
    heads = columns // HEAD_SIZE
    return pl.pallas_call(
        attend_step,
        grid_spec=pltpu.PrefetchScalarGridSpec(
            num_scalar_prefetch=1,
            grid=(rows // SPAN,),
            in_specs=[row_block(1), row_block(columns), whole_block(key), whole_block(value)],
            out_specs=[row_block(columns), row_block(heads)],
            scratch_shapes=[
                pltpu.VMEM((heads * SPAN, SPAN), jnp.float32),
                pltpu.VMEM((heads * SPAN, lanes + 128), jnp.float32),
            ],
        ),
        out_shape=[
            jax.ShapeDtypeStruct((rows, columns), jnp.bfloat16),
            jax.ShapeDtypeStruct((rows, heads), jnp.float32),
        ],
        compiler_params=pltpu.CompilerParams(
            dimension_semantics=("arbitrary",), vmem_limit_bytes=VMEM_LIMIT
        ),
        name="attend",
    )(lowest, start, query, key, value)


def attend_back_step(
    lowest_ref,
    start_ref,
    log_ref,
    query_ref,
    out_ref,
    cot_ref,
    key_ref,
    value_ref,
    query_grad_ref,
    key_grad_ref,
    value_grad_ref,
    accum,
):
    block = pl.program_id(0)
    span = query_ref.shape[0]
    lanes = key_ref.shape[1]
    scale = 1.0 / math.sqrt(HEAD_SIZE)

    @pl.when(block == 0)
    def _():
        key_grad_ref[...] = jnp.zeros_like(key_grad_ref)
        value_grad_ref[...] = jnp.zeros_like(value_grad_ref)

    query = stack_heads(query_ref[...], lanes) * jnp.bfloat16(scale)
    cot = stack_heads(cot_ref[...], lanes)
    out = stack_heads(out_ref[...], lanes)
    dots = jnp.sum(cot.astype(jnp.float32) * out.astype(jnp.float32), axis=1, keepdims=True)
    heads = log_ref.shape[1]
    logs = jnp.concatenate([log_ref[:, head : head + 1] for head in range(heads)], axis=0)
    accum[...] = jnp.zeros_like(accum)

    def visit(key_block, _):
        here = pl.ds(pl.multiple_of(key_block * span, span), span)
        keys = key_ref[here, :]
        scores = contract(query, keys, 1, 1)
        scores = mask_scores(scores, allowed_pairs(start_ref, block, key_block, span))
        probs = jnp.exp(scores - logs)
        prob_grad = contract(cot, value_ref[here, :], 1, 1)
        score_grad = (probs * (prob_grad - dots)).astype(jnp.bfloat16)
        accum[...] += contract(score_grad, keys, 1, 0)
        key_grad_ref[here, :] += contract(score_grad, query, 0, 0)
        value_grad_ref[here, :] += contract(probs.astype(jnp.bfloat16), cot, 0, 0)
        return 0

    lax.fori_loop(lowest_ref[block], block + 1, visit, 0)
    query_grad_ref[...] = unstack_heads(accum[...] * scale, lanes, span)


def attend_back(lowest, start, logs, query, out, cot, key, value):
    rows, columns = query.shape
    lanes = key.shape[1]
    heads = columns // HEAD_SIZE
    return pl.pallas_call(
        attend_back_step,
        grid_spec=pltpu.PrefetchScalarGridSpec(
            num_scalar_prefetch=1,
            grid=(rows // SPAN,),
            in_specs=[
                row_block(1),
                row_block(heads),
                row_block(columns),
                row_block(columns),
                row_block(columns),
                whole_block(key),
                whole_block(value),
            ],
            out_specs=[
                row_block(columns),
                pl.BlockSpec((rows, lanes), lambda *_: (0, 0)),
                pl.BlockSpec((rows, lanes), lambda *_: (0, 0)),
            ],
            scratch_shapes=[pltpu.VMEM((heads * SPAN, lanes), jnp.float32)],
        ),
        out_shape=[
            jax.ShapeDtypeStruct((rows, columns), jnp.float32),
            jax.ShapeDtypeStruct((rows, lanes), jnp.float32),
            jax.ShapeDtypeStruct((rows, lanes), jnp.float32),
        ],
        compiler_params=pltpu.CompilerParams(
            dimension_semantics=("arbitrary",), vmem_limit_bytes=VMEM_LIMIT
        ),
        name="attend_back",
    )(lowest, start, logs, query, out, cot, key, value)


def project_back_step(
    own_ref,
    order_ref,
    gain_ref,
    weight_ref,
    cos_ref,
    sin_ref,
    query_ref,
    key_ref,
    value_ref,
    rows_ref,
    residual_ref,
    out_ref,
    late_ref,
    act_rows,
    grad_rows,
    token_rows,
    gain_sum,
):
    phase, block = pl.program_id(0), pl.program_id(1)
    blocks = pl.num_programs(1)
    span, width = rows_ref.shape
    here = pl.ds(pl.multiple_of(block * span, span), span)

    @pl.when(phase == 0)
    def _():
        grads = jnp.concatenate([query_ref[...], key_ref[...], value_ref[...]], axis=1)
        share = grads.shape[1] // 4
        grads = turn_halves(grads, cos_ref[...], -sin_ref[...], 3 * share).astype(jnp.bfloat16)
        values = rows_ref[...].astype(jnp.float32)
        scale = scale_rows(values)
        normed = values * scale
        gain = gain_ref[...]
        act_grad = contract(grads, weight_ref[...], 1, 1)
        scaled = act_grad * gain
        token_grad = scale * (scaled - normed * jnp.mean(scaled * normed, axis=1, keepdims=True))
        per_device = residual_ref.shape[0]
        offset = block * span - own_ref[0] * per_device
        owned = (offset >= 0) & (offset < per_device)
        at = pl.ds(pl.multiple_of(jnp.where(owned, offset, 0), span), span)
        residual = jnp.where(owned, residual_ref[at, :].astype(jnp.float32), 0.0)
        token_rows[here, :] = (token_grad + residual).astype(jnp.bfloat16)
        act_rows[here, :] = (normed * gain).astype(jnp.bfloat16)
        grad_rows[here, :] = grads
        part = jnp.sum(act_grad * normed, axis=0, keepdims=True)

        @pl.when(block == 0)
        def _():
            gain_sum[...] = part

        @pl.when(block > 0)
        def _():
            gain_sum[...] += part

        @pl.when(block == blocks - 1)
        def _():
            columns = grad_rows.shape[1]
            sums = contract(act_rows[...], grad_rows[...], 0, 0)
            late_ref[:, :columns] = sums.astype(jnp.bfloat16)
            for first in range(0, width, 128):
                part = jnp.broadcast_to(gain_sum[:, first : first + 128], (128, 128))
                row = lax.broadcasted_iota(jnp.int32, (128, 128), 0)
                lane = lax.broadcasted_iota(jnp.int32, (128, 128), 1)
                column = jnp.sum(jnp.where(row == lane, part, 0.0), axis=1, keepdims=True)
                late_ref[first : first + 128, columns:] = jnp.broadcast_to(
                    column, (128, 128)
                ).astype(jnp.bfloat16)

    @pl.when(phase == 1)
    def _():
        total = token_rows.shape[0]
        places = lax.broadcasted_iota(jnp.int32, (span, total), 1)
        choose = jnp.where(order_ref[...] == places, 1.0, 0.0).astype(jnp.bfloat16)
        out_ref[...] = contract(choose, token_rows[...], 1, 0).astype(jnp.bfloat16)


def project_back(own, order_column, gain, weight, cosine, sine, query_grad, key_grad, value_grad, rows_in, residual):
    rows, width = rows_in.shape
    columns = weight.shape[1]
    share = columns // 4
    blocks = rows // SPAN
    low = jnp.bfloat16

    def early(columns):
        return pl.BlockSpec((SPAN, columns), lambda p, i, *_: (jnp.where(p == 0, i, blocks - 1), 0))

    def late(columns):
        return pl.BlockSpec((SPAN, columns), lambda p, i, *_: (jnp.where(p == 0, 0, i), 0))

    return pl.pallas_call(
        project_back_step,
        grid_spec=pltpu.PrefetchScalarGridSpec(
            num_scalar_prefetch=1,
            grid=(2, blocks),
            in_specs=[
                late(1),
                whole_block(gain),
                whole_block(weight),
                early(128),
                early(128),
                early(2 * share),
                early(share),
                early(share),
                early(width),
                whole_block(residual),
            ],
            out_specs=[
                late(width),
                pl.BlockSpec((width, columns + 128), lambda *_: (0, 0)),
            ],
            scratch_shapes=[
                pltpu.VMEM((rows, width), low),
                pltpu.VMEM((rows, columns), low),
                pltpu.VMEM((rows, width), low),
                pltpu.VMEM((1, width), jnp.float32),
            ],
        ),
        out_shape=[
            jax.ShapeDtypeStruct((rows, width), low),
            jax.ShapeDtypeStruct((width, columns + 128), low),
        ],
        compiler_params=pltpu.CompilerParams(
            dimension_semantics=("arbitrary", "arbitrary"), vmem_limit_bytes=VMEM_LIMIT
        ),
        name="project_back",
    )(own, order_column, gain, weight, cosine, sine, query_grad, key_grad, value_grad, rows_in, residual)


def body(
    tokens,
    query_weight,
    key_projection_weight,
    value_projection_weight,
    output_weight,
    router_weight,
    first_gain,
    second_gain,
    expert_gate,
    expert_up,
    expert_down,
    routes,
    dealing,
    lengths,
    cotangent,
):
    low = jnp.bfloat16
    token_rows = tokens.shape[0]
    sp_count = lax.axis_size("sp")
    sp_index = lax.axis_index("sp")
    fsdp_count = lax.axis_size("fsdp")
    fsdp_index = lax.axis_index("fsdp")
    group_rows = token_rows * sp_count
    local_experts = EXPERTS // fsdp_count
    kept_heads = KEY_VALUE_HEADS // sp_count
    ratio = QUERY_HEADS // KEY_VALUE_HEADS
    share = kept_heads * HEAD_SIZE
    shard_rows = query_weight.shape[0]
    relative = fsdp_index ^ jnp.arange(fsdp_count, dtype=jnp.int32)

    def own_columns(weight, heads):
        part = lax.dynamic_slice_in_dim(weight, sp_index * heads * HEAD_SIZE, heads * HEAD_SIZE, 1)
        return part.astype(low)

    query_part = own_columns(query_weight, kept_heads * ratio)
    query_part = query_part.reshape(shard_rows, kept_heads, ratio, HEAD_SIZE)
    query_part = jnp.swapaxes(query_part, 1, 2).reshape(shard_rows, ratio * share)
    packed = jnp.concatenate(
        [
            query_part,
            own_columns(key_projection_weight, kept_heads),
            own_columns(value_projection_weight, kept_heads),
            output_weight.astype(low),
            router_weight.astype(low),
            first_gain.astype(low)[:, None],
            second_gain.astype(low)[:, None],
            jnp.zeros((shard_rows, 128 - EXPERTS - 2), low),
        ],
        axis=1,
    )
    packed_all = lax.all_gather(packed, "fsdp", axis=0, tiled=True)
    qkv_columns = (ratio + 2) * share
    qkv_weight = packed_all[:, :qkv_columns]
    output_full = packed_all[:, qkv_columns : qkv_columns + MODEL_WIDTH]
    output_full = output_full.reshape(sp_count, kept_heads, ratio, HEAD_SIZE, MODEL_WIDTH)
    output_full = jnp.swapaxes(output_full, 1, 2).reshape(sp_count, ratio * share, MODEL_WIDTH)
    rest = packed_all[:, qkv_columns + MODEL_WIDTH :]
    router_full = rest[:, :EXPERTS]
    gain_attend = rest[:, EXPERTS].astype(jnp.float32)[None, :]
    gain_mixer = rest[:, EXPERTS + 1].astype(jnp.float32)[None, :]

    expert_range = jnp.arange(EXPERTS, dtype=jnp.int32)
    member = jnp.any(routes[:, :, None] == expert_range[None, None, :], axis=1)
    row_range = jnp.arange(token_rows, dtype=jnp.int32)
    upto = (row_range[:, None] <= row_range[None, :]).astype(low)
    rank = jnp.dot(member.T.astype(low), upto, preferred_element_type=jnp.float32)
    slots = jnp.where(member.T, rank.astype(jnp.int32) - 1, -1)

    def to_experts(by_expert):
        arrived = exchange_blocks(
            by_expert.reshape(fsdp_count, local_experts, token_rows), "fsdp"
        )
        return jnp.swapaxes(jnp.take(arrived, relative, axis=0), 0, 1)

    order_row = dealing[0]
    order_here = lax.dynamic_slice_in_dim(
        jnp.concatenate([order_row, order_row]), sp_index * token_rows, group_rows
    )
    places = jnp.arange(group_rows, dtype=jnp.int32)
    starts = sequence_starts(lengths[0], places)
    lowest = starts[::SPAN] // SPAN
    start_column = starts[:, None]
    half_dim = HEAD_SIZE // 2
    frequency = ROPE_BASE ** (-(jnp.arange(half_dim, dtype=jnp.float32) * 2.0 / HEAD_SIZE))
    angles = (places - starts).astype(jnp.float32)[:, None] * frequency[None, :]
    cosine = jnp.tile(jnp.cos(angles), (1, 4))
    sine = jnp.sin(angles)
    sine = jnp.concatenate([-sine, sine, -sine, sine], axis=1)
    slots_here = to_experts(slots)
    slots_by_row = jnp.transpose(slots_here, (1, 2, 0))
    expert_parts = [
        pack_expert(expert_gate[e].astype(low), expert_up[e].astype(low), expert_down[e].astype(low))
        for e in range(local_experts)
    ]
    stages = fsdp_count.bit_length() - 1
    ring_gates = {
        1: (cosine, sine, start_column, slots, *expert_parts),
        2: (qkv_weight, output_full, gain_attend, gain_mixer, slots_by_row, order_here),
    }
    with jax.named_scope("tokens_ring"):
        ring = ring_begin(tokens)
        for step in range(sp_count - 1):
            ring = ring_step(ring, "sp", ring_gates.get(step, ()))
            if step == 0:
                arrived_first = [part[-1] for part in ring]
    left, right = ring
    ring_end = (left[-1], right[-1])
    with jax.named_scope("cot_gather"):
        cot_lists = gather_begin(after([cotangent], *arrived_first)[0])
        cot_lists = gather_stage(cot_lists, "fsdp", 0)
    pieces = [left[-k % sp_count] for k in range(sp_count)] + right
    expert_parts = after(expert_parts, *ring_end)
    with jax.named_scope("weights_queue"):
        expert_weights = [
            lax.all_gather(part, "sp", axis=0, tiled=False) for part in expert_parts
        ]
    rows_initial, query, key, value = project(
        order_here[None, :], gain_attend, qkv_weight, cosine, sine, pieces
    )
    with jax.named_scope("cot_gather"):
        for stage in range(1, stages):
            cot_lists = gather_stage(cot_lists, "fsdp", stage)
    attended, logs = attend(lowest, start_column, query, key, value)
    attn_back = exchange_blocks(
        attended.reshape(sp_count, token_rows, ratio * share), "sp"
    )
    resid = lax.dynamic_slice_in_dim(rows_initial, sp_index * token_rows, token_rows)
    branch = jnp.einsum("stc,scd->td", attn_back, output_full, preferred_element_type=jnp.float32)
    middle = resid.astype(jnp.float32) + branch
    inv_two = lax.rsqrt(jnp.mean(middle * middle, axis=1, keepdims=True) + NORM_EPS)
    normed_two = middle * inv_two
    act_two = (normed_two * gain_mixer).astype(low)
    logits = jnp.dot(act_two, router_full, preferred_element_type=jnp.float32)
    gate_dense = jax.nn.softmax(jnp.where(member, logits, -jnp.inf), axis=-1)
    gates_here = to_experts(gate_dense.T)
    with jax.named_scope("act_gather"):
        act_lists = gather_begin(act_two)
        for stage in range(stages):
            act_lists = gather_stage(act_lists, "fsdp", stage)
    act_pieces, cot_pieces = gather_end(act_lists), gather_end(cot_lists)
    mixed_rows, back_rows, gate_grads, expert_sums = [], [], [], []
    for e in range(local_experts):
        mixed, back, gate_grad, weight_grad = run_expert(
            slots_here[e],
            gates_here[e],
            expert_weights[e],
            act_pieces,
            cot_pieces,
        )
        mixed_rows.append(mixed)
        back_rows.append(back)
        gate_grads.append(gate_grad)
        with jax.named_scope("grads_queue"):
            expert_sums.append(
                lax.psum_scatter(weight_grad, "sp", scatter_dimension=0, tiled=False)
            )
    gate_grads = jnp.stack(gate_grads, axis=1)
    gate_grad_back = exchange_blocks(jnp.take(gate_grads, relative, axis=0), "fsdp")
    with jax.named_scope("back_reduce"):
        leave = combine_rows(slots_by_row, back_rows, 1)
        leave = after(leave, gate_grad_back)
        stay = combine_rows(slots_by_row, back_rows, 0)
        for stage in range(stages):
            leave, stay = reduce_stage(leave, stay, "fsdp", stage)
            if stage == 0:
                mixed_rows = after(mixed_rows, *stay)
    grad_act_moe = jnp.concatenate(stay, axis=1)
    with jax.named_scope("mix_reduce"):
        mix_leave = combine_rows(slots_by_row, mixed_rows, 1)
        mix_stay = combine_rows(slots_by_row, mixed_rows, 0)
        mix_leave = after(mix_leave, *stay)
    upstream = cotangent.astype(jnp.float32)
    gate_grad = gate_grad_back.reshape(EXPERTS, token_rows).T
    weighted = jnp.sum(gate_dense * gate_grad, axis=1, keepdims=True)
    logit_grad = (gate_dense * (gate_grad - weighted)).astype(low)
    grad_act_two = grad_act_moe + jnp.dot(
        logit_grad, router_full.T, preferred_element_type=jnp.float32
    )
    scaled_two = grad_act_two * gain_mixer
    grad_middle = upstream + inv_two * (
        scaled_two - normed_two * jnp.mean(scaled_two * normed_two, axis=1, keepdims=True)
    )
    middle_low = grad_middle.astype(low)
    grad_attn = jnp.einsum(
        "td,scd->stc", middle_low, output_full, preferred_element_type=jnp.float32
    ).astype(low)
    grad_heads = exchange_blocks(grad_attn, "sp").reshape(group_rows, ratio * share)
    with jax.named_scope("mix_reduce"):
        mix_leave, mix_stay = reduce_stage(mix_leave, mix_stay, "fsdp", 0)
    middle_after, *_ = after([middle_low], grad_attn)
    grad_output_w = jnp.einsum(
        "stc,td->scd", attn_back, middle_after, preferred_element_type=jnp.float32
    ).astype(low)
    grad_output_w = grad_output_w.reshape(sp_count, ratio, kept_heads, HEAD_SIZE, MODEL_WIDTH)
    grad_output_w = jnp.swapaxes(grad_output_w, 1, 2).reshape(MODEL_WIDTH, MODEL_WIDTH)
    logit_grad_after, grad_act_after = after([logit_grad, grad_act_two], grad_attn)
    grad_router_w = jnp.einsum(
        "td,te->de", act_two, logit_grad_after, preferred_element_type=jnp.float32
    )
    grad_gain_two = jnp.sum(grad_act_after * normed_two, axis=0)
    early_grads = jnp.concatenate(
        [
            grad_output_w,
            grad_router_w.astype(low),
            grad_gain_two.astype(low)[:, None],
            jnp.zeros((MODEL_WIDTH, 128 - EXPERTS - 1), low),
        ],
        axis=1,
    ).reshape(fsdp_count, shard_rows, MODEL_WIDTH + 128)
    with jax.named_scope("early_fsdp"):
        early_parts = exchange_blocks(early_grads, "fsdp")
    grad_heads = after([grad_heads], *mix_leave)[0]
    with jax.named_scope("mix_reduce"):
        mix_leave, mix_stay = reduce_stage(mix_leave, mix_stay, "fsdp", 1)
    grad_query, grad_key, grad_value = attend_back(
        lowest, start_column, logs, query, attended, grad_heads, key, value
    )
    with jax.named_scope("early_fsdp"):
        early_parts = after([early_parts], grad_query)[0]
        early_sum = jnp.sum(early_parts.astype(jnp.float32), axis=0).astype(low)
    with jax.named_scope("early_sp"):
        early_parts = exchange_blocks(
            early_sum.reshape(sp_count, shard_rows // sp_count, MODEL_WIDTH + 128), "sp"
        )
    grad_query = after([grad_query], *mix_leave, early_sum, *expert_sums[:1])[0]
    with jax.named_scope("mix_reduce"):
        mix_leave, mix_stay = reduce_stage(mix_leave, mix_stay, "fsdp", 2) if stages > 2 else (
            mix_leave,
            mix_stay,
        )
    token_grads, late_grads = project_back(
        sp_index[None],
        order_here[:, None],
        gain_attend,
        qkv_weight,
        cosine,
        sine,
        grad_query,
        grad_key,
        grad_value,
        rows_initial,
        middle_low,
    )
    with jax.named_scope("tokens_back"):
        back_ring = reduce_ring_begin(
            token_grads.reshape(sp_count, token_rows, MODEL_WIDTH)
        )
        for step in range(1, sp_count):
            back_ring = reduce_ring_step(back_ring, "sp", step)
            if step == 1:
                back_first = back_ring[0]
        tokens_grad = jnp.concatenate(back_ring[0], axis=1).astype(low)
    expert_sums = after(expert_sums, *back_first)
    with jax.named_scope("late_fsdp"):
        late_parts = exchange_blocks(
            late_grads.reshape(fsdp_count, shard_rows, qkv_columns + 128), "fsdp"
        )
    with jax.named_scope("mix_reduce"):
        mix_stay = after(mix_stay, *back_first)
        for stage in range(3, stages):
            mix_leave, mix_stay = reduce_stage(mix_leave, mix_stay, "fsdp", stage)
    layer_out = (middle + jnp.concatenate(mix_stay, axis=1)).astype(low)
    with jax.named_scope("early_sp"):
        early_parts = after([early_parts], *back_first)[0]
        early_sum = jnp.sum(early_parts.astype(jnp.float32), axis=0).astype(low)
        early_all = exchange_blocks(
            jnp.broadcast_to(early_sum[None], (sp_count,) + early_sum.shape), "sp"
        )
    early_sum = early_all.reshape(shard_rows, MODEL_WIDTH + 128).astype(jnp.float32)
    with jax.named_scope("late_sp"):
        late_sum = jnp.sum(late_parts.astype(jnp.float32), axis=0).astype(low)
        late_all = exchange_blocks(
            jnp.broadcast_to(late_sum[None], (sp_count,) + late_sum.shape), "sp"
        ).astype(jnp.float32)
    query_sum = late_all[:, :, : ratio * share]
    query_sum = query_sum.reshape(sp_count, shard_rows, ratio, kept_heads, HEAD_SIZE)
    query_sum = jnp.transpose(query_sum, (1, 0, 3, 2, 4)).reshape(shard_rows, MODEL_WIDTH)
    key_sum = jnp.swapaxes(late_all[:, :, ratio * share : (ratio + 1) * share], 0, 1)
    deep = expert_gate.shape[1]

    def unpack_down(part):
        blocks = [part[:, k * deep : (k + 1) * deep] for k in range(part.shape[1] // deep)]
        return jnp.concatenate(blocks, axis=0)

    value_sum = jnp.swapaxes(late_all[:, :, (ratio + 1) * share : qkv_columns], 0, 1)
    return (
        layer_out,
        tokens_grad,
        query_sum,
        key_sum.reshape(shard_rows, KEY_VALUE_HEADS * HEAD_SIZE),
        value_sum.reshape(shard_rows, KEY_VALUE_HEADS * HEAD_SIZE),
        early_sum[:, :MODEL_WIDTH],
        early_sum[:, MODEL_WIDTH : MODEL_WIDTH + EXPERTS],
        jnp.sum(late_all[:, :, qkv_columns], axis=0),
        early_sum[:, MODEL_WIDTH + EXPERTS],
        jnp.stack([part[:deep] for part in expert_sums]).astype(jnp.float32),
        jnp.stack([part[deep : 2 * deep] for part in expert_sums]).astype(jnp.float32),
        jnp.stack([unpack_down(part[2 * deep :]) for part in expert_sums]).astype(jnp.float32),
    )


def solution(mesh):
    return jax.shard_map(
        body,
        mesh=mesh,
        in_specs=(
            P(("fsdp", "sp"), None),
            P("fsdp", None),
            P("fsdp", None),
            P("fsdp", None),
            P("fsdp", None),
            P("fsdp", None),
            P("fsdp"),
            P("fsdp"),
            P("fsdp", "sp", None),
            P("fsdp", "sp", None),
            P("fsdp", None, "sp"),
            P(("fsdp", "sp"), None),
            P("fsdp", None),
            P("fsdp", None),
            P(("fsdp", "sp"), None),
        ),
        out_specs=(
            P(("fsdp", "sp"), None),
            P(("fsdp", "sp"), None),
            P("fsdp", None),
            P("fsdp", None),
            P("fsdp", None),
            P("fsdp", None),
            P("fsdp", None),
            P("fsdp"),
            P("fsdp"),
            P("fsdp", "sp", None),
            P("fsdp", "sp", None),
            P("fsdp", None, "sp"),
        ),
        check_vma=False,
    )
```

```python
import functools
import math

import jax
import jax.numpy as jnp
from jax import lax
from jax.experimental import pallas as pl
from jax.experimental.pallas import tpu as pltpu
from jax.sharding import PartitionSpec as P

MODEL_WIDTH = 1024
QUERY_HEADS = 16
KEY_VALUE_HEADS = 8
HEAD_SIZE = 64
EXPERTS = 32
SPAN = 256
CAP = 192


NORM_EPS = 1e-06
ROPE_BASE = 10000.0
MASKED = -1e30
VMEM_LIMIT = 60 * 1024 * 1024


def contract(left, right, left_dim, right_dim):
    return lax.dot_general(
        left, right, (((left_dim,), (right_dim,)), ((), ())), preferred_element_type=jnp.float32
    )


def axis_bits(count):
    bits = [1 << place for place in range(count.bit_length() - 1)]
    return bits[::-1]


def flip(values, axis_name, bit):
    count = lax.axis_size(axis_name)
    return lax.ppermute(values, axis_name, [(place, place ^ bit) for place in range(count)])


def stage_orders(count):
    high = axis_bits(count)
    if count <= 2:
        return (high, high)
    return (high, high[1:2] + high[:1] + high[2:])


def gather_begin(values):
    half = values.shape[1] // 2
    return [{0: values[:, :half]}, {0: values[:, half:]}]


def gather_stage(lists, axis_name, stage, gates=()):
    count = lax.axis_size(axis_name)
    grown = []
    for order, pieces in zip(stage_orders(count), lists):
        keys = list(pieces)
        held = after([pieces[r] for r in keys], *gates) if gates else [pieces[r] for r in keys]
        new = dict(zip(keys, held))
        new.update({r ^ order[stage]: flip(new[r], axis_name, order[stage]) for r in keys})
        grown.append(new)
    return grown


def gather_end(lists):
    return [pieces[r] for pieces in lists for r in sorted(pieces)]


def newest(lists, stage):
    return [piece for pieces in lists for piece in list(pieces.values())[1 << stage :]]


def chunk_place(index, order):
    place = 0
    for bit in order:
        place = place * 2 + (index * 2 // bit) % 2
    return place


def reduce_stage(leave, stay, axis_name, stage, gates=()):
    count = lax.axis_size(axis_name)
    if gates:
        stay = after(stay, *gates)
    gone_next, kept_next = [], []
    for order, gone, kept in zip(stage_orders(count), leave, stay):
        arrived = flip(gone, axis_name, order[::-1][stage])
        middle = kept.shape[0] // 2
        if middle:
            total = kept[middle:].astype(jnp.float32) + arrived[middle:].astype(jnp.float32)
            gone_next.append(total.astype(jnp.bfloat16))
            total = kept[:middle].astype(jnp.float32) + arrived[:middle].astype(jnp.float32)
            kept_next.append(total.astype(jnp.bfloat16))
        else:
            kept_next.append(kept[0].astype(jnp.float32) + arrived[0].astype(jnp.float32))
    return gone_next, kept_next


def after(values, *others):
    held = lax.optimization_barrier((*values, *others))
    return list(held[: len(values)])


def shift_pairs(count, by):
    return [(place, (place + by) % count) for place in range(count)]


def exchange_blocks(values, axis_name):
    return lax.all_to_all(values, axis_name, split_axis=0, concat_axis=0, tiled=True)


def pack_expert(gate, up, down):
    rows = gate.shape[0]
    blocks = [down[k * rows : (k + 1) * rows] for k in range(down.shape[0] // rows)]
    return jnp.concatenate([gate, up, jnp.concatenate(blocks, axis=1)], axis=0)


def expert_step(own_ref, slot_ref, share_ref, weight_ref, *refs, count, first):
    acts, cots = refs[: 2 * count], refs[2 * count : 4 * count]
    mixed_ref, back_ref, share_grad_ref, weight_grad_ref = refs[4 * count : 4 * count + 4]
    act_buf, cot_buf, arrive, act_rows, hidden_rows, down_rows, gate_rows, up_rows = refs[
        4 * count + 4 :
    ]
    pair, rows = act_buf.shape[1], act_buf.shape[3]
    shards, _, packed_rows, hidden_width = weight_ref.shape
    deep = packed_rows // 3
    width = shards * deep
    tile, tiles = pl.program_id(1), pl.num_programs(1)
    step = pl.program_id(0) * tiles + tile
    steps = pl.num_programs(0) * tiles

    def copies(first, slot):
        made = []
        for source in range(pair):
            for half in range(2):
                lane = 2 * source + half
                index = half * count + first + source
                made.append(
                    pltpu.make_async_copy(
                        acts[index], act_buf.at[slot, source, half], arrive.at[slot, 0, lane]
                    )
                )
                made.append(
                    pltpu.make_async_copy(
                        cots[index], cot_buf.at[slot, source, half], arrive.at[slot, 1, lane]
                    )
                )
        return made

    def fetch(target, slot):
        for known in range(count // pair):

            @pl.when(target == known)
            def _():
                for copy in copies(known * pair, slot):
                    copy.start()

    @pl.when(step == 0)
    def _():
        fetch(0, 0)

    @pl.when(step + 1 < steps)
    def _():
        fetch((step + 1) % tiles, (step + 1) % 2)

    slot = step % 2
    for copy in copies(0, slot):
        copy.wait()

    gate_w = weight_ref[:, 0, :deep, :].reshape(width, hidden_width)
    up_w = weight_ref[:, 0, deep : 2 * deep, :].reshape(width, hidden_width)

    def down_w(shard):
        part = weight_ref[shard, 0, 2 * deep :, :]
        blocks = [part[:, k * deep : (k + 1) * deep] for k in range(hidden_width // deep)]
        return jnp.concatenate(blocks, axis=0)

    picked, cots_here, shares, masks = [], [], [], []
    expert = pl.ds(first + pl.program_id(0), 1)
    for source in range(pair):
        given = source ^ (own_ref[0] % pair)
        mask = lax.broadcasted_iota(jnp.int32, (CAP, rows), 0) == slot_ref[given, expert, :]
        choose = jnp.where(mask, 1.0, 0.0).astype(jnp.bfloat16)
        picked.append(
            jnp.concatenate(
                [contract(choose, act_buf[slot, source, half], 1, 0) for half in range(2)], axis=1
            )
        )
        cots_here.append(
            jnp.concatenate(
                [contract(choose, cot_buf[slot, source, half], 1, 0) for half in range(2)], axis=1
            )
        )
        given_share = share_ref[given, expert, :]
        shares.append(jnp.sum(jnp.where(mask, given_share, 0.0), axis=1, keepdims=True))
        masks.append(mask)
    act = jnp.concatenate(picked, 0).astype(jnp.bfloat16)
    cot = jnp.concatenate(cots_here, 0)
    share = jnp.concatenate(shares, 0)
    gate_pre = contract(act, gate_w, 1, 0)
    up_pre = contract(act, up_w, 1, 0)
    sigmoid = 1.0 / (1.0 + jnp.exp(-gate_pre))
    silu = gate_pre * sigmoid
    hidden = (silu * up_pre).astype(jnp.bfloat16)
    made = jnp.concatenate(
        [contract(hidden, down_w(shard), 1, 0) for shard in range(shards)], axis=1
    )
    made = made.astype(jnp.bfloat16).astype(jnp.float32)
    share_grad = jnp.sum(made * cot, axis=1, keepdims=True)
    mixed = (made * share).astype(jnp.bfloat16)
    made_grad = (share * cot).astype(jnp.bfloat16)
    hidden_grad = sum(
        contract(made_grad[:, shard * deep : (shard + 1) * deep], down_w(shard), 1, 1)
        for shard in range(shards)
    )
    up_grad = (hidden_grad * silu).astype(jnp.bfloat16)
    gate_grad = (
        hidden_grad * up_pre * sigmoid * (1.0 + gate_pre * (1.0 - sigmoid))
    ).astype(jnp.bfloat16)
    back = (contract(gate_grad, gate_w, 1, 1) + contract(up_grad, up_w, 1, 1)).astype(jnp.bfloat16)
    for source in range(pair):
        part = slice(source * CAP, (source + 1) * CAP)
        mixed_ref[0, source] = mixed[part]
        back_ref[0, source] = back[part]
        share_grad_ref[0, source] = jnp.sum(
            jnp.where(masks[source], share_grad[part], 0.0), axis=0, keepdims=True
        )
    here = pl.ds(pl.multiple_of(tile * pair * CAP, pair * CAP), pair * CAP)
    act_rows[here, :] = act
    hidden_rows[here, :] = hidden
    down_rows[here, :] = made_grad
    gate_rows[here, :] = gate_grad
    up_rows[here, :] = up_grad

    @pl.when(tile == tiles - 1)
    def _():
        gate_sum = contract(act_rows[...], gate_rows[...], 0, 0).astype(jnp.bfloat16)
        up_sum = contract(act_rows[...], up_rows[...], 0, 0).astype(jnp.bfloat16)
        for shard in range(shards):
            cols = slice(shard * deep, (shard + 1) * deep)
            weight_grad_ref[shard, 0, :deep, :] = gate_sum[cols]
            weight_grad_ref[shard, 0, deep : 2 * deep, :] = up_sum[cols]
            down_sum = contract(hidden_rows[...], down_rows[:, cols], 0, 0).astype(jnp.bfloat16)
            for k in range(hidden_width // deep):
                weight_grad_ref[shard, 0, 2 * deep :, k * deep : (k + 1) * deep] = down_sum[
                    k * deep : (k + 1) * deep
                ]


def run_experts(own, first, slots, shares, weights, acts, cots):
    count, known, rows = slots.shape
    half = acts[0].shape[1]
    shards, experts, packed_rows, hidden_width = weights.shape
    pair = 2
    listed = count * CAP
    low = jnp.bfloat16

    def by_source(*shape):
        return pl.BlockSpec((1, pair) + shape, lambda e, s, *_: (e, s) + (0,) * len(shape))

    given = pl.BlockSpec((pair, known, rows), lambda e, s, own: (s ^ (own[0] // pair), 0, 0))
    matrices = pl.BlockSpec((shards, 1, packed_rows, hidden_width), lambda e, s, *_: (0, e, 0, 0))
    anywhere = pl.BlockSpec(memory_space=pl.ANY)
    outs = pl.pallas_call(
        functools.partial(expert_step, count=count, first=first),
        grid_spec=pltpu.PrefetchScalarGridSpec(
            num_scalar_prefetch=1,
            grid=(experts, count // pair),
            in_specs=[given, given, matrices] + [anywhere] * (4 * count),
            out_specs=[
                by_source(CAP, 2 * half),
                by_source(CAP, 2 * half),
                by_source(1, rows),
                matrices,
            ],
            scratch_shapes=[
                pltpu.VMEM((2, pair, 2, rows, half), low),
                pltpu.VMEM((2, pair, 2, rows, half), low),
                pltpu.SemaphoreType.DMA((2, 2, 2 * pair)),
                pltpu.VMEM((listed, 2 * half), low),
                pltpu.VMEM((listed, hidden_width), low),
                pltpu.VMEM((listed, 2 * half), low),
                pltpu.VMEM((listed, hidden_width), low),
                pltpu.VMEM((listed, hidden_width), low),
            ],
        ),
        out_shape=[
            jax.ShapeDtypeStruct((experts, count, CAP, 2 * half), low),
            jax.ShapeDtypeStruct((experts, count, CAP, 2 * half), low),
            jax.ShapeDtypeStruct((experts, count, 1, rows), jnp.float32),
            jax.ShapeDtypeStruct(weights.shape, low),
        ],
        compiler_params=pltpu.CompilerParams(
            dimension_semantics=("arbitrary", "arbitrary"), vmem_limit_bytes=VMEM_LIMIT
        ),
        name="experts",
    )(own, slots, shares, weights, *acts, *cots)
    return (outs[0], outs[1], outs[2][:, :, 0], outs[3])


def combine_step(own_ref, slot_ref, *refs):
    parts, (left_ref, right_ref) = refs[:-2], refs[-2:]
    experts = sum(part.shape[0] for part in parts)
    rows, half = left_ref.shape[1:]
    place = lax.broadcasted_iota(jnp.int32, (rows, experts * CAP), 1)
    hit = None
    for expert in range(experts):
        slot = slot_ref[0, :, expert : expert + 1]
        match = place == jnp.where(slot >= 0, slot + expert * CAP, -1)
        hit = match if hit is None else hit | match
    choose = jnp.where(hit, 1.0, 0.0).astype(jnp.bfloat16)
    listed = jnp.concatenate(
        [part[:, 0].reshape(-1, 2 * half) for part in parts], axis=0
    )
    total = contract(choose, listed, 1, 0).astype(jnp.bfloat16)
    left_ref[0] = total[:, :half]
    right_ref[0] = total[:, half:]


def combine_rows(own, slots_by_row, parts, odd):
    sources, rows, experts = slots_by_row.shape
    width = parts[0].shape[3]
    orders = [order[:-1][::-1] for order in stage_orders(sources)]

    def half_of(order):
        return pl.BlockSpec((1, rows, width // 2), lambda i, *_: (chunk_place(i, order), 0, 0))

    return pl.pallas_call(
        combine_step,
        grid_spec=pltpu.PrefetchScalarGridSpec(
            num_scalar_prefetch=1,
            grid=(sources // 2,),
            in_specs=[
                pl.BlockSpec(
                    (1, rows, experts), lambda i, own: (own[0] ^ (2 * i + odd), 0, 0)
                )
            ]
            + [
                pl.BlockSpec((part.shape[0], 1, CAP, width), lambda i, *_: (0, 2 * i + odd, 0, 0))
                for part in parts
            ],
            out_specs=[half_of(order) for order in orders],
        ),
        out_shape=[jax.ShapeDtypeStruct((sources // 2, rows, width // 2), jnp.bfloat16)] * 2,
        compiler_params=pltpu.CompilerParams(
            dimension_semantics=("arbitrary",), vmem_limit_bytes=VMEM_LIMIT
        ),
        name="combine",
    )(own, slots_by_row, *parts)


def ring_begin(values):
    half = values.shape[1] // 2
    return [values[:, :half]], [values[:, half:]]


def ring_step(lists, axis_name, gates=()):
    count = lax.axis_size(axis_name)
    moving = [part[-1] for part in lists]
    if gates:
        moving = after(moving, *gates)
    return [
        part + [lax.ppermute(one, axis_name, shift_pairs(count, by))]
        for by, part, one in zip((1, -1), lists, moving)
    ]


def sequence_starts(length_row, places):
    count = length_row.shape[0]
    ends = [length_row[0]]
    for index in range(1, count):
        ends.append(ends[-1] + length_row[index])
    first = jnp.zeros_like(places)
    for index in range(count - 1):
        first = jnp.where(places >= ends[index], ends[index], first)
    return first


def turn_halves(values, cosine, sine):
    groups = []
    for first in range(0, values.shape[1], 128):
        group = values[:, first : first + 128]
        lane = lax.broadcasted_iota(jnp.int32, group.shape, 1)
        partner = jnp.where(
            lane % HEAD_SIZE < HEAD_SIZE // 2,
            pltpu.roll(group, 128 - HEAD_SIZE // 2, 1),
            pltpu.roll(group, HEAD_SIZE // 2, 1),
        )
        groups.append(group * cosine + partner * sine)
    return jnp.concatenate(groups, axis=1)


def scale_rows(values):
    return lax.rsqrt(jnp.mean(values * values, axis=1, keepdims=True) + NORM_EPS)


def block_state(bounds_ref, block, own_blocks):
    own = (block >= bounds_ref[1]) & (block < bounds_ref[1] + own_blocks)
    needed = (block >= bounds_ref[0]) & (block < bounds_ref[1] + own_blocks)
    return needed, own


def project_step(bounds_ref, order_ref, gain_ref, weight_ref, cos_ref, sin_ref, *refs, own_blocks):
    pieces, (rows_ref, query_ref, key_ref, value_ref) = refs[:-4], refs[-4:]
    count = len(pieces) // 2
    span, width = rows_ref.shape
    token_rows = pieces[0].shape[0]
    queries, keys = query_ref.shape[1], key_ref.shape[1]
    block = pl.program_id(0)
    needed, own = block_state(bounds_ref, block, own_blocks)

    @pl.when(needed)
    def _():
        places = block * span + lax.broadcasted_iota(jnp.int32, (span, token_rows), 0)
        left, right = 0.0, 0.0
        for index in range(count):
            part = order_ref[:, index * token_rows : (index + 1) * token_rows]
            choose = jnp.where(part == places, 1.0, 0.0).astype(jnp.bfloat16)
            left = left + contract(choose, pieces[index][...], 1, 0)
            right = right + contract(choose, pieces[count + index][...], 1, 0)
        values = jnp.concatenate([left, right], axis=1)
        rows_ref[...] = values.astype(jnp.bfloat16)
        act = (values * scale_rows(values) * gain_ref[...]).astype(jnp.bfloat16)
        cosine, sine = cos_ref[...], sin_ref[...]
        made = contract(act, weight_ref[:, queries : queries + keys], 1, 0)
        key_ref[...] = turn_halves(made, cosine, sine).astype(jnp.bfloat16)
        value_ref[...] = contract(act, weight_ref[:, queries + keys :], 1, 0).astype(jnp.bfloat16)

        @pl.when(own)
        def _():
            made = contract(act, weight_ref[:, :queries], 1, 0)
            query_ref[...] = turn_halves(made, cosine, sine).astype(jnp.bfloat16)


def whole_block(array):
    return pl.BlockSpec(
        array.shape, lambda *_: (0,) * array.ndim, pipeline_mode=pl.Buffered(1)
    )


def row_block(width):
    return pl.BlockSpec((SPAN, width), lambda i, *_: (i, 0))


def first_columns(rows, columns):
    return pl.BlockSpec((rows, columns), lambda *_: (0, 0), pipeline_mode=pl.Buffered(1))


def project(bounds, order_row, gain, weight, cosine, sine, pieces):
    rows = order_row.shape[1]
    width = weight.shape[0]
    token_rows = pieces[0].shape[0]
    own_blocks = token_rows // SPAN
    queries, keys = QUERY_HEADS * HEAD_SIZE, KEY_VALUE_HEADS * HEAD_SIZE
    low = jnp.bfloat16
    own_block = pl.BlockSpec(
        (SPAN, queries), lambda i, bounds: (jnp.clip(i - bounds[1], 0, own_blocks - 1), 0)
    )
    return pl.pallas_call(
        functools.partial(project_step, own_blocks=own_blocks),
        grid_spec=pltpu.PrefetchScalarGridSpec(
            num_scalar_prefetch=1,
            grid=(rows // SPAN,),
            in_specs=[
                whole_block(order_row),
                whole_block(gain),
                first_columns(width, queries + 2 * keys),
                row_block(128),
                row_block(128),
            ]
            + [whole_block(piece) for piece in pieces],
            out_specs=[row_block(width), own_block, row_block(keys), row_block(keys)],
        ),
        out_shape=[
            jax.ShapeDtypeStruct((rows, width), low),
            jax.ShapeDtypeStruct((token_rows, queries), low),
            jax.ShapeDtypeStruct((rows, keys), low),
            jax.ShapeDtypeStruct((rows, keys), low),
        ],
        compiler_params=pltpu.CompilerParams(
            dimension_semantics=("arbitrary",), vmem_limit_bytes=VMEM_LIMIT
        ),
        name="project",
    )(bounds, order_row, gain, weight, cosine, sine, *pieces)


def stack_heads(values):
    values = values.astype(jnp.float32)
    lower = lax.broadcasted_iota(jnp.int32, (values.shape[0], 128), 1) < HEAD_SIZE
    first, second = values[:, :128], values[:, 128:]
    first_turned = pltpu.roll(first, HEAD_SIZE, 1)
    second_turned = pltpu.roll(second, HEAD_SIZE, 1)
    return jnp.concatenate(
        [
            jnp.where(lower, first, 0.0),
            jnp.where(lower, first_turned, 0.0),
            jnp.where(lower, 0.0, second_turned),
            jnp.where(lower, 0.0, second),
        ],
        axis=0,
    ).astype(jnp.bfloat16)


def unstack_heads(values):
    span = values.shape[0] // 4
    parts = [values[index * span : (index + 1) * span] for index in range(4)]
    lower = lax.broadcasted_iota(jnp.int32, (span, 128), 1) < HEAD_SIZE
    first = jnp.where(lower, parts[0], pltpu.roll(parts[1], HEAD_SIZE, 1))
    second = jnp.where(lower, pltpu.roll(parts[2], HEAD_SIZE, 1), parts[3])
    return jnp.concatenate([first, second], axis=1)


def allowed_pairs(start_ref, block, key_block, span):
    query_place = block * span + lax.broadcasted_iota(jnp.int32, (span, span), 0)
    key_place = key_block * span + lax.broadcasted_iota(jnp.int32, (span, span), 1)
    return (key_place <= query_place) & (key_place >= start_ref[...])


def mask_scores(scores, allowed):
    span = allowed.shape[0]
    heads = scores.shape[0] // span
    stacked = scores.reshape(heads, span, span)
    return jnp.where(allowed[None], stacked, MASKED).reshape(scores.shape)


def attend_step(
    lowest_ref, first_ref, start_ref, query_ref, key_ref, value_ref, out_ref, log_ref, best, accum
):
    part = pl.program_id(1)
    block = first_ref[0] + part
    span = query_ref.shape[0]
    query = stack_heads(query_ref[...]) * jnp.bfloat16(1.0 / math.sqrt(HEAD_SIZE))
    lowest = lowest_ref[part]

    def scores_of(key_block):
        here = pl.ds(pl.multiple_of(key_block * span, span), span)
        scores = contract(query, key_ref[here, :], 1, 1)
        return mask_scores(scores, allowed_pairs(start_ref, block, key_block, span))

    best[...] = scores_of(block)

    def look(key_block, _):
        best[...] = jnp.maximum(best[...], scores_of(key_block))
        return 0

    lax.fori_loop(lowest, block, look, 0)
    top = jnp.max(best[...], axis=1, keepdims=True)
    accum[...] = jnp.zeros_like(accum)

    def visit(key_block, _):
        here = pl.ds(pl.multiple_of(key_block * span, span), span)
        terms = jnp.exp(scores_of(key_block) - top).astype(jnp.bfloat16)
        values = value_ref[here, :]
        values = jnp.concatenate([values, jnp.ones((span, 128), jnp.bfloat16)], axis=1)
        accum[...] += contract(terms, values, 1, 0)
        return 0

    lax.fori_loop(lowest, block + 1, visit, 0)
    total = accum[:, 128:129]
    out_ref[...] = unstack_heads(accum[:, :128] / total).astype(jnp.bfloat16)
    logs = top + jnp.log(total)
    log_ref[0] = jnp.concatenate(
        [logs[head * span : (head + 1) * span] for head in range(4)], axis=1
    )


def head_specs(rows):
    start = pl.BlockSpec((SPAN, 1), lambda j, i, *_: (i, 0))
    logs = pl.BlockSpec((1, SPAN, 4), lambda j, i, *_: (j, i, 0))
    query = pl.BlockSpec((SPAN, 256), lambda j, i, *_: (i, j))
    key = pl.BlockSpec((rows, 128), lambda j, i, *_: (0, j))
    return start, logs, query, key


def attend(lowest, first, start, query, key, value):
    rows, columns = query.shape
    pairs = key.shape[1] // 128
    start_spec, log_spec, query_spec, key_spec = head_specs(key.shape[0])
    return pl.pallas_call(
        attend_step,
        grid_spec=pltpu.PrefetchScalarGridSpec(
            num_scalar_prefetch=2,
            grid=(pairs, rows // SPAN),
            in_specs=[start_spec, query_spec, key_spec, key_spec],
            out_specs=[query_spec, log_spec],
            scratch_shapes=[
                pltpu.VMEM((4 * SPAN, SPAN), jnp.float32),
                pltpu.VMEM((4 * SPAN, 256), jnp.float32),
            ],
        ),
        out_shape=[
            jax.ShapeDtypeStruct((rows, columns), jnp.bfloat16),
            jax.ShapeDtypeStruct((pairs, rows, 4), jnp.float32),
        ],
        compiler_params=pltpu.CompilerParams(
            dimension_semantics=("arbitrary", "arbitrary"), vmem_limit_bytes=VMEM_LIMIT
        ),
        name="attend",
    )(lowest, first, start, query, key, value)


def attend_back_step(
    lowest_ref,
    first_ref,
    start_ref,
    log_ref,
    query_ref,
    out_ref,
    cot_ref,
    key_ref,
    value_ref,
    query_grad_ref,
    key_grad_ref,
    value_grad_ref,
    accum,
):
    part = pl.program_id(1)
    block = first_ref[0] + part
    span = query_ref.shape[0]
    scale = 1.0 / math.sqrt(HEAD_SIZE)

    @pl.when(part == 0)
    def _():
        key_grad_ref[...] = jnp.zeros_like(key_grad_ref)
        value_grad_ref[...] = jnp.zeros_like(value_grad_ref)

    query = stack_heads(query_ref[...]) * jnp.bfloat16(scale)
    cot = stack_heads(cot_ref[...])
    out = stack_heads(out_ref[...])
    dots = jnp.sum(cot.astype(jnp.float32) * out.astype(jnp.float32), axis=1, keepdims=True)
    logs = jnp.concatenate([log_ref[0, :, head : head + 1] for head in range(4)], axis=0)
    accum[...] = jnp.zeros_like(accum)

    def visit(key_block, _):
        here = pl.ds(pl.multiple_of(key_block * span, span), span)
        keys = key_ref[here, :]
        scores = contract(query, keys, 1, 1)
        scores = mask_scores(scores, allowed_pairs(start_ref, block, key_block, span))
        probs = jnp.exp(scores - logs)
        prob_grad = contract(cot, value_ref[here, :], 1, 1)
        score_grad = (probs * (prob_grad - dots)).astype(jnp.bfloat16)
        accum[...] += contract(score_grad, keys, 1, 0)
        key_grad_ref[here, :] += contract(score_grad, query, 0, 0)
        value_grad_ref[here, :] += contract(probs.astype(jnp.bfloat16), cot, 0, 0)
        return 0

    lax.fori_loop(lowest_ref[part], block + 1, visit, 0)
    query_grad_ref[...] = unstack_heads(accum[...] * scale)


def attend_back(lowest, first, start, logs, query, out, cot, key, value):
    rows, columns = query.shape
    pairs = key.shape[1] // 128
    start_spec, log_spec, query_spec, key_spec = head_specs(key.shape[0])
    return pl.pallas_call(
        attend_back_step,
        grid_spec=pltpu.PrefetchScalarGridSpec(
            num_scalar_prefetch=2,
            grid=(pairs, rows // SPAN),
            in_specs=[
                start_spec,
                log_spec,
                query_spec,
                query_spec,
                query_spec,
                key_spec,
                key_spec,
            ],
            out_specs=[query_spec, key_spec, key_spec],
            scratch_shapes=[pltpu.VMEM((4 * SPAN, 128), jnp.float32)],
        ),
        out_shape=[
            jax.ShapeDtypeStruct((rows, columns), jnp.float32),
            jax.ShapeDtypeStruct(key.shape, jnp.float32),
            jax.ShapeDtypeStruct(key.shape, jnp.float32),
        ],
        compiler_params=pltpu.CompilerParams(
            dimension_semantics=("arbitrary", "arbitrary"), vmem_limit_bytes=VMEM_LIMIT
        ),
        name="attend_back",
    )(lowest, first, start, logs, query, out, cot, key, value)


def weight_back_step(
    bounds_ref,
    gain_ref,
    cos_ref,
    sin_ref,
    query_ref,
    key_ref,
    value_ref,
    rows_ref,
    key_rows,
    query_rows,
    leave_left_ref,
    leave_right_ref,
    stay_left_ref,
    stay_right_ref,
    act_rows,
    left_sums,
    right_sums,
    *,
    orders,
):
    block = pl.program_id(0)
    span, width = rows_ref.shape
    own_rows, queries = query_rows.shape
    here = pl.ds(pl.multiple_of(block * span, span), span)
    needed, own = block_state(bounds_ref, block, own_rows // span)

    @pl.when(jnp.logical_not(needed))
    def _():
        act_rows[here, :] = jnp.zeros((span, width), jnp.bfloat16)
        key_rows[here, :] = jnp.zeros((span, key_rows.shape[1]), jnp.bfloat16)

    @pl.when(needed)
    def _():
        cosine, sine = cos_ref[...], -sin_ref[...]
        key_grads = turn_halves(key_ref[...], cosine, sine)
        key_rows[here, :] = jnp.concatenate([key_grads, value_ref[...]], axis=1).astype(
            jnp.bfloat16
        )
        values = rows_ref[...].astype(jnp.float32)
        act_rows[here, :] = (values * scale_rows(values) * gain_ref[...]).astype(jnp.bfloat16)

        @pl.when(own)
        def _():
            at = pl.ds(pl.multiple_of((block - bounds_ref[1]) * span, span), span)
            query_rows[at, :] = turn_halves(query_ref[...], cosine, sine).astype(jnp.bfloat16)

    @pl.when(block == pl.num_programs(0) - 1)
    def _():
        count, shard = left_sums.shape[:2]
        own_all = pl.ds(pl.multiple_of(bounds_ref[1] * span, span), own_rows)
        sums = contract(act_rows[own_all, :], query_rows[...], 0, 0).astype(jnp.bfloat16)
        left_sums[...] = sums.reshape(left_sums.shape)
        sums = contract(act_rows[...], key_rows[...], 0, 0).astype(jnp.bfloat16)
        right_sums[...] = sums.reshape(right_sums.shape)
        for index in range(count // 2):
            for odd, targets in (
                (1, (leave_left_ref, leave_right_ref)),
                (0, (stay_left_ref, stay_right_ref)),
            ):
                source = bounds_ref[2] ^ (2 * index + odd)
                for order, target, sums in zip(orders, targets, (left_sums, right_sums)):
                    target[chunk_place(index, order)] = sums[source]


def weight_back(bounds, gain, cosine, sine, query_grad, key_grad, value_grad, rows_in, shards):
    rows, width = rows_in.shape
    token_rows, queries = query_grad.shape
    keys = key_grad.shape[1]
    own_blocks = token_rows // SPAN
    shard = width // shards
    low = jnp.bfloat16
    own = pl.BlockSpec(
        (SPAN, queries), lambda i, bounds: (jnp.clip(i - bounds[1], 0, own_blocks - 1), 0)
    )
    widths = (queries, 2 * keys)
    sums = [jax.ShapeDtypeStruct((shards // 2, shard, columns), low) for columns in widths]
    made = [
        jax.ShapeDtypeStruct((rows, 2 * keys), low),
        jax.ShapeDtypeStruct((token_rows, queries), low),
    ]
    return pl.pallas_call(
        functools.partial(
            weight_back_step, orders=[order[:-1][::-1] for order in stage_orders(shards)]
        ),
        grid_spec=pltpu.PrefetchScalarGridSpec(
            num_scalar_prefetch=1,
            grid=(rows // SPAN,),
            in_specs=[
                whole_block(gain),
                row_block(128),
                row_block(128),
                own,
                row_block(keys),
                row_block(keys),
                row_block(width),
            ],
            out_specs=[whole_block(one) for one in made + sums + sums],
            scratch_shapes=[pltpu.VMEM((rows, width), low)]
            + [pltpu.VMEM((shards, shard, columns), low) for columns in widths],
        ),
        out_shape=made + sums + sums,
        compiler_params=pltpu.CompilerParams(
            dimension_semantics=("arbitrary",), vmem_limit_bytes=VMEM_LIMIT
        ),
        name="weight_back",
    )(bounds, gain, cosine, sine, query_grad, key_grad, value_grad, rows_in)


def token_back_step(
    bounds_ref,
    order_ref,
    gain_ref,
    weight_ref,
    query_ref,
    key_ref,
    rows_ref,
    residual_ref,
    out_ref,
    token_rows,
    act_grad,
):
    phase, block = pl.program_id(0), pl.program_id(1)
    span, width = rows_ref.shape
    own_rows, queries = query_ref.shape
    here = pl.ds(pl.multiple_of(block * span, span), span)
    needed, own = block_state(bounds_ref, block, own_rows // span)
    own_at = pl.ds(
        pl.multiple_of(jnp.where(own, block - bounds_ref[1], 0) * span, span), span
    )

    @pl.when((phase == 0) & jnp.logical_not(needed))
    def _():
        token_rows[here, :] = jnp.zeros((span, width), jnp.bfloat16)

    @pl.when((phase == 0) & needed)
    def _():
        act_grad[...] = contract(key_ref[...], weight_ref[:, queries:], 1, 1)

        @pl.when(own)
        def _():
            act_grad[...] += contract(query_ref[own_at, :], weight_ref[:, :queries], 1, 1)

        values = rows_ref[...].astype(jnp.float32)
        scale = scale_rows(values)
        normed = values * scale
        scaled = act_grad[...] * gain_ref[...]
        token_grad = scale * (scaled - normed * jnp.mean(scaled * normed, axis=1, keepdims=True))
        residual = jnp.where(own, residual_ref[own_at, :].astype(jnp.float32), 0.0)
        token_rows[here, :] = (token_grad + residual).astype(jnp.bfloat16)

    @pl.when(phase == 1)
    def _():
        total = token_rows.shape[0]
        places = lax.broadcasted_iota(jnp.int32, (span, total), 1)
        choose = jnp.where(order_ref[...] == places, 1.0, 0.0).astype(jnp.bfloat16)
        out_ref[...] = contract(choose, token_rows[...], 1, 0).astype(jnp.bfloat16)


def token_back(bounds, order_column, gain, weight, query_rows, key_rows, rows_in, residual):
    rows, width = rows_in.shape
    blocks = rows // SPAN
    low = jnp.bfloat16

    def early(columns):
        return pl.BlockSpec((SPAN, columns), lambda p, i, *_: (jnp.where(p == 0, i, blocks - 1), 0))

    def late(columns):
        return pl.BlockSpec((SPAN, columns), lambda p, i, *_: (jnp.where(p == 0, 0, i), 0))

    return pl.pallas_call(
        token_back_step,
        grid_spec=pltpu.PrefetchScalarGridSpec(
            num_scalar_prefetch=1,
            grid=(2, blocks),
            in_specs=[
                late(1),
                whole_block(gain),
                first_columns(width, query_rows.shape[1] + key_rows.shape[1]),
                whole_block(query_rows),
                early(key_rows.shape[1]),
                early(width),
                whole_block(residual),
            ],
            out_specs=late(width),
            scratch_shapes=[
                pltpu.VMEM((rows, width), low),
                pltpu.VMEM((SPAN, width), jnp.float32),
            ],
        ),
        out_shape=jax.ShapeDtypeStruct((rows, width), low),
        compiler_params=pltpu.CompilerParams(
            dimension_semantics=("arbitrary", "arbitrary"), vmem_limit_bytes=VMEM_LIMIT
        ),
        name="token_back",
    )(bounds, order_column, gain, weight, query_rows, key_rows, rows_in, residual)


def body(
    tokens,
    query_weight,
    key_projection_weight,
    value_projection_weight,
    output_weight,
    router_weight,
    first_gain,
    second_gain,
    expert_gate,
    expert_up,
    expert_down,
    routes,
    dealing,
    lengths,
    cotangent,
):
    low = jnp.bfloat16
    token_rows = tokens.shape[0]
    sp_count = lax.axis_size("sp")
    sp_index = lax.axis_index("sp")
    fsdp_count = lax.axis_size("fsdp")
    fsdp_index = lax.axis_index("fsdp")
    group_rows = token_rows * sp_count
    local_experts = EXPERTS // fsdp_count
    shard_rows = query_weight.shape[0]
    relative = fsdp_index ^ jnp.arange(fsdp_count, dtype=jnp.int32)
    packed = jnp.concatenate(
        [
            query_weight.astype(low),
            key_projection_weight.astype(low),
            value_projection_weight.astype(low),
            output_weight.astype(low),
            router_weight.astype(low),
            first_gain.astype(low)[:, None],
            second_gain.astype(low)[:, None],
            jnp.zeros((shard_rows, 128 - EXPERTS - 2), low),
        ],
        axis=1,
    )
    packed_all = lax.all_gather(packed, "fsdp", axis=0, tiled=True)
    query_columns = QUERY_HEADS * HEAD_SIZE
    key_columns = KEY_VALUE_HEADS * HEAD_SIZE
    qkv_columns = query_columns + 2 * key_columns
    output_full = packed_all[:, qkv_columns : qkv_columns + MODEL_WIDTH]
    rest = packed_all[:, qkv_columns + MODEL_WIDTH :]
    router_full = rest[:, :EXPERTS]
    gain_attend = rest[:, EXPERTS].astype(jnp.float32)[None, :]
    gain_mixer = rest[:, EXPERTS + 1].astype(jnp.float32)[None, :]

    expert_range = jnp.arange(EXPERTS, dtype=jnp.int32)
    member = jnp.any(routes[:, :, None] == expert_range[None, None, :], axis=1)
    row_range = jnp.arange(token_rows, dtype=jnp.int32)
    upto = (row_range[:, None] <= row_range[None, :]).astype(low)
    rank = jnp.dot(member.T.astype(low), upto, preferred_element_type=jnp.float32)
    slots = jnp.where(member.T, rank.astype(jnp.int32) - 1, -1)

    def to_experts(by_expert):
        return exchange_blocks(
            by_expert.reshape(fsdp_count, local_experts, token_rows), "fsdp"
        )

    own = fsdp_index.astype(jnp.int32)[None]
    order_row = dealing[0]
    order_here = lax.dynamic_slice_in_dim(
        jnp.concatenate([order_row, order_row]), sp_index * token_rows, group_rows
    )
    places = jnp.arange(group_rows, dtype=jnp.int32)
    starts = sequence_starts(lengths[0], places)
    own_starts = lax.dynamic_slice_in_dim(starts, sp_index * token_rows, token_rows)
    lowest = own_starts[::SPAN] // SPAN
    start_column = own_starts[:, None]
    first_block = sp_index * (token_rows // SPAN)
    bounds = jnp.stack([lowest[0], first_block, fsdp_index]).astype(jnp.int32)
    half_dim = HEAD_SIZE // 2
    frequency = ROPE_BASE ** (-(jnp.arange(half_dim, dtype=jnp.float32) * 2.0 / HEAD_SIZE))
    angles = (places - starts).astype(jnp.float32)[:, None] * frequency[None, :]
    cosine = jnp.tile(jnp.cos(angles), (1, 4))
    sine = jnp.sin(angles)
    sine = jnp.concatenate([-sine, sine, -sine, sine], axis=1)
    slots_here = to_experts(slots)
    slots_by_row = jnp.swapaxes(slots_here, 1, 2)
    merged = max(local_experts // 2, 1)
    groups = [range(first, first + merged) for first in range(0, local_experts, merged)]
    expert_parts = [
        jnp.stack(
            [
                pack_expert(
                    expert_gate[e].astype(low), expert_up[e].astype(low), expert_down[e].astype(low)
                )
                for e in members
            ]
        )
        for members in groups
    ]
    stages = fsdp_count.bit_length() - 1
    ring_gates = {
        2: (cosine, sine, start_column, slots_by_row, order_here, bounds, *expert_parts),
    }
    with jax.named_scope("tokens_ring"):
        ring = ring_begin(tokens)
        for step in range(sp_count - 1):
            ring = ring_step(ring, "sp", ring_gates.get(step, ()))
            if step == 0:
                arrived_first = [part[-1] for part in ring]
    left, right = ring
    ring_end = (left[-1], right[-1])
    with jax.named_scope("cot_gather"):
        cot_lists = gather_begin(after([cotangent], *arrived_first)[0])
        cot_lists = gather_stage(cot_lists, "fsdp", 0)
    pieces = [left[-k % sp_count] for k in range(sp_count)] + right
    expert_parts = after(expert_parts, *ring_end, packed_all)
    with jax.named_scope("weights_queue"):
        expert_weights = [
            lax.all_gather(part, "sp", axis=0, tiled=False) for part in expert_parts
        ]
    rows_initial, query, key, value = project(
        bounds, order_here[None, :], gain_attend, packed_all, cosine, sine, pieces
    )
    with jax.named_scope("cot_gather"):
        for stage in range(1, stages):
            cot_lists = gather_stage(cot_lists, "fsdp", stage)
    attended, logs = attend(lowest, first_block[None], start_column, query, key, value)
    resid = lax.dynamic_slice_in_dim(rows_initial, sp_index * token_rows, token_rows)
    branch = jnp.dot(attended, output_full, preferred_element_type=jnp.float32)
    middle = resid.astype(jnp.float32) + branch
    inv_two = lax.rsqrt(jnp.mean(middle * middle, axis=1, keepdims=True) + NORM_EPS)
    normed_two = middle * inv_two
    act_two = (normed_two * gain_mixer).astype(low)
    logits = jnp.dot(act_two, router_full, preferred_element_type=jnp.float32)
    gate_dense = jax.nn.softmax(jnp.where(member, logits, -jnp.inf), axis=-1)
    gates_here = to_experts(gate_dense.T)
    with jax.named_scope("act_gather"):
        act_lists = gather_begin(act_two)
        for stage in range(stages):
            act_lists = gather_stage(act_lists, "fsdp", stage)
    act_pieces, cot_pieces = gather_end(act_lists), gather_end(cot_lists)
    mixed_rows, back_rows, gate_grads, expert_sums = [], [], [], []
    for members, weights in zip(groups, expert_weights):
        turn = after([own], *mixed_rows[-1:])[0]
        mixed, back, gate_grad, weight_grad = run_experts(
            turn, members[0], slots_here, gates_here, weights, act_pieces, cot_pieces
        )
        mixed_rows.append(mixed)
        back_rows.append(back)
        gate_grads.append(gate_grad)
        with jax.named_scope("grads_queue"):
            expert_sums.append(
                lax.psum_scatter(weight_grad, "sp", scatter_dimension=0, tiled=False)
            )
    gate_grads = jnp.swapaxes(jnp.concatenate(gate_grads, axis=0), 0, 1)
    gate_grad_back = exchange_blocks(jnp.take(gate_grads, relative, axis=0), "fsdp")
    with jax.named_scope("back_reduce"):
        leave = combine_rows(own, slots_by_row, back_rows, 1)
        leave = after(leave, gate_grad_back)
        stay = combine_rows(own, slots_by_row, back_rows, 0)
        for stage in range(stages):
            leave, stay = reduce_stage(leave, stay, "fsdp", stage)
    grad_act_moe = jnp.concatenate(stay, axis=1)
    upstream = cotangent.astype(jnp.float32)
    gate_grad = gate_grad_back.reshape(EXPERTS, token_rows).T
    weighted = jnp.sum(gate_dense * gate_grad, axis=1, keepdims=True)
    logit_grad = (gate_dense * (gate_grad - weighted)).astype(low)
    grad_act_two = grad_act_moe + jnp.dot(
        logit_grad, router_full.T, preferred_element_type=jnp.float32
    )
    scaled_two = grad_act_two * gain_mixer
    grad_middle = upstream + inv_two * (
        scaled_two - normed_two * jnp.mean(scaled_two * normed_two, axis=1, keepdims=True)
    )
    middle_low = grad_middle.astype(low)
    grad_attn = contract(middle_low, output_full, 1, 1).astype(low)
    middle_after, *_ = after([middle_low], grad_attn)
    grad_output_w = contract(attended, middle_after, 0, 0).astype(low)
    logit_grad_after, grad_act_after = after([logit_grad, grad_act_two], grad_attn)
    grad_router_w = jnp.einsum(
        "td,te->de", act_two, logit_grad_after, preferred_element_type=jnp.float32
    )
    grad_gain_two = jnp.sum(grad_act_after * normed_two, axis=0)
    early_grads = jnp.concatenate(
        [
            grad_output_w,
            grad_router_w.astype(low),
            grad_gain_two.astype(low)[:, None],
            jnp.zeros((MODEL_WIDTH, 128 - EXPERTS - 1), low),
        ],
        axis=1,
    ).reshape(fsdp_count, shard_rows, MODEL_WIDTH + 128)
    with jax.named_scope("early_fsdp"):
        early_parts = exchange_blocks(early_grads, "fsdp")
    grad_held = after([grad_attn], expert_sums[0], early_grads)[0]
    grad_query, grad_key, grad_value = attend_back(
        lowest, first_block[None], start_column, logs, query, attended, grad_held, key, value
    )
    key_rows, query_rows, *late_parts = weight_back(
        bounds, gain_attend, cosine, sine, grad_query, grad_key, grad_value, rows_initial, fsdp_count
    )
    token_grads = token_back(
        bounds,
        order_row[:, None],
        gain_attend,
        packed_all,
        after([query_rows], *expert_sums[1:-1])[0],
        key_rows,
        rows_initial,
        middle_low,
    )
    with jax.named_scope("tokens_back"):
        tokens_grad = lax.psum_scatter(token_grads, "sp", scatter_dimension=0, tiled=True)
    with jax.named_scope("early_fsdp"):
        early_parts = after([early_parts], token_grads)[0]
        early_sum = jnp.sum(early_parts.astype(jnp.float32), axis=0).astype(low)
    with jax.named_scope("late_fsdp"):
        late_leave, late_stay = late_parts[:2], late_parts[2:]
        mix_leave, mix_stay = None, None
        for stage in range(stages):
            gates = (token_grads,) if stage == 0 else ()
            late_leave, late_stay = reduce_stage(late_leave, late_stay, "fsdp", stage, gates)
            if stage < 2:
                mixed_held = after(mixed_rows, *late_stay)
                made = combine_rows(own, slots_by_row, mixed_held, 1 - stage)
                if stage == 0:
                    mix_leave = made
                else:
                    mix_stay = made
        late_stay = after(late_stay, *mix_leave, *mix_stay)
        row_sums = jnp.concatenate([early_sum] + [part.astype(low) for part in late_stay], axis=1)
    deep = expert_gate.shape[1]

    def unpack_down(part):
        blocks = [part[:, :, k * deep : (k + 1) * deep] for k in range(part.shape[2] // deep)]
        return jnp.concatenate(blocks, axis=1)

    expert_sums = after(expert_sums, row_sums)
    expert_grads = [
        jnp.concatenate([part[:, :deep] for part in expert_sums]).astype(jnp.float32),
        jnp.concatenate([part[:, deep : 2 * deep] for part in expert_sums]).astype(jnp.float32),
        jnp.concatenate([unpack_down(part[:, 2 * deep :]) for part in expert_sums]).astype(
            jnp.float32
        ),
    ]
    with jax.named_scope("mix_reduce"):
        for stage in range(stages):
            mix_leave, mix_stay = reduce_stage(mix_leave, mix_stay, "fsdp", stage)
            if stage == 0:
                mix_leave = after(mix_leave, *expert_grads)
    layer_out = (middle + jnp.concatenate(mix_stay, axis=1)).astype(low)
    with jax.named_scope("sums_sp"):
        row_sums = exchange_blocks(
            row_sums.reshape(sp_count, shard_rows // sp_count, row_sums.shape[1]), "sp"
        )
        row_sums = jnp.sum(row_sums.astype(jnp.float32), axis=0).astype(low)
        row_sums = exchange_blocks(
            jnp.broadcast_to(row_sums[None], (sp_count,) + row_sums.shape), "sp"
        )
    row_sums = row_sums.reshape(shard_rows, -1).astype(jnp.float32)
    early_sum = row_sums[:, : MODEL_WIDTH + 128]
    late_all = row_sums[:, MODEL_WIDTH + 128 :]
    return (
        layer_out,
        tokens_grad,
        late_all[:, :query_columns],
        late_all[:, query_columns : query_columns + key_columns],
        late_all[:, query_columns + key_columns : qkv_columns],
        early_sum[:, :MODEL_WIDTH],
        early_sum[:, MODEL_WIDTH : MODEL_WIDTH + EXPERTS],
        jnp.sum(late_all * packed[:, :qkv_columns].astype(jnp.float32), axis=1)
        / first_gain.astype(low).astype(jnp.float32),
        early_sum[:, MODEL_WIDTH + EXPERTS],
        *expert_grads,
    )


def solution(mesh):
    return jax.shard_map(
        body,
        mesh=mesh,
        in_specs=(
            P(("fsdp", "sp"), None),
            P("fsdp", None),
            P("fsdp", None),
            P("fsdp", None),
            P("fsdp", None),
            P("fsdp", None),
            P("fsdp"),
            P("fsdp"),
            P("fsdp", "sp", None),
            P("fsdp", "sp", None),
            P("fsdp", None, "sp"),
            P(("fsdp", "sp"), None),
            P("fsdp", None),
            P("fsdp", None),
            P(("fsdp", "sp"), None),
        ),
        out_specs=(
            P(("fsdp", "sp"), None),
            P(("fsdp", "sp"), None),
            P("fsdp", None),
            P("fsdp", None),
            P("fsdp", None),
            P("fsdp", None),
            P("fsdp", None),
            P("fsdp"),
            P("fsdp"),
            P("fsdp", "sp", None),
            P("fsdp", "sp", None),
            P("fsdp", None, "sp"),
        ),
        check_vma=False,
    )
```

```python
import functools
import math

import jax
import jax.numpy as jnp
from jax import lax
from jax.experimental import pallas as pl
from jax.experimental.pallas import tpu as pltpu
from jax.sharding import PartitionSpec as P

MODEL_WIDTH = 1024
QUERY_HEADS = 16
KEY_VALUE_HEADS = 8
HEAD_SIZE = 64
EXPERTS = 32
SPAN = 256
CAP = 192


NORM_EPS = 1e-06
ROPE_BASE = 10000.0
MASKED = -1e30
VMEM_LIMIT = 60 * 1024 * 1024


def contract(left, right, left_dim, right_dim):
    return lax.dot_general(
        left, right, (((left_dim,), (right_dim,)), ((), ())), preferred_element_type=jnp.float32
    )


def axis_bits(count):
    bits = [1 << place for place in range(count.bit_length() - 1)]
    return bits[::-1]


def flip(values, axis_name, bit):
    count = lax.axis_size(axis_name)
    return lax.ppermute(values, axis_name, [(place, place ^ bit) for place in range(count)])


def stage_orders(count):
    high = axis_bits(count)
    if count <= 2:
        return (high, high)
    return (high, high[1:2] + high[:1] + high[2:])


def gather_begin(values):
    half = values.shape[1] // 2
    return [{0: values[:, :half]}, {0: values[:, half:]}]


def gather_stage(lists, axis_name, stage, gates=()):
    count = lax.axis_size(axis_name)
    grown = []
    for order, pieces in zip(stage_orders(count), lists):
        keys = list(pieces)
        held = after([pieces[r] for r in keys], *gates) if gates else [pieces[r] for r in keys]
        new = dict(zip(keys, held))
        new.update({r ^ order[stage]: flip(new[r], axis_name, order[stage]) for r in keys})
        grown.append(new)
    return grown


def gather_end(lists):
    return [pieces[r] for pieces in lists for r in sorted(pieces)]


def newest(lists, stage):
    return [piece for pieces in lists for piece in list(pieces.values())[1 << stage :]]


def chunk_place(index, order):
    place = 0
    for bit in order:
        place = place * 2 + (index * 2 // bit) % 2
    return place


def reduce_stage(leave, stay, axis_name, stage, gates=()):
    count = lax.axis_size(axis_name)
    if gates:
        stay = after(stay, *gates)
    gone_next, kept_next = [], []
    for order, gone, kept in zip(stage_orders(count), leave, stay):
        arrived = flip(gone, axis_name, order[::-1][stage])
        middle = kept.shape[0] // 2
        if middle:
            total = kept[middle:].astype(jnp.float32) + arrived[middle:].astype(jnp.float32)
            gone_next.append(total.astype(jnp.bfloat16))
            total = kept[:middle].astype(jnp.float32) + arrived[:middle].astype(jnp.float32)
            kept_next.append(total.astype(jnp.bfloat16))
        else:
            kept_next.append(kept[0].astype(jnp.float32) + arrived[0].astype(jnp.float32))
    return gone_next, kept_next


def after(values, *others):
    held = lax.optimization_barrier((*values, *others))
    return list(held[: len(values)])


def shift_pairs(count, by):
    return [(place, (place + by) % count) for place in range(count)]


def exchange_blocks(values, axis_name):
    return lax.all_to_all(values, axis_name, split_axis=0, concat_axis=0, tiled=True)


def pack_expert(gate, up, down):
    rows = gate.shape[0]
    blocks = [down[k * rows : (k + 1) * rows] for k in range(down.shape[0] // rows)]
    return jnp.concatenate([gate, up, jnp.concatenate(blocks, axis=1)], axis=0)


def expert_step(own_ref, slot_ref, share_ref, weight_ref, *refs, count, first):
    acts, cots = refs[: 2 * count], refs[2 * count : 4 * count]
    mixed_ref, back_ref, share_grad_ref, weight_grad_ref = refs[4 * count : 4 * count + 4]
    act_buf, cot_buf, arrive, act_rows, hidden_rows, down_rows, gate_rows, up_rows = refs[
        4 * count + 4 :
    ]
    pair, rows = act_buf.shape[1], act_buf.shape[3]
    shards, _, packed_rows, hidden_width = weight_ref.shape
    deep = packed_rows // 3
    width = shards * deep
    tile, tiles = pl.program_id(1), pl.num_programs(1)
    step = pl.program_id(0) * tiles + tile
    steps = pl.num_programs(0) * tiles

    def copies(first, slot):
        made = []
        for source in range(pair):
            for half in range(2):
                lane = 2 * source + half
                index = half * count + first + source
                made.append(
                    pltpu.make_async_copy(
                        acts[index], act_buf.at[slot, source, half], arrive.at[slot, 0, lane]
                    )
                )
                made.append(
                    pltpu.make_async_copy(
                        cots[index], cot_buf.at[slot, source, half], arrive.at[slot, 1, lane]
                    )
                )
        return made

    def fetch(target, slot):
        for known in range(count // pair):

            @pl.when(target == known)
            def _():
                for copy in copies(known * pair, slot):
                    copy.start()

    @pl.when(step == 0)
    def _():
        fetch(0, 0)

    @pl.when(step + 1 < steps)
    def _():
        fetch((step + 1) % tiles, (step + 1) % 2)

    slot = step % 2
    for copy in copies(0, slot):
        copy.wait()

    gate_w = weight_ref[:, 0, :deep, :].reshape(width, hidden_width)
    up_w = weight_ref[:, 0, deep : 2 * deep, :].reshape(width, hidden_width)

    def down_w(shard):
        part = weight_ref[shard, 0, 2 * deep :, :]
        blocks = [part[:, k * deep : (k + 1) * deep] for k in range(hidden_width // deep)]
        return jnp.concatenate(blocks, axis=0)

    picked, cots_here, shares, masks = [], [], [], []
    expert = pl.ds(first + pl.program_id(0), 1)
    for source in range(pair):
        given = source ^ (own_ref[0] % pair)
        mask = lax.broadcasted_iota(jnp.int32, (CAP, rows), 0) == slot_ref[given, expert, :]
        choose = jnp.where(mask, 1.0, 0.0).astype(jnp.bfloat16)
        picked.append(
            jnp.concatenate(
                [contract(choose, act_buf[slot, source, half], 1, 0) for half in range(2)], axis=1
            )
        )
        cots_here.append(
            jnp.concatenate(
                [contract(choose, cot_buf[slot, source, half], 1, 0) for half in range(2)], axis=1
            )
        )
        given_share = share_ref[given, expert, :]
        shares.append(jnp.sum(jnp.where(mask, given_share, 0.0), axis=1, keepdims=True))
        masks.append(mask)
    act = jnp.concatenate(picked, 0).astype(jnp.bfloat16)
    cot = jnp.concatenate(cots_here, 0)
    share = jnp.concatenate(shares, 0)
    gate_pre = contract(act, gate_w, 1, 0)
    up_pre = contract(act, up_w, 1, 0)
    sigmoid = 1.0 / (1.0 + jnp.exp(-gate_pre))
    silu = gate_pre * sigmoid
    hidden = (silu * up_pre).astype(jnp.bfloat16)
    made = jnp.concatenate(
        [contract(hidden, down_w(shard), 1, 0) for shard in range(shards)], axis=1
    )
    made = made.astype(jnp.bfloat16).astype(jnp.float32)
    share_grad = jnp.sum(made * cot, axis=1, keepdims=True)
    mixed = (made * share).astype(jnp.bfloat16)
    made_grad = (share * cot).astype(jnp.bfloat16)
    hidden_grad = sum(
        contract(made_grad[:, shard * deep : (shard + 1) * deep], down_w(shard), 1, 1)
        for shard in range(shards)
    )
    up_grad = (hidden_grad * silu).astype(jnp.bfloat16)
    gate_grad = (
        hidden_grad * up_pre * sigmoid * (1.0 + gate_pre * (1.0 - sigmoid))
    ).astype(jnp.bfloat16)
    back = (contract(gate_grad, gate_w, 1, 1) + contract(up_grad, up_w, 1, 1)).astype(jnp.bfloat16)
    for source in range(pair):
        part = slice(source * CAP, (source + 1) * CAP)
        mixed_ref[0, source] = mixed[part]
        back_ref[0, source] = back[part]
        share_grad_ref[0, source] = jnp.sum(
            jnp.where(masks[source], share_grad[part], 0.0), axis=0, keepdims=True
        )
    here = pl.ds(pl.multiple_of(tile * pair * CAP, pair * CAP), pair * CAP)
    act_rows[here, :] = act
    hidden_rows[here, :] = hidden
    down_rows[here, :] = made_grad
    gate_rows[here, :] = gate_grad
    up_rows[here, :] = up_grad

    @pl.when(tile == tiles - 1)
    def _():
        gate_sum = contract(act_rows[...], gate_rows[...], 0, 0).astype(jnp.bfloat16)
        up_sum = contract(act_rows[...], up_rows[...], 0, 0).astype(jnp.bfloat16)
        for shard in range(shards):
            cols = slice(shard * deep, (shard + 1) * deep)
            weight_grad_ref[shard, 0, :deep, :] = gate_sum[cols]
            weight_grad_ref[shard, 0, deep : 2 * deep, :] = up_sum[cols]
            down_sum = contract(hidden_rows[...], down_rows[:, cols], 0, 0).astype(jnp.bfloat16)
            for k in range(hidden_width // deep):
                weight_grad_ref[shard, 0, 2 * deep :, k * deep : (k + 1) * deep] = down_sum[
                    k * deep : (k + 1) * deep
                ]


def run_experts(own, first, slots, shares, weights, acts, cots):
    count, known, rows = slots.shape
    half = acts[0].shape[1]
    shards, experts, packed_rows, hidden_width = weights.shape
    pair = 2
    listed = count * CAP
    low = jnp.bfloat16

    def by_source(*shape):
        return pl.BlockSpec((1, pair) + shape, lambda e, s, *_: (e, s) + (0,) * len(shape))

    given = pl.BlockSpec((pair, known, rows), lambda e, s, own: (s ^ (own[0] // pair), 0, 0))
    matrices = pl.BlockSpec((shards, 1, packed_rows, hidden_width), lambda e, s, *_: (0, e, 0, 0))
    anywhere = pl.BlockSpec(memory_space=pl.ANY)
    outs = pl.pallas_call(
        functools.partial(expert_step, count=count, first=first),
        grid_spec=pltpu.PrefetchScalarGridSpec(
            num_scalar_prefetch=1,
            grid=(experts, count // pair),
            in_specs=[given, given, matrices] + [anywhere] * (4 * count),
            out_specs=[
                by_source(CAP, 2 * half),
                by_source(CAP, 2 * half),
                by_source(1, rows),
                matrices,
            ],
            scratch_shapes=[
                pltpu.VMEM((2, pair, 2, rows, half), low),
                pltpu.VMEM((2, pair, 2, rows, half), low),
                pltpu.SemaphoreType.DMA((2, 2, 2 * pair)),
                pltpu.VMEM((listed, 2 * half), low),
                pltpu.VMEM((listed, hidden_width), low),
                pltpu.VMEM((listed, 2 * half), low),
                pltpu.VMEM((listed, hidden_width), low),
                pltpu.VMEM((listed, hidden_width), low),
            ],
        ),
        out_shape=[
            jax.ShapeDtypeStruct((experts, count, CAP, 2 * half), low),
            jax.ShapeDtypeStruct((experts, count, CAP, 2 * half), low),
            jax.ShapeDtypeStruct((experts, count, 1, rows), jnp.float32),
            jax.ShapeDtypeStruct(weights.shape, low),
        ],
        compiler_params=pltpu.CompilerParams(
            dimension_semantics=("arbitrary", "arbitrary"), vmem_limit_bytes=VMEM_LIMIT
        ),
        name="experts",
    )(own, slots, shares, weights, *acts, *cots)
    return (outs[0], outs[1], outs[2][:, :, 0], outs[3])


def combine_step(own_ref, slot_ref, *refs):
    parts, (left_ref, right_ref) = refs[:-2], refs[-2:]
    experts = sum(part.shape[0] for part in parts)
    rows, half = left_ref.shape[1:]
    place = lax.broadcasted_iota(jnp.int32, (rows, experts * CAP), 1)
    hit = None
    for expert in range(experts):
        slot = slot_ref[0, :, expert : expert + 1]
        match = place == jnp.where(slot >= 0, slot + expert * CAP, -1)
        hit = match if hit is None else hit | match
    choose = jnp.where(hit, 1.0, 0.0).astype(jnp.bfloat16)
    listed = jnp.concatenate(
        [part[:, 0].reshape(-1, 2 * half) for part in parts], axis=0
    )
    total = contract(choose, listed, 1, 0).astype(jnp.bfloat16)
    left_ref[0] = total[:, :half]
    right_ref[0] = total[:, half:]


def combine_rows(own, slots_by_row, parts, odd):
    sources, rows, experts = slots_by_row.shape
    width = parts[0].shape[3]
    orders = [order[:-1][::-1] for order in stage_orders(sources)]

    def half_of(order):
        return pl.BlockSpec((1, rows, width // 2), lambda i, *_: (chunk_place(i, order), 0, 0))

    return pl.pallas_call(
        combine_step,
        grid_spec=pltpu.PrefetchScalarGridSpec(
            num_scalar_prefetch=1,
            grid=(sources // 2,),
            in_specs=[
                pl.BlockSpec(
                    (1, rows, experts), lambda i, own: (own[0] ^ (2 * i + odd), 0, 0)
                )
            ]
            + [
                pl.BlockSpec((part.shape[0], 1, CAP, width), lambda i, *_: (0, 2 * i + odd, 0, 0))
                for part in parts
            ],
            out_specs=[half_of(order) for order in orders],
        ),
        out_shape=[jax.ShapeDtypeStruct((sources // 2, rows, width // 2), jnp.bfloat16)] * 2,
        compiler_params=pltpu.CompilerParams(
            dimension_semantics=("arbitrary",), vmem_limit_bytes=VMEM_LIMIT
        ),
        name="combine",
    )(own, slots_by_row, *parts)


def ring_begin(values):
    rows, half = values.shape[0] // 2, values.shape[1] // 2
    parts = [values[:, :half], values[:, half:]]
    return [[part[first : first + rows]] for part in parts for first in (0, rows)]


def ring_step(lists, axis_name, gates=()):
    count = lax.axis_size(axis_name)
    moving = [part[-1] for part in lists]
    if gates:
        moving = after(moving, *gates)
    return [
        part + [lax.ppermute(one, axis_name, shift_pairs(count, by))]
        for by, part, one in zip((1, 1, -1, -1), lists, moving)
    ]


def sequence_starts(length_row, places):
    count = length_row.shape[0]
    ends = [length_row[0]]
    for index in range(1, count):
        ends.append(ends[-1] + length_row[index])
    first = jnp.zeros_like(places)
    for index in range(count - 1):
        first = jnp.where(places >= ends[index], ends[index], first)
    return first


def turn_halves(values, cosine, sine):
    groups = []
    for first in range(0, values.shape[1], 128):
        group = values[:, first : first + 128]
        lane = lax.broadcasted_iota(jnp.int32, group.shape, 1)
        partner = jnp.where(
            lane % HEAD_SIZE < HEAD_SIZE // 2,
            pltpu.roll(group, 128 - HEAD_SIZE // 2, 1),
            pltpu.roll(group, HEAD_SIZE // 2, 1),
        )
        groups.append(group * cosine + partner * sine)
    return jnp.concatenate(groups, axis=1)


def scale_rows(values):
    return lax.rsqrt(jnp.mean(values * values, axis=1, keepdims=True) + NORM_EPS)


def block_state(bounds_ref, block, own_blocks):
    own = (block >= bounds_ref[1]) & (block < bounds_ref[1] + own_blocks)
    needed = (block >= bounds_ref[0]) & (block < bounds_ref[1] + own_blocks)
    return needed, own


def project_step(bounds_ref, order_ref, gain_ref, weight_ref, cos_ref, sin_ref, *refs, own_blocks):
    pieces, (rows_ref, query_ref, key_ref, value_ref) = refs[:-4], refs[-4:]
    count = len(pieces) // 2
    span, width = rows_ref.shape
    token_rows = pieces[0].shape[0]
    queries, keys = query_ref.shape[1], key_ref.shape[1]
    block = pl.program_id(0)
    needed, own = block_state(bounds_ref, block, own_blocks)

    @pl.when(needed)
    def _():
        places = block * span + lax.broadcasted_iota(jnp.int32, (span, token_rows), 0)
        left, right = 0.0, 0.0
        for index in range(count):
            part = order_ref[:, index * token_rows : (index + 1) * token_rows]
            choose = jnp.where(part == places, 1.0, 0.0).astype(jnp.bfloat16)
            left = left + contract(choose, pieces[index][...], 1, 0)
            right = right + contract(choose, pieces[count + index][...], 1, 0)
        values = jnp.concatenate([left, right], axis=1)
        rows_ref[...] = values.astype(jnp.bfloat16)
        act = (values * scale_rows(values) * gain_ref[...]).astype(jnp.bfloat16)
        cosine, sine = cos_ref[...], sin_ref[...]
        made = contract(act, weight_ref[:, queries : queries + keys], 1, 0)
        key_ref[...] = turn_halves(made, cosine, sine).astype(jnp.bfloat16)
        value_ref[...] = contract(act, weight_ref[:, queries + keys :], 1, 0).astype(jnp.bfloat16)

        @pl.when(own)
        def _():
            made = contract(act, weight_ref[:, :queries], 1, 0)
            query_ref[...] = turn_halves(made, cosine, sine).astype(jnp.bfloat16)


def whole_block(array):
    return pl.BlockSpec(
        array.shape, lambda *_: (0,) * array.ndim, pipeline_mode=pl.Buffered(1)
    )


def row_block(width):
    return pl.BlockSpec((SPAN, width), lambda i, *_: (i, 0))


def first_columns(rows, columns):
    return pl.BlockSpec((rows, columns), lambda *_: (0, 0), pipeline_mode=pl.Buffered(1))


def project(bounds, order_row, gain, weight, cosine, sine, pieces, token_rows):
    rows = order_row.shape[1]
    width = weight.shape[0]
    own_blocks = token_rows // SPAN
    queries, keys = QUERY_HEADS * HEAD_SIZE, KEY_VALUE_HEADS * HEAD_SIZE
    low = jnp.bfloat16
    own_block = pl.BlockSpec(
        (SPAN, queries), lambda i, bounds: (jnp.clip(i - bounds[1], 0, own_blocks - 1), 0)
    )
    return pl.pallas_call(
        functools.partial(project_step, own_blocks=own_blocks),
        grid_spec=pltpu.PrefetchScalarGridSpec(
            num_scalar_prefetch=1,
            grid=(rows // SPAN,),
            in_specs=[
                whole_block(order_row),
                whole_block(gain),
                first_columns(width, queries + 2 * keys),
                row_block(128),
                row_block(128),
            ]
            + [whole_block(piece) for piece in pieces],
            out_specs=[row_block(width), own_block, row_block(keys), row_block(keys)],
        ),
        out_shape=[
            jax.ShapeDtypeStruct((rows, width), low),
            jax.ShapeDtypeStruct((token_rows, queries), low),
            jax.ShapeDtypeStruct((rows, keys), low),
            jax.ShapeDtypeStruct((rows, keys), low),
        ],
        compiler_params=pltpu.CompilerParams(
            dimension_semantics=("arbitrary",), vmem_limit_bytes=VMEM_LIMIT
        ),
        name="project",
    )(bounds, order_row, gain, weight, cosine, sine, *pieces)


def stack_heads(values):
    values = values.astype(jnp.float32)
    lower = lax.broadcasted_iota(jnp.int32, (values.shape[0], 128), 1) < HEAD_SIZE
    first, second = values[:, :128], values[:, 128:]
    first_turned = pltpu.roll(first, HEAD_SIZE, 1)
    second_turned = pltpu.roll(second, HEAD_SIZE, 1)
    return jnp.concatenate(
        [
            jnp.where(lower, first, 0.0),
            jnp.where(lower, first_turned, 0.0),
            jnp.where(lower, 0.0, second_turned),
            jnp.where(lower, 0.0, second),
        ],
        axis=0,
    ).astype(jnp.bfloat16)


def unstack_heads(values):
    span = values.shape[0] // 4
    parts = [values[index * span : (index + 1) * span] for index in range(4)]
    lower = lax.broadcasted_iota(jnp.int32, (span, 128), 1) < HEAD_SIZE
    first = jnp.where(lower, parts[0], pltpu.roll(parts[1], HEAD_SIZE, 1))
    second = jnp.where(lower, pltpu.roll(parts[2], HEAD_SIZE, 1), parts[3])
    return jnp.concatenate([first, second], axis=1)


def allowed_pairs(start_ref, block, key_block, span):
    query_place = block * span + lax.broadcasted_iota(jnp.int32, (span, span), 0)
    key_place = key_block * span + lax.broadcasted_iota(jnp.int32, (span, span), 1)
    return (key_place <= query_place) & (key_place >= start_ref[...])


def mask_scores(scores, allowed):
    span = allowed.shape[0]
    heads = scores.shape[0] // span
    stacked = scores.reshape(heads, span, span)
    return jnp.where(allowed[None], stacked, MASKED).reshape(scores.shape)


def attend_step(
    lowest_ref, first_ref, start_ref, query_ref, key_ref, value_ref, out_ref, log_ref, best, accum
):
    part = pl.program_id(1)
    block = first_ref[0] + part
    span = query_ref.shape[0]
    query = stack_heads(query_ref[...]) * jnp.bfloat16(1.0 / math.sqrt(HEAD_SIZE))
    lowest = lowest_ref[part]

    def scores_of(key_block):
        here = pl.ds(pl.multiple_of(key_block * span, span), span)
        scores = contract(query, key_ref[here, :], 1, 1)
        return mask_scores(scores, allowed_pairs(start_ref, block, key_block, span))

    best[...] = scores_of(block)

    def look(key_block, _):
        best[...] = jnp.maximum(best[...], scores_of(key_block))
        return 0

    lax.fori_loop(lowest, block, look, 0)
    top = jnp.max(best[...], axis=1, keepdims=True)
    accum[...] = jnp.zeros_like(accum)

    def visit(key_block, _):
        here = pl.ds(pl.multiple_of(key_block * span, span), span)
        terms = jnp.exp(scores_of(key_block) - top).astype(jnp.bfloat16)
        values = value_ref[here, :]
        values = jnp.concatenate([values, jnp.ones((span, 128), jnp.bfloat16)], axis=1)
        accum[...] += contract(terms, values, 1, 0)
        return 0

    lax.fori_loop(lowest, block + 1, visit, 0)
    total = accum[:, 128:129]
    out_ref[...] = unstack_heads(accum[:, :128] / total).astype(jnp.bfloat16)
    logs = top + jnp.log(total)
    log_ref[0] = jnp.concatenate(
        [logs[head * span : (head + 1) * span] for head in range(4)], axis=1
    )


def head_specs(rows):
    start = pl.BlockSpec((SPAN, 1), lambda j, i, *_: (i, 0))
    logs = pl.BlockSpec((1, SPAN, 4), lambda j, i, *_: (j, i, 0))
    query = pl.BlockSpec((SPAN, 256), lambda j, i, *_: (i, j))
    key = pl.BlockSpec((rows, 128), lambda j, i, *_: (0, j))
    return start, logs, query, key


def attend(lowest, first, start, query, key, value):
    rows, columns = query.shape
    pairs = key.shape[1] // 128
    start_spec, log_spec, query_spec, key_spec = head_specs(key.shape[0])
    return pl.pallas_call(
        attend_step,
        grid_spec=pltpu.PrefetchScalarGridSpec(
            num_scalar_prefetch=2,
            grid=(pairs, rows // SPAN),
            in_specs=[start_spec, query_spec, key_spec, key_spec],
            out_specs=[query_spec, log_spec],
            scratch_shapes=[
                pltpu.VMEM((4 * SPAN, SPAN), jnp.float32),
                pltpu.VMEM((4 * SPAN, 256), jnp.float32),
            ],
        ),
        out_shape=[
            jax.ShapeDtypeStruct((rows, columns), jnp.bfloat16),
            jax.ShapeDtypeStruct((pairs, rows, 4), jnp.float32),
        ],
        compiler_params=pltpu.CompilerParams(
            dimension_semantics=("arbitrary", "arbitrary"), vmem_limit_bytes=VMEM_LIMIT
        ),
        name="attend",
    )(lowest, first, start, query, key, value)


def attend_back_step(
    lowest_ref,
    first_ref,
    start_ref,
    log_ref,
    query_ref,
    out_ref,
    cot_ref,
    key_ref,
    value_ref,
    query_grad_ref,
    key_grad_ref,
    value_grad_ref,
    accum,
):
    part = pl.program_id(1)
    block = first_ref[0] + part
    span = query_ref.shape[0]
    scale = 1.0 / math.sqrt(HEAD_SIZE)

    @pl.when(part == 0)
    def _():
        key_grad_ref[...] = jnp.zeros_like(key_grad_ref)
        value_grad_ref[...] = jnp.zeros_like(value_grad_ref)

    query = stack_heads(query_ref[...]) * jnp.bfloat16(scale)
    cot = stack_heads(cot_ref[...])
    out = stack_heads(out_ref[...])
    dots = jnp.sum(cot.astype(jnp.float32) * out.astype(jnp.float32), axis=1, keepdims=True)
    logs = jnp.concatenate([log_ref[0, :, head : head + 1] for head in range(4)], axis=0)
    accum[...] = jnp.zeros_like(accum)

    def visit(key_block, _):
        here = pl.ds(pl.multiple_of(key_block * span, span), span)
        keys = key_ref[here, :]
        scores = contract(query, keys, 1, 1)
        scores = mask_scores(scores, allowed_pairs(start_ref, block, key_block, span))
        probs = jnp.exp(scores - logs)
        prob_grad = contract(cot, value_ref[here, :], 1, 1)
        score_grad = (probs * (prob_grad - dots)).astype(jnp.bfloat16)
        accum[...] += contract(score_grad, keys, 1, 0)
        key_grad_ref[here, :] += contract(score_grad, query, 0, 0)
        value_grad_ref[here, :] += contract(probs.astype(jnp.bfloat16), cot, 0, 0)
        return 0

    lax.fori_loop(lowest_ref[part], block + 1, visit, 0)
    query_grad_ref[...] = unstack_heads(accum[...] * scale)


def attend_back(lowest, first, start, logs, query, out, cot, key, value):
    rows, columns = query.shape
    pairs = key.shape[1] // 128
    start_spec, log_spec, query_spec, key_spec = head_specs(key.shape[0])
    return pl.pallas_call(
        attend_back_step,
        grid_spec=pltpu.PrefetchScalarGridSpec(
            num_scalar_prefetch=2,
            grid=(pairs, rows // SPAN),
            in_specs=[
                start_spec,
                log_spec,
                query_spec,
                query_spec,
                query_spec,
                key_spec,
                key_spec,
            ],
            out_specs=[query_spec, key_spec, key_spec],
            scratch_shapes=[pltpu.VMEM((4 * SPAN, 128), jnp.float32)],
        ),
        out_shape=[
            jax.ShapeDtypeStruct((rows, columns), jnp.float32),
            jax.ShapeDtypeStruct(key.shape, jnp.float32),
            jax.ShapeDtypeStruct(key.shape, jnp.float32),
        ],
        compiler_params=pltpu.CompilerParams(
            dimension_semantics=("arbitrary", "arbitrary"), vmem_limit_bytes=VMEM_LIMIT
        ),
        name="attend_back",
    )(lowest, first, start, logs, query, out, cot, key, value)


def weight_back_step(
    bounds_ref,
    gain_ref,
    cos_ref,
    sin_ref,
    query_ref,
    key_ref,
    value_ref,
    rows_ref,
    key_rows,
    query_rows,
    leave_left_ref,
    leave_right_ref,
    stay_left_ref,
    stay_right_ref,
    act_rows,
    left_sums,
    right_sums,
    *,
    orders,
):
    block = pl.program_id(0)
    span, width = rows_ref.shape
    own_rows, queries = query_rows.shape
    here = pl.ds(pl.multiple_of(block * span, span), span)
    needed, own = block_state(bounds_ref, block, own_rows // span)

    @pl.when(jnp.logical_not(needed))
    def _():
        act_rows[here, :] = jnp.zeros((span, width), jnp.bfloat16)
        key_rows[here, :] = jnp.zeros((span, key_rows.shape[1]), jnp.bfloat16)

    @pl.when(needed)
    def _():
        cosine, sine = cos_ref[...], -sin_ref[...]
        key_grads = turn_halves(key_ref[...], cosine, sine)
        key_rows[here, :] = jnp.concatenate([key_grads, value_ref[...]], axis=1).astype(
            jnp.bfloat16
        )
        values = rows_ref[...].astype(jnp.float32)
        act_rows[here, :] = (values * scale_rows(values) * gain_ref[...]).astype(jnp.bfloat16)

        @pl.when(own)
        def _():
            at = pl.ds(pl.multiple_of((block - bounds_ref[1]) * span, span), span)
            query_rows[at, :] = turn_halves(query_ref[...], cosine, sine).astype(jnp.bfloat16)

    @pl.when(block == pl.num_programs(0) - 1)
    def _():
        count, shard = left_sums.shape[:2]
        own_all = pl.ds(pl.multiple_of(bounds_ref[1] * span, span), own_rows)
        sums = contract(act_rows[own_all, :], query_rows[...], 0, 0).astype(jnp.bfloat16)
        left_sums[...] = sums.reshape(left_sums.shape)
        sums = contract(act_rows[...], key_rows[...], 0, 0).astype(jnp.bfloat16)
        right_sums[...] = sums.reshape(right_sums.shape)
        for index in range(count // 2):
            for odd, targets in (
                (1, (leave_left_ref, leave_right_ref)),
                (0, (stay_left_ref, stay_right_ref)),
            ):
                source = bounds_ref[2] ^ (2 * index + odd)
                for order, target, sums in zip(orders, targets, (left_sums, right_sums)):
                    target[chunk_place(index, order)] = sums[source]


def weight_back(bounds, gain, cosine, sine, query_grad, key_grad, value_grad, rows_in, shards):
    rows, width = rows_in.shape
    token_rows, queries = query_grad.shape
    keys = key_grad.shape[1]
    own_blocks = token_rows // SPAN
    shard = width // shards
    low = jnp.bfloat16
    own = pl.BlockSpec(
        (SPAN, queries), lambda i, bounds: (jnp.clip(i - bounds[1], 0, own_blocks - 1), 0)
    )
    widths = (queries, 2 * keys)
    sums = [jax.ShapeDtypeStruct((shards // 2, shard, columns), low) for columns in widths]
    made = [
        jax.ShapeDtypeStruct((rows, 2 * keys), low),
        jax.ShapeDtypeStruct((token_rows, queries), low),
    ]
    return pl.pallas_call(
        functools.partial(
            weight_back_step, orders=[order[:-1][::-1] for order in stage_orders(shards)]
        ),
        grid_spec=pltpu.PrefetchScalarGridSpec(
            num_scalar_prefetch=1,
            grid=(rows // SPAN,),
            in_specs=[
                whole_block(gain),
                row_block(128),
                row_block(128),
                own,
                row_block(keys),
                row_block(keys),
                row_block(width),
            ],
            out_specs=[whole_block(one) for one in made + sums + sums],
            scratch_shapes=[pltpu.VMEM((rows, width), low)]
            + [pltpu.VMEM((shards, shard, columns), low) for columns in widths],
        ),
        out_shape=made + sums + sums,
        compiler_params=pltpu.CompilerParams(
            dimension_semantics=("arbitrary",), vmem_limit_bytes=VMEM_LIMIT
        ),
        name="weight_back",
    )(bounds, gain, cosine, sine, query_grad, key_grad, value_grad, rows_in)


def token_back_step(
    bounds_ref,
    order_ref,
    gain_ref,
    weight_ref,
    query_ref,
    key_ref,
    rows_ref,
    residual_ref,
    out_ref,
    token_rows,
    act_grad,
):
    phase, block = pl.program_id(0), pl.program_id(1)
    span, width = rows_ref.shape
    own_rows, queries = query_ref.shape
    here = pl.ds(pl.multiple_of(block * span, span), span)
    needed, own = block_state(bounds_ref, block, own_rows // span)
    own_at = pl.ds(
        pl.multiple_of(jnp.where(own, block - bounds_ref[1], 0) * span, span), span
    )

    @pl.when((phase == 0) & jnp.logical_not(needed))
    def _():
        token_rows[here, :] = jnp.zeros((span, width), jnp.bfloat16)

    @pl.when((phase == 0) & needed)
    def _():
        act_grad[...] = contract(key_ref[...], weight_ref[:, queries:], 1, 1)

        @pl.when(own)
        def _():
            act_grad[...] += contract(query_ref[own_at, :], weight_ref[:, :queries], 1, 1)

        values = rows_ref[...].astype(jnp.float32)
        scale = scale_rows(values)
        normed = values * scale
        scaled = act_grad[...] * gain_ref[...]
        token_grad = scale * (scaled - normed * jnp.mean(scaled * normed, axis=1, keepdims=True))
        residual = jnp.where(own, residual_ref[own_at, :].astype(jnp.float32), 0.0)
        token_rows[here, :] = (token_grad + residual).astype(jnp.bfloat16)

    @pl.when(phase == 1)
    def _():
        total = token_rows.shape[0]
        places = lax.broadcasted_iota(jnp.int32, (span, total), 1)
        choose = jnp.where(order_ref[...] == places, 1.0, 0.0).astype(jnp.bfloat16)
        out_ref[...] = contract(choose, token_rows[...], 1, 0).astype(jnp.bfloat16)


def token_back(bounds, order_column, gain, weight, query_rows, key_rows, rows_in, residual):
    rows, width = rows_in.shape
    blocks = rows // SPAN
    low = jnp.bfloat16

    def early(columns):
        return pl.BlockSpec((SPAN, columns), lambda p, i, *_: (jnp.where(p == 0, i, blocks - 1), 0))

    def late(columns):
        return pl.BlockSpec((SPAN, columns), lambda p, i, *_: (jnp.where(p == 0, 0, i), 0))

    return pl.pallas_call(
        token_back_step,
        grid_spec=pltpu.PrefetchScalarGridSpec(
            num_scalar_prefetch=1,
            grid=(2, blocks),
            in_specs=[
                late(1),
                whole_block(gain),
                first_columns(width, query_rows.shape[1] + key_rows.shape[1]),
                whole_block(query_rows),
                early(key_rows.shape[1]),
                early(width),
                whole_block(residual),
            ],
            out_specs=late(width),
            scratch_shapes=[
                pltpu.VMEM((rows, width), low),
                pltpu.VMEM((SPAN, width), jnp.float32),
            ],
        ),
        out_shape=jax.ShapeDtypeStruct((rows, width), low),
        compiler_params=pltpu.CompilerParams(
            dimension_semantics=("arbitrary", "arbitrary"), vmem_limit_bytes=VMEM_LIMIT
        ),
        name="token_back",
    )(bounds, order_column, gain, weight, query_rows, key_rows, rows_in, residual)


def body(
    tokens,
    query_weight,
    key_projection_weight,
    value_projection_weight,
    output_weight,
    router_weight,
    first_gain,
    second_gain,
    expert_gate,
    expert_up,
    expert_down,
    routes,
    dealing,
    lengths,
    cotangent,
):
    low = jnp.bfloat16
    token_rows = tokens.shape[0]
    sp_count = lax.axis_size("sp")
    sp_index = lax.axis_index("sp")
    fsdp_count = lax.axis_size("fsdp")
    fsdp_index = lax.axis_index("fsdp")
    group_rows = token_rows * sp_count
    local_experts = EXPERTS // fsdp_count
    shard_rows = query_weight.shape[0]
    relative = fsdp_index ^ jnp.arange(fsdp_count, dtype=jnp.int32)
    ring = ring_begin(tokens)
    held = after(
        [query_weight, key_projection_weight, value_projection_weight, output_weight],
        *[part[0] for part in ring],
    )
    packed = jnp.concatenate(
        [
            held[0].astype(low),
            held[1].astype(low),
            held[2].astype(low),
            held[3].astype(low),
            router_weight.astype(low),
            first_gain.astype(low)[:, None],
            second_gain.astype(low)[:, None],
            jnp.zeros((shard_rows, 128 - EXPERTS - 2), low),
        ],
        axis=1,
    )
    packed_all = lax.all_gather(packed, "fsdp", axis=0, tiled=True)
    query_columns = QUERY_HEADS * HEAD_SIZE
    key_columns = KEY_VALUE_HEADS * HEAD_SIZE
    qkv_columns = query_columns + 2 * key_columns
    output_full = packed_all[:, qkv_columns : qkv_columns + MODEL_WIDTH]
    rest = packed_all[:, qkv_columns + MODEL_WIDTH :]
    router_full = rest[:, :EXPERTS]
    gain_attend = rest[:, EXPERTS].astype(jnp.float32)[None, :]
    gain_mixer = rest[:, EXPERTS + 1].astype(jnp.float32)[None, :]

    expert_range = jnp.arange(EXPERTS, dtype=jnp.int32)
    member = jnp.any(routes[:, :, None] == expert_range[None, None, :], axis=1)
    row_range = jnp.arange(token_rows, dtype=jnp.int32)
    upto = (row_range[:, None] <= row_range[None, :]).astype(low)
    rank = jnp.dot(member.T.astype(low), upto, preferred_element_type=jnp.float32)
    slots = jnp.where(member.T, rank.astype(jnp.int32) - 1, -1)

    def to_experts(by_expert):
        return exchange_blocks(
            by_expert.reshape(fsdp_count, local_experts, token_rows), "fsdp"
        )

    own = fsdp_index.astype(jnp.int32)[None]
    order_row = dealing[0]
    order_here = lax.dynamic_slice_in_dim(
        jnp.concatenate([order_row, order_row]), sp_index * token_rows, group_rows
    )
    places = jnp.arange(group_rows, dtype=jnp.int32)
    starts = sequence_starts(lengths[0], places)
    own_starts = lax.dynamic_slice_in_dim(starts, sp_index * token_rows, token_rows)
    lowest = own_starts[::SPAN] // SPAN
    start_column = own_starts[:, None]
    first_block = sp_index * (token_rows // SPAN)
    bounds = jnp.stack([lowest[0], first_block, fsdp_index]).astype(jnp.int32)
    half_dim = HEAD_SIZE // 2
    frequency = ROPE_BASE ** (-(jnp.arange(half_dim, dtype=jnp.float32) * 2.0 / HEAD_SIZE))
    angles = (places - starts).astype(jnp.float32)[:, None] * frequency[None, :]
    cosine = jnp.tile(jnp.cos(angles), (1, 4))
    sine = jnp.sin(angles)
    sine = jnp.concatenate([-sine, sine, -sine, sine], axis=1)
    merged = max(local_experts // 2, 1)
    groups = [range(first, first + merged) for first in range(0, local_experts, merged)]
    expert_parts = [
        jnp.stack(
            [
                pack_expert(
                    expert_gate[e].astype(low), expert_up[e].astype(low), expert_down[e].astype(low)
                )
                for e in members
            ]
        )
        for members in groups
    ]
    stages = fsdp_count.bit_length() - 1
    with jax.named_scope("tokens_ring"):
        ring = ring_step(ring, "sp")
    arrived_first = [part[-1] for part in ring]
    slots_here = to_experts(after([slots], *arrived_first)[0])
    slots_by_row = jnp.swapaxes(slots_here, 1, 2)
    ring_gates = {
        2: (cosine, sine, start_column, slots_by_row, order_here, bounds, *expert_parts),
    }
    with jax.named_scope("tokens_ring"):
        for step in range(1, sp_count - 1):
            ring = ring_step(ring, "sp", ring_gates.get(step, ()))
    ring_end = [part[-1] for part in ring]
    with jax.named_scope("cot_gather"):
        cot_lists = gather_begin(after([cotangent], *arrived_first)[0])
        cot_lists = gather_stage(cot_lists, "fsdp", 0)
    pieces = [part[-k % sp_count] for k in range(sp_count) for part in ring[:2]]
    pieces += [part[k] for k in range(sp_count) for part in ring[2:]]
    expert_parts = after(expert_parts, *ring_end, packed_all)
    with jax.named_scope("weights_queue"):
        expert_weights = [
            lax.all_gather(part, "sp", axis=0, tiled=False) for part in expert_parts
        ]
    rows_initial, query, key, value = project(
        bounds, order_here[None, :], gain_attend, packed_all, cosine, sine, pieces, token_rows
    )
    with jax.named_scope("cot_gather"):
        for stage in range(1, stages):
            cot_lists = gather_stage(cot_lists, "fsdp", stage)
    attended, logs = attend(lowest, first_block[None], start_column, query, key, value)
    resid = lax.dynamic_slice_in_dim(rows_initial, sp_index * token_rows, token_rows)
    branch = jnp.dot(attended, output_full, preferred_element_type=jnp.float32)
    middle = resid.astype(jnp.float32) + branch
    inv_two = lax.rsqrt(jnp.mean(middle * middle, axis=1, keepdims=True) + NORM_EPS)
    normed_two = middle * inv_two
    act_two = (normed_two * gain_mixer).astype(low)
    logits = jnp.dot(act_two, router_full, preferred_element_type=jnp.float32)
    gate_dense = jax.nn.softmax(jnp.where(member, logits, -jnp.inf), axis=-1)
    gates_here = to_experts(gate_dense.T)
    with jax.named_scope("act_gather"):
        act_lists = gather_begin(act_two)
        for stage in range(stages):
            act_lists = gather_stage(act_lists, "fsdp", stage)
    act_pieces, cot_pieces = gather_end(act_lists), gather_end(cot_lists)
    mixed_rows, back_rows, gate_grads, expert_sums = [], [], [], []
    for members, weights in zip(groups, expert_weights):
        turn = after([own], *mixed_rows[-1:])[0]
        mixed, back, gate_grad, weight_grad = run_experts(
            turn, members[0], slots_here, gates_here, weights, act_pieces, cot_pieces
        )
        mixed_rows.append(mixed)
        back_rows.append(back)
        gate_grads.append(gate_grad)
        with jax.named_scope("grads_queue"):
            expert_sums.append(
                lax.psum_scatter(weight_grad, "sp", scatter_dimension=0, tiled=False)
            )
    gate_grads = jnp.swapaxes(jnp.concatenate(gate_grads, axis=0), 0, 1)
    gate_grad_back = exchange_blocks(jnp.take(gate_grads, relative, axis=0), "fsdp")
    with jax.named_scope("back_reduce"):
        leave = combine_rows(own, slots_by_row, back_rows, 1)
        leave = after(leave, gate_grad_back)
        stay = combine_rows(own, slots_by_row, back_rows, 0)
        for stage in range(stages):
            leave, stay = reduce_stage(leave, stay, "fsdp", stage)
    grad_act_moe = jnp.concatenate(stay, axis=1)
    upstream = cotangent.astype(jnp.float32)
    gate_grad = gate_grad_back.reshape(EXPERTS, token_rows).T
    weighted = jnp.sum(gate_dense * gate_grad, axis=1, keepdims=True)
    logit_grad = (gate_dense * (gate_grad - weighted)).astype(low)
    grad_act_two = grad_act_moe + jnp.dot(
        logit_grad, router_full.T, preferred_element_type=jnp.float32
    )
    scaled_two = grad_act_two * gain_mixer
    grad_middle = upstream + inv_two * (
        scaled_two - normed_two * jnp.mean(scaled_two * normed_two, axis=1, keepdims=True)
    )
    middle_low = grad_middle.astype(low)
    grad_attn = contract(middle_low, output_full, 1, 1).astype(low)
    middle_after, *_ = after([middle_low], grad_attn)
    grad_output_w = contract(attended, middle_after, 0, 0).astype(low)
    logit_grad_after, grad_act_after = after([logit_grad, grad_act_two], grad_attn)
    grad_router_w = jnp.einsum(
        "td,te->de", act_two, logit_grad_after, preferred_element_type=jnp.float32
    )
    grad_gain_two = jnp.sum(grad_act_after * normed_two, axis=0)
    early_grads = jnp.concatenate(
        [
            grad_output_w,
            grad_router_w.astype(low),
            grad_gain_two.astype(low)[:, None],
            jnp.zeros((MODEL_WIDTH, 128 - EXPERTS - 1), low),
        ],
        axis=1,
    ).reshape(fsdp_count, shard_rows, MODEL_WIDTH + 128)
    with jax.named_scope("early_fsdp"):
        early_parts = exchange_blocks(early_grads, "fsdp")
    grad_held = after([grad_attn], expert_sums[0], early_grads)[0]
    grad_query, grad_key, grad_value = attend_back(
        lowest, first_block[None], start_column, logs, query, attended, grad_held, key, value
    )
    key_rows, query_rows, *late_parts = weight_back(
        bounds, gain_attend, cosine, sine, grad_query, grad_key, grad_value, rows_initial, fsdp_count
    )
    token_grads = token_back(
        bounds,
        order_row[:, None],
        gain_attend,
        packed_all,
        after([query_rows], *expert_sums[1:-1])[0],
        key_rows,
        rows_initial,
        middle_low,
    )
    with jax.named_scope("tokens_back"):
        tokens_grad = lax.psum_scatter(token_grads, "sp", scatter_dimension=0, tiled=True)
    with jax.named_scope("early_fsdp"):
        early_parts = after([early_parts], token_grads)[0]
        early_sum = jnp.sum(early_parts.astype(jnp.float32), axis=0).astype(low)
    with jax.named_scope("late_fsdp"):
        late_leave, late_stay = late_parts[:2], late_parts[2:]
        mix_leave, mix_stay = None, None
        for stage in range(stages):
            gates = (token_grads,) if stage == 0 else ()
            late_leave, late_stay = reduce_stage(late_leave, late_stay, "fsdp", stage, gates)
            if stage < 2:
                mixed_held = after(mixed_rows, *late_stay)
                made = combine_rows(own, slots_by_row, mixed_held, 1 - stage)
                if stage == 0:
                    mix_leave = made
                else:
                    mix_stay = made
        late_stay = after(late_stay, *mix_leave, *mix_stay)
        row_sums = jnp.concatenate([early_sum] + [part.astype(low) for part in late_stay], axis=1)
    deep = expert_gate.shape[1]

    def unpack_down(part):
        blocks = [part[:, :, k * deep : (k + 1) * deep] for k in range(part.shape[2] // deep)]
        return jnp.concatenate(blocks, axis=1)

    expert_sums = after(expert_sums, row_sums)
    expert_grads = [
        jnp.concatenate([part[:, :deep] for part in expert_sums]).astype(jnp.float32),
        jnp.concatenate([part[:, deep : 2 * deep] for part in expert_sums]).astype(jnp.float32),
        jnp.concatenate([unpack_down(part[:, 2 * deep :]) for part in expert_sums]).astype(
            jnp.float32
        ),
    ]
    with jax.named_scope("mix_reduce"):
        for stage in range(stages):
            mix_leave, mix_stay = reduce_stage(mix_leave, mix_stay, "fsdp", stage)
            if stage == 0:
                mix_leave = after(mix_leave, *expert_grads)
    layer_out = (middle + jnp.concatenate(mix_stay, axis=1)).astype(low)
    with jax.named_scope("sums_sp"):
        row_sums = exchange_blocks(
            row_sums.reshape(sp_count, shard_rows // sp_count, row_sums.shape[1]), "sp"
        )
        row_sums = jnp.sum(row_sums.astype(jnp.float32), axis=0).astype(low)
        row_sums = exchange_blocks(
            jnp.broadcast_to(row_sums[None], (sp_count,) + row_sums.shape), "sp"
        )
    row_sums = row_sums.reshape(shard_rows, -1).astype(jnp.float32)
    early_sum = row_sums[:, : MODEL_WIDTH + 128]
    late_all = row_sums[:, MODEL_WIDTH + 128 :]
    return (
        layer_out,
        tokens_grad,
        late_all[:, :query_columns],
        late_all[:, query_columns : query_columns + key_columns],
        late_all[:, query_columns + key_columns : qkv_columns],
        early_sum[:, :MODEL_WIDTH],
        early_sum[:, MODEL_WIDTH : MODEL_WIDTH + EXPERTS],
        jnp.sum(late_all * packed[:, :qkv_columns].astype(jnp.float32), axis=1)
        / first_gain.astype(low).astype(jnp.float32),
        early_sum[:, MODEL_WIDTH + EXPERTS],
        *expert_grads,
    )


def solution(mesh):
    return jax.shard_map(
        body,
        mesh=mesh,
        in_specs=(
            P(("fsdp", "sp"), None),
            P("fsdp", None),
            P("fsdp", None),
            P("fsdp", None),
            P("fsdp", None),
            P("fsdp", None),
            P("fsdp"),
            P("fsdp"),
            P("fsdp", "sp", None),
            P("fsdp", "sp", None),
            P("fsdp", None, "sp"),
            P(("fsdp", "sp"), None),
            P("fsdp", None),
            P("fsdp", None),
            P(("fsdp", "sp"), None),
        ),
        out_specs=(
            P(("fsdp", "sp"), None),
            P(("fsdp", "sp"), None),
            P("fsdp", None),
            P("fsdp", None),
            P("fsdp", None),
            P("fsdp", None),
            P("fsdp", None),
            P("fsdp"),
            P("fsdp"),
            P("fsdp", "sp", None),
            P("fsdp", "sp", None),
            P("fsdp", None, "sp"),
        ),
        check_vma=False,
    )
```

```python
import functools
import math

import jax
import jax.numpy as jnp
from jax import lax
from jax.experimental import pallas as pl
from jax.experimental.pallas import tpu as pltpu
from jax.sharding import PartitionSpec as P

MODEL_WIDTH = 1024
QUERY_HEADS = 16
KEY_VALUE_HEADS = 8
HEAD_SIZE = 64
EXPERTS = 32
SPAN = 256
CAP = 192


NORM_EPS = 1e-06
ROPE_BASE = 10000.0
MASKED = -1e30
VMEM_LIMIT = 60 * 1024 * 1024


def contract(left, right, left_dim, right_dim):
    return lax.dot_general(
        left, right, (((left_dim,), (right_dim,)), ((), ())), preferred_element_type=jnp.float32
    )


def axis_bits(count):
    bits = [1 << place for place in range(count.bit_length() - 1)]
    return bits[::-1]


def flip(values, axis_name, bit):
    count = lax.axis_size(axis_name)
    return lax.ppermute(values, axis_name, [(place, place ^ bit) for place in range(count)])


def stage_orders(count):
    high = axis_bits(count)
    if count <= 2:
        return (high, high)
    return (high, high[1:2] + high[:1] + high[2:])


def gather_begin(values):
    half = values.shape[1] // 2
    return [{0: values[:, :half]}, {0: values[:, half:]}]


def gather_stage(lists, axis_name, stage, gates=()):
    count = lax.axis_size(axis_name)
    grown = []
    for order, pieces in zip(stage_orders(count), lists):
        keys = list(pieces)
        held = after([pieces[r] for r in keys], *gates) if gates else [pieces[r] for r in keys]
        new = dict(zip(keys, held))
        new.update({r ^ order[stage]: flip(new[r], axis_name, order[stage]) for r in keys})
        grown.append(new)
    return grown


def gather_end(lists):
    return [pieces[r] for pieces in lists for r in sorted(pieces)]


def newest(lists, stage):
    return [piece for pieces in lists for piece in list(pieces.values())[1 << stage :]]


def chunk_place(index, order):
    place = 0
    for bit in order:
        place = place * 2 + (index * 2 // bit) % 2
    return place


def reduce_stage(leave, stay, axis_name, stage, gates=()):
    count = lax.axis_size(axis_name)
    if gates:
        stay = after(stay, *gates)
    gone_next, kept_next = [], []
    for order, gone, kept in zip(stage_orders(count), leave, stay):
        arrived = flip(gone, axis_name, order[::-1][stage])
        middle = kept.shape[0] // 2
        if middle:
            total = kept[middle:].astype(jnp.float32) + arrived[middle:].astype(jnp.float32)
            gone_next.append(total.astype(jnp.bfloat16))
            total = kept[:middle].astype(jnp.float32) + arrived[:middle].astype(jnp.float32)
            kept_next.append(total.astype(jnp.bfloat16))
        else:
            kept_next.append(kept[0].astype(jnp.float32) + arrived[0].astype(jnp.float32))
    return gone_next, kept_next


def after(values, *others):
    held = lax.optimization_barrier((*values, *others))
    return list(held[: len(values)])


def shift_pairs(count, by):
    return [(place, (place + by) % count) for place in range(count)]


def exchange_blocks(values, axis_name):
    return lax.all_to_all(values, axis_name, split_axis=0, concat_axis=0, tiled=True)


def pack_expert(gate, up, down):
    rows = gate.shape[0]
    blocks = [down[k * rows : (k + 1) * rows] for k in range(down.shape[0] // rows)]
    return jnp.concatenate([gate, up, jnp.concatenate(blocks, axis=1)], axis=0)


def expert_step(own_ref, slot_ref, share_ref, weight_ref, *refs, count, first):
    acts, cots = refs[: 2 * count], refs[2 * count : 4 * count]
    mixed_ref, back_ref, share_grad_ref, weight_grad_ref = refs[4 * count : 4 * count + 4]
    act_buf, cot_buf, arrive, act_rows, hidden_rows, down_rows, gate_rows, up_rows = refs[
        4 * count + 4 :
    ]
    pair, rows = act_buf.shape[1], act_buf.shape[3]
    shards, _, packed_rows, hidden_width = weight_ref.shape
    deep = packed_rows // 3
    width = shards * deep
    tile, tiles = pl.program_id(1), pl.num_programs(1)
    step = pl.program_id(0) * tiles + tile
    steps = pl.num_programs(0) * tiles

    def copies(first, slot):
        made = []
        for source in range(pair):
            for half in range(2):
                lane = 2 * source + half
                index = half * count + first + source
                made.append(
                    pltpu.make_async_copy(
                        acts[index], act_buf.at[slot, source, half], arrive.at[slot, 0, lane]
                    )
                )
                made.append(
                    pltpu.make_async_copy(
                        cots[index], cot_buf.at[slot, source, half], arrive.at[slot, 1, lane]
                    )
                )
        return made

    def fetch(target, slot):
        for known in range(count // pair):

            @pl.when(target == known)
            def _():
                for copy in copies(known * pair, slot):
                    copy.start()

    @pl.when(step == 0)
    def _():
        fetch(0, 0)

    @pl.when(step + 1 < steps)
    def _():
        fetch((step + 1) % tiles, (step + 1) % 2)

    slot = step % 2
    for copy in copies(0, slot):
        copy.wait()

    gate_w = weight_ref[:, 0, :deep, :].reshape(width, hidden_width)
    up_w = weight_ref[:, 0, deep : 2 * deep, :].reshape(width, hidden_width)

    def down_w(shard):
        part = weight_ref[shard, 0, 2 * deep :, :]
        blocks = [part[:, k * deep : (k + 1) * deep] for k in range(hidden_width // deep)]
        return jnp.concatenate(blocks, axis=0)

    picked, cots_here, shares, masks = [], [], [], []
    expert = pl.ds(first + pl.program_id(0), 1)
    for source in range(pair):
        given = source ^ (own_ref[0] % pair)
        mask = lax.broadcasted_iota(jnp.int32, (CAP, rows), 0) == slot_ref[given, expert, :]
        choose = jnp.where(mask, 1.0, 0.0).astype(jnp.bfloat16)
        picked.append(
            jnp.concatenate(
                [contract(choose, act_buf[slot, source, half], 1, 0) for half in range(2)], axis=1
            )
        )
        cots_here.append(
            jnp.concatenate(
                [contract(choose, cot_buf[slot, source, half], 1, 0) for half in range(2)], axis=1
            )
        )
        given_share = share_ref[given, expert, :]
        shares.append(jnp.sum(jnp.where(mask, given_share, 0.0), axis=1, keepdims=True))
        masks.append(mask)
    act = jnp.concatenate(picked, 0).astype(jnp.bfloat16)
    cot = jnp.concatenate(cots_here, 0)
    share = jnp.concatenate(shares, 0)
    gate_pre = contract(act, gate_w, 1, 0)
    up_pre = contract(act, up_w, 1, 0)
    sigmoid = 1.0 / (1.0 + jnp.exp(-gate_pre))
    silu = gate_pre * sigmoid
    hidden = (silu * up_pre).astype(jnp.bfloat16)
    made = jnp.concatenate(
        [contract(hidden, down_w(shard), 1, 0) for shard in range(shards)], axis=1
    )
    made = made.astype(jnp.bfloat16).astype(jnp.float32)
    share_grad = jnp.sum(made * cot, axis=1, keepdims=True)
    mixed = (made * share).astype(jnp.bfloat16)
    made_grad = (share * cot).astype(jnp.bfloat16)
    hidden_grad = sum(
        contract(made_grad[:, shard * deep : (shard + 1) * deep], down_w(shard), 1, 1)
        for shard in range(shards)
    )
    up_grad = (hidden_grad * silu).astype(jnp.bfloat16)
    gate_grad = (
        hidden_grad * up_pre * sigmoid * (1.0 + gate_pre * (1.0 - sigmoid))
    ).astype(jnp.bfloat16)
    back = (contract(gate_grad, gate_w, 1, 1) + contract(up_grad, up_w, 1, 1)).astype(jnp.bfloat16)
    for source in range(pair):
        part = slice(source * CAP, (source + 1) * CAP)
        mixed_ref[0, source] = mixed[part]
        back_ref[0, source] = back[part]
        share_grad_ref[0, source] = jnp.sum(
            jnp.where(masks[source], share_grad[part], 0.0), axis=0, keepdims=True
        )
    here = pl.ds(pl.multiple_of(tile * pair * CAP, pair * CAP), pair * CAP)
    act_rows[here, :] = act
    hidden_rows[here, :] = hidden
    down_rows[here, :] = made_grad
    gate_rows[here, :] = gate_grad
    up_rows[here, :] = up_grad

    @pl.when(tile == tiles - 1)
    def _():
        gate_sum = contract(act_rows[...], gate_rows[...], 0, 0).astype(jnp.bfloat16)
        up_sum = contract(act_rows[...], up_rows[...], 0, 0).astype(jnp.bfloat16)
        for shard in range(shards):
            cols = slice(shard * deep, (shard + 1) * deep)
            weight_grad_ref[shard, 0, :deep, :] = gate_sum[cols]
            weight_grad_ref[shard, 0, deep : 2 * deep, :] = up_sum[cols]
            down_sum = contract(hidden_rows[...], down_rows[:, cols], 0, 0).astype(jnp.bfloat16)
            for k in range(hidden_width // deep):
                weight_grad_ref[shard, 0, 2 * deep :, k * deep : (k + 1) * deep] = down_sum[
                    k * deep : (k + 1) * deep
                ]


def run_experts(own, first, slots, shares, weights, acts, cots):
    count, known, rows = slots.shape
    half = acts[0].shape[1]
    shards, experts, packed_rows, hidden_width = weights.shape
    pair = 2
    listed = count * CAP
    low = jnp.bfloat16

    def by_source(*shape):
        return pl.BlockSpec((1, pair) + shape, lambda e, s, *_: (e, s) + (0,) * len(shape))

    given = pl.BlockSpec((pair, known, rows), lambda e, s, own: (s ^ (own[0] // pair), 0, 0))
    matrices = pl.BlockSpec((shards, 1, packed_rows, hidden_width), lambda e, s, *_: (0, e, 0, 0))
    anywhere = pl.BlockSpec(memory_space=pl.ANY)
    outs = pl.pallas_call(
        functools.partial(expert_step, count=count, first=first),
        grid_spec=pltpu.PrefetchScalarGridSpec(
            num_scalar_prefetch=1,
            grid=(experts, count // pair),
            in_specs=[given, given, matrices] + [anywhere] * (4 * count),
            out_specs=[
                by_source(CAP, 2 * half),
                by_source(CAP, 2 * half),
                by_source(1, rows),
                matrices,
            ],
            scratch_shapes=[
                pltpu.VMEM((2, pair, 2, rows, half), low),
                pltpu.VMEM((2, pair, 2, rows, half), low),
                pltpu.SemaphoreType.DMA((2, 2, 2 * pair)),
                pltpu.VMEM((listed, 2 * half), low),
                pltpu.VMEM((listed, hidden_width), low),
                pltpu.VMEM((listed, 2 * half), low),
                pltpu.VMEM((listed, hidden_width), low),
                pltpu.VMEM((listed, hidden_width), low),
            ],
        ),
        out_shape=[
            jax.ShapeDtypeStruct((experts, count, CAP, 2 * half), low),
            jax.ShapeDtypeStruct((experts, count, CAP, 2 * half), low),
            jax.ShapeDtypeStruct((experts, count, 1, rows), jnp.float32),
            jax.ShapeDtypeStruct(weights.shape, low),
        ],
        compiler_params=pltpu.CompilerParams(
            dimension_semantics=("arbitrary", "arbitrary"), vmem_limit_bytes=VMEM_LIMIT
        ),
        name="experts",
    )(own, slots, shares, weights, *acts, *cots)
    return (outs[0], outs[1], outs[2][:, :, 0], outs[3])


def combine_step(own_ref, slot_ref, *refs):
    parts, (left_ref, right_ref) = refs[:-2], refs[-2:]
    experts = sum(part.shape[0] for part in parts)
    rows, half = left_ref.shape[1:]
    place = lax.broadcasted_iota(jnp.int32, (rows, experts * CAP), 1)
    hit = None
    for expert in range(experts):
        slot = slot_ref[0, :, expert : expert + 1]
        match = place == jnp.where(slot >= 0, slot + expert * CAP, -1)
        hit = match if hit is None else hit | match
    choose = jnp.where(hit, 1.0, 0.0).astype(jnp.bfloat16)
    listed = jnp.concatenate(
        [part[:, 0].reshape(-1, 2 * half) for part in parts], axis=0
    )
    total = contract(choose, listed, 1, 0).astype(jnp.bfloat16)
    left_ref[0] = total[:, :half]
    right_ref[0] = total[:, half:]


def combine_rows(own, slots_by_row, parts, odd):
    sources, rows, experts = slots_by_row.shape
    width = parts[0].shape[3]
    orders = [order[:-1][::-1] for order in stage_orders(sources)]

    def half_of(order):
        return pl.BlockSpec((1, rows, width // 2), lambda i, *_: (chunk_place(i, order), 0, 0))

    return pl.pallas_call(
        combine_step,
        grid_spec=pltpu.PrefetchScalarGridSpec(
            num_scalar_prefetch=1,
            grid=(sources // 2,),
            in_specs=[
                pl.BlockSpec(
                    (1, rows, experts), lambda i, own: (own[0] ^ (2 * i + odd), 0, 0)
                )
            ]
            + [
                pl.BlockSpec((part.shape[0], 1, CAP, width), lambda i, *_: (0, 2 * i + odd, 0, 0))
                for part in parts
            ],
            out_specs=[half_of(order) for order in orders],
        ),
        out_shape=[jax.ShapeDtypeStruct((sources // 2, rows, width // 2), jnp.bfloat16)] * 2,
        compiler_params=pltpu.CompilerParams(
            dimension_semantics=("arbitrary",), vmem_limit_bytes=VMEM_LIMIT
        ),
        name="combine",
    )(own, slots_by_row, *parts)


def ring_begin(values):
    rows, half = values.shape[0] // 2, values.shape[1] // 2
    parts = [values[:, :half], values[:, half:]]
    return [[part[first : first + rows]] for part in parts for first in (0, rows)]


def ring_step(lists, axis_name, gates=()):
    count = lax.axis_size(axis_name)
    moving = [part[-1] for part in lists]
    if gates:
        moving = after(moving, *gates)
    return [
        part + [lax.ppermute(one, axis_name, shift_pairs(count, by))]
        for by, part, one in zip((1, 1, -1, -1), lists, moving)
    ]


def sequence_starts(length_row, places):
    count = length_row.shape[0]
    ends = [length_row[0]]
    for index in range(1, count):
        ends.append(ends[-1] + length_row[index])
    first = jnp.zeros_like(places)
    for index in range(count - 1):
        first = jnp.where(places >= ends[index], ends[index], first)
    return first


def turn_halves(values, cosine, sine):
    groups = []
    for first in range(0, values.shape[1], 128):
        group = values[:, first : first + 128]
        lane = lax.broadcasted_iota(jnp.int32, group.shape, 1)
        partner = jnp.where(
            lane % HEAD_SIZE < HEAD_SIZE // 2,
            pltpu.roll(group, 128 - HEAD_SIZE // 2, 1),
            pltpu.roll(group, HEAD_SIZE // 2, 1),
        )
        groups.append(group * cosine + partner * sine)
    return jnp.concatenate(groups, axis=1)


def scale_rows(values):
    return lax.rsqrt(jnp.mean(values * values, axis=1, keepdims=True) + NORM_EPS)


def block_state(bounds_ref, block, own_blocks):
    own = (block >= bounds_ref[1]) & (block < bounds_ref[1] + own_blocks)
    needed = (block >= bounds_ref[0]) & (block < bounds_ref[1] + own_blocks)
    return needed, own


def project_step(bounds_ref, order_ref, gain_ref, weight_ref, cos_ref, sin_ref, *refs, own_blocks):
    pieces, (rows_ref, query_ref, key_ref, value_ref) = refs[:-4], refs[-4:]
    count = len(pieces) // 2
    span, width = rows_ref.shape
    token_rows = pieces[0].shape[0]
    queries, keys = query_ref.shape[1], key_ref.shape[1]
    block = pl.program_id(0)
    needed, own = block_state(bounds_ref, block, own_blocks)

    @pl.when(needed)
    def _():
        places = block * span + lax.broadcasted_iota(jnp.int32, (span, token_rows), 0)
        left, right = 0.0, 0.0
        for index in range(count):
            part = order_ref[:, index * token_rows : (index + 1) * token_rows]
            choose = jnp.where(part == places, 1.0, 0.0).astype(jnp.bfloat16)
            left = left + contract(choose, pieces[index][...], 1, 0)
            right = right + contract(choose, pieces[count + index][...], 1, 0)
        values = jnp.concatenate([left, right], axis=1)
        rows_ref[...] = values.astype(jnp.bfloat16)
        act = (values * scale_rows(values) * gain_ref[...]).astype(jnp.bfloat16)
        cosine, sine = cos_ref[...], sin_ref[...]
        made = contract(act, weight_ref[:, queries : queries + keys], 1, 0)
        key_ref[...] = turn_halves(made, cosine, sine).astype(jnp.bfloat16)
        value_ref[...] = contract(act, weight_ref[:, queries + keys :], 1, 0).astype(jnp.bfloat16)

        @pl.when(own)
        def _():
            made = contract(act, weight_ref[:, :queries], 1, 0)
            query_ref[...] = turn_halves(made, cosine, sine).astype(jnp.bfloat16)


def whole_block(array):
    return pl.BlockSpec(
        array.shape, lambda *_: (0,) * array.ndim, pipeline_mode=pl.Buffered(1)
    )


def row_block(width):
    return pl.BlockSpec((SPAN, width), lambda i, *_: (i, 0))


def first_columns(rows, columns):
    return pl.BlockSpec((rows, columns), lambda *_: (0, 0), pipeline_mode=pl.Buffered(1))


def project(bounds, order_row, gain, weight, cosine, sine, pieces, token_rows):
    rows = order_row.shape[1]
    width = weight.shape[0]
    own_blocks = token_rows // SPAN
    queries, keys = QUERY_HEADS * HEAD_SIZE, KEY_VALUE_HEADS * HEAD_SIZE
    low = jnp.bfloat16
    own_block = pl.BlockSpec(
        (SPAN, queries), lambda i, bounds: (jnp.clip(i - bounds[1], 0, own_blocks - 1), 0)
    )
    return pl.pallas_call(
        functools.partial(project_step, own_blocks=own_blocks),
        grid_spec=pltpu.PrefetchScalarGridSpec(
            num_scalar_prefetch=1,
            grid=(rows // SPAN,),
            in_specs=[
                whole_block(order_row),
                whole_block(gain),
                first_columns(width, queries + 2 * keys),
                row_block(128),
                row_block(128),
            ]
            + [whole_block(piece) for piece in pieces],
            out_specs=[row_block(width), own_block, row_block(keys), row_block(keys)],
        ),
        out_shape=[
            jax.ShapeDtypeStruct((rows, width), low),
            jax.ShapeDtypeStruct((token_rows, queries), low),
            jax.ShapeDtypeStruct((rows, keys), low),
            jax.ShapeDtypeStruct((rows, keys), low),
        ],
        compiler_params=pltpu.CompilerParams(
            dimension_semantics=("arbitrary",), vmem_limit_bytes=VMEM_LIMIT
        ),
        name="project",
    )(bounds, order_row, gain, weight, cosine, sine, *pieces)


def stack_heads(values):
    values = values.astype(jnp.float32)
    lower = lax.broadcasted_iota(jnp.int32, (values.shape[0], 128), 1) < HEAD_SIZE
    first, second = values[:, :128], values[:, 128:]
    first_turned = pltpu.roll(first, HEAD_SIZE, 1)
    second_turned = pltpu.roll(second, HEAD_SIZE, 1)
    return jnp.concatenate(
        [
            jnp.where(lower, first, 0.0),
            jnp.where(lower, first_turned, 0.0),
            jnp.where(lower, 0.0, second_turned),
            jnp.where(lower, 0.0, second),
        ],
        axis=0,
    ).astype(jnp.bfloat16)


def unstack_heads(values):
    span = values.shape[0] // 4
    parts = [values[index * span : (index + 1) * span] for index in range(4)]
    lower = lax.broadcasted_iota(jnp.int32, (span, 128), 1) < HEAD_SIZE
    first = jnp.where(lower, parts[0], pltpu.roll(parts[1], HEAD_SIZE, 1))
    second = jnp.where(lower, pltpu.roll(parts[2], HEAD_SIZE, 1), parts[3])
    return jnp.concatenate([first, second], axis=1)


def allowed_pairs(start_ref, block, key_block, span):
    query_place = block * span + lax.broadcasted_iota(jnp.int32, (span, span), 0)
    key_place = key_block * span + lax.broadcasted_iota(jnp.int32, (span, span), 1)
    return (key_place <= query_place) & (key_place >= start_ref[...])


def mask_scores(scores, allowed):
    span = allowed.shape[0]
    heads = scores.shape[0] // span
    stacked = scores.reshape(heads, span, span)
    return jnp.where(allowed[None], stacked, MASKED).reshape(scores.shape)


def attend_step(
    lowest_ref, first_ref, start_ref, query_ref, key_ref, value_ref, out_ref, log_ref, best, accum
):
    part = pl.program_id(1)
    block = first_ref[0] + part
    span = query_ref.shape[0]
    query = stack_heads(query_ref[...]) * jnp.bfloat16(1.0 / math.sqrt(HEAD_SIZE))
    lowest = lowest_ref[part]

    def scores_of(key_block):
        here = pl.ds(pl.multiple_of(key_block * span, span), span)
        scores = contract(query, key_ref[here, :], 1, 1)
        return mask_scores(scores, allowed_pairs(start_ref, block, key_block, span))

    best[...] = scores_of(block)

    def look(key_block, _):
        best[...] = jnp.maximum(best[...], scores_of(key_block))
        return 0

    lax.fori_loop(lowest, block, look, 0)
    top = jnp.max(best[...], axis=1, keepdims=True)
    accum[...] = jnp.zeros_like(accum)

    def visit(key_block, _):
        here = pl.ds(pl.multiple_of(key_block * span, span), span)
        terms = jnp.exp(scores_of(key_block) - top).astype(jnp.bfloat16)
        values = value_ref[here, :]
        values = jnp.concatenate([values, jnp.ones((span, 128), jnp.bfloat16)], axis=1)
        accum[...] += contract(terms, values, 1, 0)
        return 0

    lax.fori_loop(lowest, block + 1, visit, 0)
    total = accum[:, 128:129]
    out_ref[...] = unstack_heads(accum[:, :128] / total).astype(jnp.bfloat16)
    logs = top + jnp.log(total)
    log_ref[0] = jnp.concatenate(
        [logs[head * span : (head + 1) * span] for head in range(4)], axis=1
    )


def head_specs(rows):
    start = pl.BlockSpec((SPAN, 1), lambda j, i, *_: (i, 0))
    logs = pl.BlockSpec((1, SPAN, 4), lambda j, i, *_: (j, i, 0))
    query = pl.BlockSpec((SPAN, 256), lambda j, i, *_: (i, j))
    key = pl.BlockSpec((rows, 128), lambda j, i, *_: (0, j))
    return start, logs, query, key


def attend(lowest, first, start, query, key, value):
    rows, columns = query.shape
    pairs = key.shape[1] // 128
    start_spec, log_spec, query_spec, key_spec = head_specs(key.shape[0])
    return pl.pallas_call(
        attend_step,
        grid_spec=pltpu.PrefetchScalarGridSpec(
            num_scalar_prefetch=2,
            grid=(pairs, rows // SPAN),
            in_specs=[start_spec, query_spec, key_spec, key_spec],
            out_specs=[query_spec, log_spec],
            scratch_shapes=[
                pltpu.VMEM((4 * SPAN, SPAN), jnp.float32),
                pltpu.VMEM((4 * SPAN, 256), jnp.float32),
            ],
        ),
        out_shape=[
            jax.ShapeDtypeStruct((rows, columns), jnp.bfloat16),
            jax.ShapeDtypeStruct((pairs, rows, 4), jnp.float32),
        ],
        compiler_params=pltpu.CompilerParams(
            dimension_semantics=("arbitrary", "arbitrary"), vmem_limit_bytes=VMEM_LIMIT
        ),
        name="attend",
    )(lowest, first, start, query, key, value)


def attend_back_step(
    lowest_ref,
    first_ref,
    start_ref,
    log_ref,
    query_ref,
    out_ref,
    cot_ref,
    key_ref,
    value_ref,
    query_grad_ref,
    key_grad_ref,
    value_grad_ref,
    accum,
):
    part = pl.program_id(1)
    block = first_ref[0] + part
    span = query_ref.shape[0]
    scale = 1.0 / math.sqrt(HEAD_SIZE)

    @pl.when(part == 0)
    def _():
        key_grad_ref[...] = jnp.zeros_like(key_grad_ref)
        value_grad_ref[...] = jnp.zeros_like(value_grad_ref)

    query = stack_heads(query_ref[...]) * jnp.bfloat16(scale)
    cot = stack_heads(cot_ref[...])
    out = stack_heads(out_ref[...])
    dots = jnp.sum(cot.astype(jnp.float32) * out.astype(jnp.float32), axis=1, keepdims=True)
    logs = jnp.concatenate([log_ref[0, :, head : head + 1] for head in range(4)], axis=0)
    accum[...] = jnp.zeros_like(accum)

    def visit(key_block, _):
        here = pl.ds(pl.multiple_of(key_block * span, span), span)
        keys = key_ref[here, :]
        scores = contract(query, keys, 1, 1)
        scores = mask_scores(scores, allowed_pairs(start_ref, block, key_block, span))
        probs = jnp.exp(scores - logs)
        prob_grad = contract(cot, value_ref[here, :], 1, 1)
        score_grad = (probs * (prob_grad - dots)).astype(jnp.bfloat16)
        accum[...] += contract(score_grad, keys, 1, 0)
        key_grad_ref[here, :] += contract(score_grad, query, 0, 0)
        value_grad_ref[here, :] += contract(probs.astype(jnp.bfloat16), cot, 0, 0)
        return 0

    lax.fori_loop(lowest_ref[part], block + 1, visit, 0)
    query_grad_ref[...] = unstack_heads(accum[...] * scale)


def attend_back(lowest, first, start, logs, query, out, cot, key, value):
    rows, columns = query.shape
    pairs = key.shape[1] // 128
    start_spec, log_spec, query_spec, key_spec = head_specs(key.shape[0])
    return pl.pallas_call(
        attend_back_step,
        grid_spec=pltpu.PrefetchScalarGridSpec(
            num_scalar_prefetch=2,
            grid=(pairs, rows // SPAN),
            in_specs=[
                start_spec,
                log_spec,
                query_spec,
                query_spec,
                query_spec,
                key_spec,
                key_spec,
            ],
            out_specs=[query_spec, key_spec, key_spec],
            scratch_shapes=[pltpu.VMEM((4 * SPAN, 128), jnp.float32)],
        ),
        out_shape=[
            jax.ShapeDtypeStruct((rows, columns), jnp.float32),
            jax.ShapeDtypeStruct(key.shape, jnp.float32),
            jax.ShapeDtypeStruct(key.shape, jnp.float32),
        ],
        compiler_params=pltpu.CompilerParams(
            dimension_semantics=("arbitrary", "arbitrary"), vmem_limit_bytes=VMEM_LIMIT
        ),
        name="attend_back",
    )(lowest, first, start, logs, query, out, cot, key, value)


def weight_back_step(
    bounds_ref,
    gain_ref,
    cos_ref,
    sin_ref,
    query_ref,
    key_ref,
    value_ref,
    rows_ref,
    key_rows,
    query_rows,
    leave_left_ref,
    leave_right_ref,
    stay_left_ref,
    stay_right_ref,
    act_rows,
    left_sums,
    right_sums,
    *,
    orders,
):
    block = pl.program_id(0)
    span, width = rows_ref.shape
    own_rows, queries = query_rows.shape
    here = pl.ds(pl.multiple_of(block * span, span), span)
    needed, own = block_state(bounds_ref, block, own_rows // span)

    @pl.when(jnp.logical_not(needed))
    def _():
        act_rows[here, :] = jnp.zeros((span, width), jnp.bfloat16)
        key_rows[here, :] = jnp.zeros((span, key_rows.shape[1]), jnp.bfloat16)

    @pl.when(needed)
    def _():
        cosine, sine = cos_ref[...], -sin_ref[...]
        key_grads = turn_halves(key_ref[...], cosine, sine)
        key_rows[here, :] = jnp.concatenate([key_grads, value_ref[...]], axis=1).astype(
            jnp.bfloat16
        )
        values = rows_ref[...].astype(jnp.float32)
        act_rows[here, :] = (values * scale_rows(values) * gain_ref[...]).astype(jnp.bfloat16)

        @pl.when(own)
        def _():
            at = pl.ds(pl.multiple_of((block - bounds_ref[1]) * span, span), span)
            query_rows[at, :] = turn_halves(query_ref[...], cosine, sine).astype(jnp.bfloat16)

    @pl.when(block == pl.num_programs(0) - 1)
    def _():
        count, shard = left_sums.shape[:2]
        own_all = pl.ds(pl.multiple_of(bounds_ref[1] * span, span), own_rows)
        sums = contract(act_rows[own_all, :], query_rows[...], 0, 0).astype(jnp.bfloat16)
        left_sums[...] = sums.reshape(left_sums.shape)
        sums = contract(act_rows[...], key_rows[...], 0, 0).astype(jnp.bfloat16)
        right_sums[...] = sums.reshape(right_sums.shape)
        for index in range(count // 2):
            for odd, targets in (
                (1, (leave_left_ref, leave_right_ref)),
                (0, (stay_left_ref, stay_right_ref)),
            ):
                source = bounds_ref[2] ^ (2 * index + odd)
                for order, target, sums in zip(orders, targets, (left_sums, right_sums)):
                    target[chunk_place(index, order)] = sums[source]


def weight_back(bounds, gain, cosine, sine, query_grad, key_grad, value_grad, rows_in, shards):
    rows, width = rows_in.shape
    token_rows, queries = query_grad.shape
    keys = key_grad.shape[1]
    own_blocks = token_rows // SPAN
    shard = width // shards
    low = jnp.bfloat16
    own = pl.BlockSpec(
        (SPAN, queries), lambda i, bounds: (jnp.clip(i - bounds[1], 0, own_blocks - 1), 0)
    )
    widths = (queries, 2 * keys)
    sums = [jax.ShapeDtypeStruct((shards // 2, shard, columns), low) for columns in widths]
    made = [
        jax.ShapeDtypeStruct((rows, 2 * keys), low),
        jax.ShapeDtypeStruct((token_rows, queries), low),
    ]
    return pl.pallas_call(
        functools.partial(
            weight_back_step, orders=[order[:-1][::-1] for order in stage_orders(shards)]
        ),
        grid_spec=pltpu.PrefetchScalarGridSpec(
            num_scalar_prefetch=1,
            grid=(rows // SPAN,),
            in_specs=[
                whole_block(gain),
                row_block(128),
                row_block(128),
                own,
                row_block(keys),
                row_block(keys),
                row_block(width),
            ],
            out_specs=[whole_block(one) for one in made + sums + sums],
            scratch_shapes=[pltpu.VMEM((rows, width), low)]
            + [pltpu.VMEM((shards, shard, columns), low) for columns in widths],
        ),
        out_shape=made + sums + sums,
        compiler_params=pltpu.CompilerParams(
            dimension_semantics=("arbitrary",), vmem_limit_bytes=VMEM_LIMIT
        ),
        name="weight_back",
    )(bounds, gain, cosine, sine, query_grad, key_grad, value_grad, rows_in)


def token_back_step(
    bounds_ref,
    order_ref,
    gain_ref,
    weight_ref,
    query_ref,
    key_ref,
    rows_ref,
    residual_ref,
    out_ref,
    token_rows,
    act_grad,
):
    phase, block = pl.program_id(0), pl.program_id(1)
    span, width = rows_ref.shape
    own_rows, queries = query_ref.shape
    here = pl.ds(pl.multiple_of(block * span, span), span)
    needed, own = block_state(bounds_ref, block, own_rows // span)
    own_at = pl.ds(
        pl.multiple_of(jnp.where(own, block - bounds_ref[1], 0) * span, span), span
    )

    @pl.when((phase == 0) & jnp.logical_not(needed))
    def _():
        token_rows[here, :] = jnp.zeros((span, width), jnp.bfloat16)

    @pl.when((phase == 0) & needed)
    def _():
        act_grad[...] = contract(key_ref[...], weight_ref[:, queries:], 1, 1)

        @pl.when(own)
        def _():
            act_grad[...] += contract(query_ref[own_at, :], weight_ref[:, :queries], 1, 1)

        values = rows_ref[...].astype(jnp.float32)
        scale = scale_rows(values)
        normed = values * scale
        scaled = act_grad[...] * gain_ref[...]
        token_grad = scale * (scaled - normed * jnp.mean(scaled * normed, axis=1, keepdims=True))
        residual = jnp.where(own, residual_ref[own_at, :].astype(jnp.float32), 0.0)
        token_rows[here, :] = (token_grad + residual).astype(jnp.bfloat16)

    @pl.when(phase == 1)
    def _():
        total = token_rows.shape[0]
        places = lax.broadcasted_iota(jnp.int32, (span, total), 1)
        choose = jnp.where(order_ref[...] == places, 1.0, 0.0).astype(jnp.bfloat16)
        out_ref[...] = contract(choose, token_rows[...], 1, 0).astype(jnp.bfloat16)


def token_back(bounds, order_column, gain, weight, query_rows, key_rows, rows_in, residual):
    rows, width = rows_in.shape
    blocks = rows // SPAN
    low = jnp.bfloat16

    def early(columns):
        return pl.BlockSpec((SPAN, columns), lambda p, i, *_: (jnp.where(p == 0, i, blocks - 1), 0))

    def late(columns):
        return pl.BlockSpec((SPAN, columns), lambda p, i, *_: (jnp.where(p == 0, 0, i), 0))

    return pl.pallas_call(
        token_back_step,
        grid_spec=pltpu.PrefetchScalarGridSpec(
            num_scalar_prefetch=1,
            grid=(2, blocks),
            in_specs=[
                late(1),
                whole_block(gain),
                first_columns(width, query_rows.shape[1] + key_rows.shape[1]),
                whole_block(query_rows),
                early(key_rows.shape[1]),
                early(width),
                whole_block(residual),
            ],
            out_specs=late(width),
            scratch_shapes=[
                pltpu.VMEM((rows, width), low),
                pltpu.VMEM((SPAN, width), jnp.float32),
            ],
        ),
        out_shape=jax.ShapeDtypeStruct((rows, width), low),
        compiler_params=pltpu.CompilerParams(
            dimension_semantics=("arbitrary", "arbitrary"), vmem_limit_bytes=VMEM_LIMIT
        ),
        name="token_back",
    )(bounds, order_column, gain, weight, query_rows, key_rows, rows_in, residual)


def body(
    tokens,
    query_weight,
    key_projection_weight,
    value_projection_weight,
    output_weight,
    router_weight,
    first_gain,
    second_gain,
    expert_gate,
    expert_up,
    expert_down,
    routes,
    dealing,
    lengths,
    cotangent,
):
    low = jnp.bfloat16
    token_rows = tokens.shape[0]
    sp_count = lax.axis_size("sp")
    sp_index = lax.axis_index("sp")
    fsdp_count = lax.axis_size("fsdp")
    fsdp_index = lax.axis_index("fsdp")
    group_rows = token_rows * sp_count
    local_experts = EXPERTS // fsdp_count
    shard_rows = query_weight.shape[0]
    relative = fsdp_index ^ jnp.arange(fsdp_count, dtype=jnp.int32)
    ring = ring_begin(tokens)
    held = after(
        [query_weight, key_projection_weight, value_projection_weight, output_weight],
        *[part[0] for part in ring],
    )
    packed = jnp.concatenate(
        [
            held[0].astype(low),
            held[1].astype(low),
            held[2].astype(low),
            held[3].astype(low),
            router_weight.astype(low),
            first_gain.astype(low)[:, None],
            second_gain.astype(low)[:, None],
            jnp.zeros((shard_rows, 128 - EXPERTS - 2), low),
        ],
        axis=1,
    )
    packed_all = lax.all_gather(packed, "fsdp", axis=0, tiled=True)
    query_columns = QUERY_HEADS * HEAD_SIZE
    key_columns = KEY_VALUE_HEADS * HEAD_SIZE
    qkv_columns = query_columns + 2 * key_columns
    output_full = packed_all[:, qkv_columns : qkv_columns + MODEL_WIDTH]
    rest = packed_all[:, qkv_columns + MODEL_WIDTH :]
    router_full = rest[:, :EXPERTS]
    gain_attend = rest[:, EXPERTS].astype(jnp.float32)[None, :]
    gain_mixer = rest[:, EXPERTS + 1].astype(jnp.float32)[None, :]

    expert_range = jnp.arange(EXPERTS, dtype=jnp.int32)
    member = jnp.any(routes[:, :, None] == expert_range[None, None, :], axis=1)
    row_range = jnp.arange(token_rows, dtype=jnp.int32)
    upto = (row_range[:, None] <= row_range[None, :]).astype(low)
    rank = jnp.dot(member.T.astype(low), upto, preferred_element_type=jnp.float32)
    slots = jnp.where(member.T, rank.astype(jnp.int32) - 1, -1)

    def to_experts(by_expert):
        return exchange_blocks(
            by_expert.reshape(fsdp_count, local_experts, token_rows), "fsdp"
        )

    own = fsdp_index.astype(jnp.int32)[None]
    order_row = dealing[0]
    order_here = lax.dynamic_slice_in_dim(
        jnp.concatenate([order_row, order_row]), sp_index * token_rows, group_rows
    )
    places = jnp.arange(group_rows, dtype=jnp.int32)
    starts = sequence_starts(lengths[0], places)
    own_starts = lax.dynamic_slice_in_dim(starts, sp_index * token_rows, token_rows)
    lowest = own_starts[::SPAN] // SPAN
    start_column = own_starts[:, None]
    first_block = sp_index * (token_rows // SPAN)
    bounds = jnp.stack([lowest[0], first_block, fsdp_index]).astype(jnp.int32)
    half_dim = HEAD_SIZE // 2
    frequency = ROPE_BASE ** (-(jnp.arange(half_dim, dtype=jnp.float32) * 2.0 / HEAD_SIZE))
    angles = (places - starts).astype(jnp.float32)[:, None] * frequency[None, :]
    cosine = jnp.tile(jnp.cos(angles), (1, 4))
    sine = jnp.sin(angles)
    sine = jnp.concatenate([-sine, sine, -sine, sine], axis=1)
    merged = max(local_experts // 2, 1)
    groups = [range(first, first + merged) for first in range(0, local_experts, merged)]
    expert_parts = [
        jnp.stack(
            [
                pack_expert(
                    expert_gate[e].astype(low), expert_up[e].astype(low), expert_down[e].astype(low)
                )
                for e in members
            ]
        )
        for members in groups
    ]
    stages = fsdp_count.bit_length() - 1
    with jax.named_scope("tokens_ring"):
        ring = ring_step(ring, "sp")
    arrived_first = [part[-1] for part in ring]
    slots_here = to_experts(after([slots], *arrived_first)[0])
    slots_by_row = jnp.swapaxes(slots_here, 1, 2)
    ring_gates = {
        2: (cosine, sine, start_column, slots_by_row, order_here, bounds, *expert_parts),
    }
    with jax.named_scope("tokens_ring"):
        for step in range(1, sp_count - 1):
            ring = ring_step(ring, "sp", ring_gates.get(step, ()))
    ring_end = [part[-1] for part in ring]
    with jax.named_scope("cot_gather"):
        cot_lists = gather_begin(after([cotangent], *arrived_first)[0])
        cot_lists = gather_stage(cot_lists, "fsdp", 0)
    pieces = [part[-k % sp_count] for k in range(sp_count) for part in ring[:2]]
    pieces += [part[k] for k in range(sp_count) for part in ring[2:]]
    expert_parts = after(expert_parts, *ring_end, packed_all)
    with jax.named_scope("weights_queue"):
        expert_weights = [
            lax.all_gather(part, "sp", axis=0, tiled=False) for part in expert_parts
        ]
    rows_initial, query, key, value = project(
        bounds, order_here[None, :], gain_attend, packed_all, cosine, sine, pieces, token_rows
    )
    with jax.named_scope("cot_gather"):
        for stage in range(1, stages):
            cot_lists = gather_stage(cot_lists, "fsdp", stage)
    attended, logs = attend(lowest, first_block[None], start_column, query, key, value)
    resid = lax.dynamic_slice_in_dim(rows_initial, sp_index * token_rows, token_rows)
    branch = jnp.dot(attended, output_full, preferred_element_type=jnp.float32)
    middle = resid.astype(jnp.float32) + branch
    inv_two = lax.rsqrt(jnp.mean(middle * middle, axis=1, keepdims=True) + NORM_EPS)
    normed_two = middle * inv_two
    act_two = (normed_two * gain_mixer).astype(low)
    logits = jnp.dot(act_two, router_full, preferred_element_type=jnp.float32)
    gate_dense = jax.nn.softmax(jnp.where(member, logits, -jnp.inf), axis=-1)
    gates_here = to_experts(gate_dense.T)
    with jax.named_scope("act_gather"):
        act_lists = gather_begin(act_two)
        for stage in range(stages):
            act_lists = gather_stage(act_lists, "fsdp", stage)
    act_pieces, cot_pieces = gather_end(act_lists), gather_end(cot_lists)
    mixed_rows, back_rows, gate_grads, expert_sums = [], [], [], []
    for members, weights in zip(groups, expert_weights):
        turn = after([own], *mixed_rows[-1:])[0]
        mixed, back, gate_grad, weight_grad = run_experts(
            turn, members[0], slots_here, gates_here, weights, act_pieces, cot_pieces
        )
        mixed_rows.append(mixed)
        back_rows.append(back)
        gate_grads.append(gate_grad)
        with jax.named_scope("grads_queue"):
            expert_sums.append(
                lax.psum_scatter(weight_grad, "sp", scatter_dimension=0, tiled=False)
            )
    gate_grads = jnp.swapaxes(jnp.concatenate(gate_grads, axis=0), 0, 1)
    gate_grad_back = exchange_blocks(jnp.take(gate_grads, relative, axis=0), "fsdp")
    with jax.named_scope("back_reduce"):
        leave = combine_rows(own, slots_by_row, back_rows, 1)
        leave = after(leave, gate_grad_back)
        stay = combine_rows(own, slots_by_row, back_rows, 0)
        for stage in range(stages):
            leave, stay = reduce_stage(leave, stay, "fsdp", stage)
    grad_act_moe = jnp.concatenate(stay, axis=1)
    upstream = cotangent.astype(jnp.float32)
    gate_grad = gate_grad_back.reshape(EXPERTS, token_rows).T
    weighted = jnp.sum(gate_dense * gate_grad, axis=1, keepdims=True)
    logit_grad = (gate_dense * (gate_grad - weighted)).astype(low)
    grad_act_two = grad_act_moe + jnp.dot(
        logit_grad, router_full.T, preferred_element_type=jnp.float32
    )
    scaled_two = grad_act_two * gain_mixer
    grad_middle = upstream + inv_two * (
        scaled_two - normed_two * jnp.mean(scaled_two * normed_two, axis=1, keepdims=True)
    )
    middle_low = grad_middle.astype(low)
    grad_attn = contract(middle_low, output_full, 1, 1).astype(low)
    middle_after, *_ = after([middle_low], grad_attn)
    grad_output_w = contract(attended, middle_after, 0, 0).astype(low)
    logit_grad_after, grad_act_after = after([logit_grad, grad_act_two], grad_attn)
    grad_router_w = jnp.einsum(
        "td,te->de", act_two, logit_grad_after, preferred_element_type=jnp.float32
    )
    grad_gain_two = jnp.sum(grad_act_after * normed_two, axis=0)
    early_grads = jnp.concatenate(
        [
            grad_output_w,
            grad_router_w.astype(low),
            grad_gain_two.astype(low)[:, None],
            jnp.zeros((MODEL_WIDTH, 128 - EXPERTS - 1), low),
        ],
        axis=1,
    ).reshape(fsdp_count, shard_rows, MODEL_WIDTH + 128)
    with jax.named_scope("early_fsdp"):
        early_parts = exchange_blocks(early_grads, "fsdp")
    grad_held = after([grad_attn], expert_sums[0], early_grads)[0]
    grad_query, grad_key, grad_value = attend_back(
        lowest, first_block[None], start_column, logs, query, attended, grad_held, key, value
    )
    key_rows, query_rows, *late_parts = weight_back(
        bounds, gain_attend, cosine, sine, grad_query, grad_key, grad_value, rows_initial, fsdp_count
    )
    token_grads = token_back(
        bounds,
        order_row[:, None],
        gain_attend,
        packed_all,
        after([query_rows], *expert_sums[1:-1])[0],
        key_rows,
        rows_initial,
        middle_low,
    )
    with jax.named_scope("tokens_back"):
        tokens_grad = lax.psum_scatter(token_grads, "sp", scatter_dimension=0, tiled=True)
    with jax.named_scope("early_fsdp"):
        early_parts = after([early_parts], token_grads)[0]
        early_sum = jnp.sum(early_parts.astype(jnp.float32), axis=0).astype(low)
    with jax.named_scope("late_fsdp"):
        late_leave, late_stay = late_parts[:2], late_parts[2:]
        mix_leave, mix_stay = None, None
        for stage in range(stages):
            gates = (token_grads,) if stage == 0 else ()
            late_leave, late_stay = reduce_stage(late_leave, late_stay, "fsdp", stage, gates)
            if stage < 2:
                mixed_held = after(mixed_rows, *late_stay)
                made = combine_rows(own, slots_by_row, mixed_held, 1 - stage)
                if stage == 0:
                    mix_leave = made
                else:
                    mix_stay = made
        late_stay = after(late_stay, *mix_leave)
        row_sums = jnp.concatenate([early_sum] + [part.astype(low) for part in late_stay], axis=1)
    deep = expert_gate.shape[1]

    def unpack_down(part):
        blocks = [part[:, :, k * deep : (k + 1) * deep] for k in range(part.shape[2] // deep)]
        return jnp.concatenate(blocks, axis=1)

    expert_sums = after(expert_sums, row_sums)
    expert_grads = [
        jnp.concatenate([part[:, :deep] for part in expert_sums]).astype(jnp.float32),
        jnp.concatenate([part[:, deep : 2 * deep] for part in expert_sums]).astype(jnp.float32),
        jnp.concatenate([unpack_down(part[:, 2 * deep :]) for part in expert_sums]).astype(
            jnp.float32
        ),
    ]
    with jax.named_scope("mix_reduce"):
        for stage in range(stages):
            mix_leave, mix_stay = reduce_stage(mix_leave, mix_stay, "fsdp", stage)
            if stage == 0:
                mix_leave = after(mix_leave, *expert_grads)
    layer_out = (middle + jnp.concatenate(mix_stay, axis=1)).astype(low)
    with jax.named_scope("sums_sp"):
        row_sums = exchange_blocks(
            row_sums.reshape(sp_count, shard_rows // sp_count, row_sums.shape[1]), "sp"
        )
        row_sums = jnp.sum(row_sums.astype(jnp.float32), axis=0).astype(low)
        row_sums = exchange_blocks(
            jnp.broadcast_to(row_sums[None], (sp_count,) + row_sums.shape), "sp"
        )
    row_sums = row_sums.reshape(shard_rows, -1).astype(jnp.float32)
    early_sum = row_sums[:, : MODEL_WIDTH + 128]
    late_all = row_sums[:, MODEL_WIDTH + 128 :]
    return (
        layer_out,
        tokens_grad,
        late_all[:, :query_columns],
        late_all[:, query_columns : query_columns + key_columns],
        late_all[:, query_columns + key_columns : qkv_columns],
        early_sum[:, :MODEL_WIDTH],
        early_sum[:, MODEL_WIDTH : MODEL_WIDTH + EXPERTS],
        jnp.sum(late_all * packed[:, :qkv_columns].astype(jnp.float32), axis=1)
        / first_gain.astype(low).astype(jnp.float32),
        early_sum[:, MODEL_WIDTH + EXPERTS],
        *expert_grads,
    )


def solution(mesh):
    return jax.shard_map(
        body,
        mesh=mesh,
        in_specs=(
            P(("fsdp", "sp"), None),
            P("fsdp", None),
            P("fsdp", None),
            P("fsdp", None),
            P("fsdp", None),
            P("fsdp", None),
            P("fsdp"),
            P("fsdp"),
            P("fsdp", "sp", None),
            P("fsdp", "sp", None),
            P("fsdp", None, "sp"),
            P(("fsdp", "sp"), None),
            P("fsdp", None),
            P("fsdp", None),
            P(("fsdp", "sp"), None),
        ),
        out_specs=(
            P(("fsdp", "sp"), None),
            P(("fsdp", "sp"), None),
            P("fsdp", None),
            P("fsdp", None),
            P("fsdp", None),
            P("fsdp", None),
            P("fsdp", None),
            P("fsdp"),
            P("fsdp"),
            P("fsdp", "sp", None),
            P("fsdp", "sp", None),
            P("fsdp", None, "sp"),
        ),
        check_vma=False,
    )
```
